512 devices in a mesh: seq: 128 (over z, y, core), head: 4 (over x).
Axes of the slice: x: 4, y: 4, z: 16, core: 2. Of those that a mesh axis runs over, the one named last changes fastest.
Arguments:
- queries: bfloat16 [16384, 1024], P('seq', 'head'), may hold values from -8 to 8
- keys: bfloat16 [16384, 1024], P('seq', 'head'), may hold values from -8 to 8
- values: bfloat16 [16384, 1024], P('seq', 'head'), may hold values from -6 to 6
- out_grad: bfloat16 [16384, 1024], P('seq', 'head'), may hold values from -6 to 6
- rel_emb: bfloat16 [512, 1024], replicated, may hold values from -6 to 6
- w_query: bfloat16 [1024, 1024], P(None, 'head'), may hold values from -0.1875 to 0.1875
- w_key: bfloat16 [1024, 1024], P(None, 'head'), may hold values from -0.1875 to 0.1875
- doc_lengths: int32 [64], replicated, may hold values from 1 to 512, 16384 in all
- bucket_table: int32 [1024], replicated, may hold values from 0 to 511, as said below
Outputs:
- query_grad: bfloat16 [16384, 1024], P('seq', 'head')
- key_grad: bfloat16 [16384, 1024], P('seq', 'head')
- value_grad: bfloat16 [16384, 1024], P('seq', 'head')
- rel_emb_grad: float32 [512, 1024], P(None, 'head')
- w_query_grad: float32 [1024, 1024], P('seq', 'head')
- w_key_grad: float32 [1024, 1024], P('seq', 'head')
The draws below stay inside these ranges and needn't reach their ends.
Inputs may be any that keep to these rules, and one draw needn't show every extreme that they name: `doc_lengths`: the lengths sum to 16384 and the longest is exactly 512. `bucket_table`: entry o is the bucket of the relative offset o - 512; entries never fall as o grows, and equal o - 512 + 512 // 2 wherever o - 512 lies between -128 and 128.
All inputs are finite; a program needn't handle non-finite values.
Results may differ from the reference program's by a relative error of at most 0.01.
Values may be sent and summed in bfloat16 or wider, within the bound.
A program may use at most 64 MiB of HBM per device.

```python
import math
import jax
import jax.numpy as jnp
import numpy as np
from jax import lax

D = 1024
HEADS = 16
HD = 64
BUCKETS = 512
TOK_DEV = 128
DOC_MAX = 512
TOKENS = 16384
NDOCS = 64


def draw_queries(key, part):
    shape = (TOKENS, HEADS * HD)
    base = jax.random.truncated_normal(jax.random.fold_in(key, 1), -6.0, 6.0, shape, jnp.float32)
    return base.astype(jnp.bfloat16)


def draw_keys(key, part):
    shape = (TOKENS, HEADS * HD)
    base = jax.random.truncated_normal(jax.random.fold_in(key, 2), -6.0, 6.0, shape, jnp.float32)
    return base.astype(jnp.bfloat16)


def draw_bucket_table(key, part):
    half_count = BUCKETS // 2
    near_count = BUCKETS // 4
    distance = jnp.arange(DOC_MAX + 1, dtype=jnp.int32)

    def one_side(side_key):
        advance = (jax.random.randint(side_key, (DOC_MAX + 1,), 0, 4) == 0).astype(jnp.int32)
        advance = jnp.where(distance > DOC_MAX - half_count, 1, advance)
        advance = jnp.where(distance <= near_count, 0, advance)
        return jnp.where(distance <= near_count, distance, near_count + jnp.cumsum(advance).astype(jnp.int32))
    upper_level = one_side(jax.random.fold_in(key, 21))
    lower_level = one_side(jax.random.fold_in(key, 22))
    upper_side = half_count + jnp.minimum(half_count - 1, upper_level)
    lower_side = half_count - jnp.minimum(half_count, lower_level)
    table = jnp.concatenate([jnp.flip(lower_side[1:]), upper_side[:DOC_MAX]])
    return table.astype(jnp.int32)


def levels(key, shape, cuts, low, high):
    factor_of = 1.0
    for dim, shards_of in cuts:
        heights = jax.random.uniform(jax.random.fold_in(jax.random.fold_in(key, 6), dim), (shards_of,), jnp.float32, low / len(cuts), high / len(cuts))
        factor_of = factor_of * jnp.repeat(jnp.exp(heights), shape[dim] // shards_of).reshape((-1,) + (1,) * (len(shape) - 1 - dim))
    return factor_of


def length_profile(count, total, bound, lean):
    portions = [(1 << 20) // math.isqrt(grade ** lean) + 1 for grade in range(2, count + 1)]
    surplus, holding = total - bound - (count - 1), [1] * (count - 1)
    while surplus > 0:
        movable = [i for i in range(count - 1) if holding[i] < bound]
        pool, remaining = sum([portions[i] for i in movable]), surplus
        for i in movable:
            more = min(bound - holding[i], max(1, remaining * portions[i] // pool), surplus)
            holding[i] = holding[i] + more
            surplus = surplus - more
    return np.array([bound] + holding)


def ragged(key, amount, total, bound, skew):
    if amount == 2:
        one = jax.random.randint(key, (), max(1, total - bound), min(bound, total - 1) + 1)
        return jnp.stack([one, total - one])
    tallies = jnp.asarray(length_profile(amount, total, bound, skew), jnp.int32)
    twos = (amount - 1) // 2
    donor, taker = tallies[1:1 + 2 * twos:2], tallies[2:2 + 2 * twos:2]
    slack = jnp.minimum(donor - 1, bound - taker)
    moved = jax.random.randint(jax.random.fold_in(key, 1), (twos,), 0, 1 << 20) % (slack + 1)
    tallies = tallies.at[1:1 + 2 * twos:2].set(donor - moved).at[2:2 + 2 * twos:2].set(taker + moved)
    return tallies[jax.random.permutation(jax.random.fold_in(key, 2), amount)]


def normal_values(stream_key, dims, scale, most, shards=(), kind=jnp.bfloat16):
    result = scale * jax.random.normal(stream_key, dims, jnp.float32)
    if shards:
        result = result * levels(stream_key, dims, shards, -0.22, 0.18)
    return jnp.clip(result, -most, most).astype(kind)


def setup_inputs(seed: int = 0) -> dict:
    arg_keys = jax.random.split(jax.random.key(seed), 10)
    queries = draw_queries(jax.random.fold_in(arg_keys[9], 71), 0)
    keys = draw_keys(jax.random.fold_in(arg_keys[9], 71), 0)
    values = normal_values(arg_keys[2], (TOKENS, HEADS * HD), 1.0, 6.0, ((0, 128), (1, 4)))
    out_grad = normal_values(arg_keys[3], (TOKENS, HEADS * HD), 1.0, 6.0, ((0, 128), (1, 4)))
    rel_emb = normal_values(arg_keys[4], (BUCKETS, D), 1.0, 6.0)
    w_query = normal_values(arg_keys[5], (D, HEADS * HD), D ** -0.5, 0.1875, ((1, 4),))
    w_key = normal_values(arg_keys[6], (D, HEADS * HD), D ** -0.5, 0.1875, ((1, 4),))
    doc_lengths = ragged(arg_keys[7], NDOCS, TOKENS, DOC_MAX, 2).astype(jnp.int32)
    bucket_table = draw_bucket_table(jax.random.fold_in(arg_keys[9], 71), 0)
    return {"queries": queries, "keys": keys, "values": values, "out_grad": out_grad, "rel_emb": rel_emb, "w_query": w_query, "w_key": w_key, "doc_lengths": doc_lengths, "bucket_table": bucket_table}


masked_score = -1e+30

def contract(left, right, left_dim, right_dim):
    return lax.dot_general(left, right, (((left_dim,), (right_dim,)), ((), ())), preferred_element_type=jnp.float32)

def doc_index(position, doc_ends, extent):
    inside = (position >= 0) & (position < extent)
    owner = lax.optimization_barrier(jnp.sum((doc_ends[None, :] <= position[:, None]).astype(jnp.int32), axis=1))
    return jnp.where(inside, owner, -1)

def pair_tables(query_pos, key_pos, doc_ends, bucket_table, extent):
    offset_span = bucket_table.shape[0] // 2
    query_doc = doc_index(query_pos, doc_ends, extent)
    key_doc = doc_index(key_pos, doc_ends, extent)
    same_doc = query_doc[:, None] == key_doc[None, :]
    relative = query_pos[:, None] - key_pos[None, :]
    ahead_bucket = bucket_table[jnp.clip(relative + offset_span, 0, 2 * offset_span - 1)]
    behind_bucket = bucket_table[jnp.clip(offset_span - relative, 0, 2 * offset_span - 1)]
    return (same_doc, ahead_bucket, behind_bucket)

def pair_scores(query_rows, key_rows, pos_keys, pos_queries, ahead_bucket, behind_bucket, same_doc, score_scale):
    row_number = jnp.arange(query_rows.shape[0])[:, None]
    key_number = jnp.arange(key_rows.shape[0])[None, :]
    content = contract(query_rows, key_rows, 1, 1)
    query_term = contract(query_rows, pos_keys, 1, 1)[row_number, ahead_bucket]
    key_term = contract(key_rows, pos_queries, 1, 1)[key_number, behind_bucket]
    return jnp.where(same_doc, score_scale * (content + query_term + key_term), masked_score)

def query_side(query_rows, key_rows, value_rows, grad_rows, pos_keys, pos_queries, ahead_bucket, behind_bucket, same_doc, score_scale):
    scores = pair_scores(query_rows, key_rows, pos_keys, pos_queries, ahead_bucket, behind_bucket, same_doc, score_scale)
    row_max = lax.optimization_barrier(jnp.max(scores, axis=1, keepdims=True))
    expd = jnp.where(same_doc, jnp.exp(scores - row_max), 0.0)
    row_sum = lax.optimization_barrier(jnp.sum(expd, axis=1, keepdims=True))
    probs = expd / row_sum
    probs_low = probs.astype(jnp.bfloat16)
    dprobs = contract(grad_rows, value_rows, 1, 1)
    row_dot = lax.optimization_barrier(jnp.sum(probs * dprobs, axis=1, keepdims=True))
    dscores = probs * (dprobs - row_dot)
    dscores_low = dscores.astype(jnp.bfloat16)
    dscores_back = dscores_low.astype(jnp.float32)
    row_number = jnp.arange(query_rows.shape[0])[:, None]
    key_number = jnp.arange(key_rows.shape[0])[None, :]
    buckets = pos_keys.shape[0]
    ahead_grad = jnp.zeros((query_rows.shape[0], buckets), jnp.float32).at[row_number, ahead_bucket].add(dscores_back)
    ahead_low = ahead_grad.astype(jnp.bfloat16)
    behind_grad = jnp.zeros((key_rows.shape[0], buckets), jnp.float32).at[key_number, behind_bucket].add(dscores_back)
    behind_low = behind_grad.astype(jnp.bfloat16)
    query_grad = score_scale * (contract(dscores_low, key_rows, 1, 0) + contract(ahead_low, pos_keys, 1, 0))
    key_grad = score_scale * (contract(dscores_low, query_rows, 0, 0) + contract(behind_low, pos_queries, 1, 0))
    value_grad = contract(probs_low, grad_rows, 0, 0)
    bucket_key = score_scale * contract(ahead_low, query_rows, 0, 0)
    bucket_query = score_scale * contract(behind_low, key_rows, 0, 0)
    return (query_grad, key_grad, value_grad, bucket_key, bucket_query)

def split_heads(matrix):
    return matrix.reshape(matrix.shape[0], HEADS, HD).transpose(1, 0, 2)

def join_heads(stacked):
    return stacked.transpose(1, 0, 2).reshape(stacked.shape[1], HEADS * HD)

def reference(queries, keys, values, out_grad, rel_emb, w_query, w_key, doc_lengths, bucket_table):
    score_scale = 1.0 / math.sqrt(3.0 * HD)
    feature_count = HEADS * HD
    pos_key = jnp.dot(rel_emb, w_key, preferred_element_type=jnp.float32).astype(jnp.bfloat16)
    pos_query = jnp.dot(rel_emb, w_query, preferred_element_type=jnp.float32).astype(jnp.bfloat16)
    pos_key_heads = split_heads(pos_key)
    pos_query_heads = split_heads(pos_query)
    doc_ends = jnp.cumsum(doc_lengths).astype(jnp.int32)
    keys_padded = jnp.pad(keys, ((DOC_MAX, DOC_MAX), (0, 0)))
    values_padded = jnp.pad(values, ((DOC_MAX, DOC_MAX), (0, 0)))
    window = TOK_DEV + 2 * DOC_MAX
    block_count = TOKENS // TOK_DEV

    def advance(running, block_index):
        key_acc, value_acc, bucket_key_acc, bucket_query_acc = running
        first_token = (block_index * TOK_DEV).astype(jnp.int32)
        query_block = lax.dynamic_slice_in_dim(queries, first_token, TOK_DEV, 0)
        grad_block = lax.dynamic_slice_in_dim(out_grad, first_token, TOK_DEV, 0)
        key_window = lax.dynamic_slice_in_dim(keys_padded, first_token, window, 0)
        value_window = lax.dynamic_slice_in_dim(values_padded, first_token, window, 0)
        query_pos = first_token + jnp.arange(TOK_DEV, dtype=jnp.int32)
        key_pos = first_token - DOC_MAX + jnp.arange(window, dtype=jnp.int32)
        same_doc, ahead_bucket, behind_bucket = pair_tables(query_pos, key_pos, doc_ends, bucket_table, TOKENS)

        def per_head(query_rows, key_rows, value_rows, grad_rows, pos_keys, pos_queries):
            return query_side(query_rows, key_rows, value_rows, grad_rows, pos_keys, pos_queries, ahead_bucket, behind_bucket, same_doc, score_scale)
        query_grad, key_grad, value_grad, bucket_key, bucket_query = jax.vmap(per_head)(split_heads(query_block), split_heads(key_window), split_heads(value_window), split_heads(grad_block), pos_key_heads, pos_query_heads)
        old_keys = lax.dynamic_slice_in_dim(key_acc, first_token, window, 0)
        key_acc = lax.dynamic_update_slice_in_dim(key_acc, old_keys + join_heads(key_grad), first_token, 0)
        old_values = lax.dynamic_slice_in_dim(value_acc, first_token, window, 0)
        value_acc = lax.dynamic_update_slice_in_dim(value_acc, old_values + join_heads(value_grad), first_token, 0)
        running = (key_acc, value_acc, bucket_key_acc + bucket_key, bucket_query_acc + bucket_query)
        return (running, join_heads(query_grad))
    start_state = (jnp.zeros((TOKENS + 2 * DOC_MAX, feature_count), jnp.float32), jnp.zeros((TOKENS + 2 * DOC_MAX, feature_count), jnp.float32), jnp.zeros((HEADS, BUCKETS, HD), jnp.float32), jnp.zeros((HEADS, BUCKETS, HD), jnp.float32))
    final_state, query_blocks = lax.scan(advance, start_state, jnp.arange(block_count, dtype=jnp.int32))
    key_acc, value_acc, bucket_key_acc, bucket_query_acc = final_state
    query_grad = query_blocks.reshape(TOKENS, feature_count).astype(jnp.bfloat16)
    key_grad = key_acc[DOC_MAX:DOC_MAX + TOKENS].astype(jnp.bfloat16)
    value_grad = value_acc[DOC_MAX:DOC_MAX + TOKENS].astype(jnp.bfloat16)
    bucket_key = join_heads(bucket_key_acc).astype(jnp.bfloat16)
    bucket_query = join_heads(bucket_query_acc).astype(jnp.bfloat16)
    rel_emb_grad = contract(bucket_key, w_key, 1, 1) + contract(bucket_query, w_query, 1, 1)
    w_key_grad = contract(rel_emb, bucket_key, 0, 0)
    w_query_grad = contract(rel_emb, bucket_query, 0, 0)
    return (query_grad, key_grad, value_grad, rel_emb_grad, w_query_grad, w_key_grad)
```

```python
import functools
import math

import jax
import jax.numpy as jnp
from jax import lax
from jax.experimental import pallas as pl
from jax.experimental.pallas import tpu as pltpu
from jax.sharding import PartitionSpec as P

HD = 64
T = 128
NY = 4
f32 = jnp.float32
bf16 = jnp.bfloat16
SCALE = 1.0 / math.sqrt(3.0 * HD)
ANY = pl.BlockSpec(memory_space=pl.ANY)
VM = pl.BlockSpec(memory_space=pltpu.VMEM)


def dot(a, b, ca=1, cb=0):
    return lax.dot_general(a, b, (((ca,), (cb,)), ((), ())), preferred_element_type=f32)


def remote(src, dst, send, recv, seq, head=None):
    where = {"seq": seq} if head is None else {"seq": seq, "head": head}
    return pltpu.make_async_remote_copy(
        src_ref=src, dst_ref=dst, send_sem=send, recv_sem=recv,
        device_id=where, device_id_type=pl.DeviceIdType.MESH,
    )


def greet(seq, head=None):
    where = {"seq": seq} if head is None else {"seq": seq, "head": head}
    pl.semaphore_signal(
        pltpu.get_barrier_semaphore(), inc=1, device_id=where,
        device_id_type=pl.DeviceIdType.MESH,
    )


def lanes(p):
    return pl.ds(pl.multiple_of(p * T, T), T)


def rows(start):
    return pl.ds(pl.multiple_of(start, T), T)


def halo_kernel(nc, q_ref, k_ref, v_ref, g_ref, rel_ref, wq_ref, wk_ref, rev_ref,
                q2_ref, g2_ref, kw_ref, vw_ref, pb_ref,
                rel_v, w_v, send, recv, local):
    s = lax.axis_index("seq")
    c, p = s // 2, lax.rem(s, 2)
    o = 1 - p
    far = [-2, 2, -1, 1]

    def chip(d):
        return lax.rem(c + d + nc, nc)

    for d in far:
        for pp in range(2):
            greet(2 * chip(d) + pp)
    greet(2 * c + o)

    loads = []

    def load(src, dst):
        copy = pltpu.make_async_copy(src, dst, local.at[len(loads)])
        copy.start()
        loads.append(copy)

    load(rel_ref, rel_v)
    load(wk_ref.at[:, lanes(p)], w_v.at[0])
    load(wq_ref.at[:, lanes(p)], w_v.at[1])
    load(k_ref.at[:, lanes(p)], kw_ref.at[rows(2 * 2 * T + T * p)])
    load(v_ref.at[:, lanes(p)], vw_ref.at[rows(2 * 2 * T + T * p)])
    load(q_ref.at[:, lanes(p)], q2_ref.at[rows(T * p)])
    load(g_ref.at[:, lanes(p)], g2_ref.at[rows(T * p)])

    pl.semaphore_wait(pltpu.get_barrier_semaphore(), 9)

    sent = []

    def push(src, dst, slot, seq):
        copy = remote(src, dst, send.at[len(sent)], recv.at[slot], seq)
        copy.start()
        sent.append(copy)

    for d in far:
        for pp in range(2):
            row = rows(2 * T * (2 - d) + T * p)
            base = ((d + 2) * 2 + p) * 2
            push(k_ref.at[:, pl.ds(pp * T, T)], kw_ref.at[row], base, 2 * chip(d) + pp)
            push(v_ref.at[:, pl.ds(pp * T, T)], vw_ref.at[row], base + 1, 2 * chip(d) + pp)
    row = rows(4 * T + T * p)
    push(k_ref.at[:, lanes(o)], kw_ref.at[row], 20, 2 * c + o)
    push(v_ref.at[:, lanes(o)], vw_ref.at[row], 21, 2 * c + o)
    push(q_ref.at[:, lanes(o)], q2_ref.at[rows(T * p)], 22, 2 * c + o)
    push(g_ref.at[:, lanes(o)], g2_ref.at[rows(T * p)], 23, 2 * c + o)

    for copy in loads[:3]:
        copy.wait()
    pos_key = dot(rel_v[...], w_v[0]).astype(bf16)
    pos_query = dot(rel_v[...], w_v[1]).astype(bf16)
    both = jnp.concatenate([pos_key, pos_query], 1)
    buckets = both.shape[0]
    column = jnp.transpose(jnp.broadcast_to(rev_ref[...], (T, rev_ref.shape[1])))
    lane = lax.broadcasted_iota(jnp.int32, column.shape, 1)
    onehot = jnp.concatenate(
        [(column == lane + T * b).astype(f32).astype(bf16) for b in range(buckets // T)], 1
    )
    pb_ref[...] = dot(onehot, both).astype(bf16)

    for copy in loads[3:]:
        copy.wait()
    for copy in sent:
        copy.wait_send()
    for d in far:
        for pp in range(2):
            row = pl.ds(2 * T * (2 - d) + T * pp, T)
            base = ((d + 2) * 2 + pp) * 2
            remote(kw_ref.at[row], kw_ref.at[row], send.at[0], recv.at[base], s).wait_recv()
            remote(vw_ref.at[row], vw_ref.at[row], send.at[0], recv.at[base + 1], s).wait_recv()
    row = rows(4 * T + T * o)
    remote(kw_ref.at[row], kw_ref.at[row], send.at[0], recv.at[20], s).wait_recv()
    remote(vw_ref.at[row], vw_ref.at[row], send.at[0], recv.at[21], s).wait_recv()
    row = rows(T * o)
    remote(q2_ref.at[row], q2_ref.at[row], send.at[0], recv.at[22], s).wait_recv()
    remote(g2_ref.at[row], g2_ref.at[row], send.at[0], recv.at[23], s).wait_recv()


def halo(q, k, v, g, rel, wq, wk, rev, nc):
    return pl.pallas_call(
        functools.partial(halo_kernel, nc),
        out_shape=(
            jax.ShapeDtypeStruct((2 * T, T), bf16),
            jax.ShapeDtypeStruct((2 * T, T), bf16),
            jax.ShapeDtypeStruct((10 * T, T), bf16),
            jax.ShapeDtypeStruct((10 * T, T), bf16),
            jax.ShapeDtypeStruct((rev.shape[1], 2 * T), bf16),
        ),
        in_specs=[ANY] * 7 + [VM],
        out_specs=(VM,) * 5,
        scratch_shapes=[
            pltpu.VMEM(rel.shape, bf16),
            pltpu.VMEM((2, wq.shape[0], T), bf16),
            pltpu.SemaphoreType.DMA((20,)),
            pltpu.SemaphoreType.DMA((24,)),
            pltpu.SemaphoreType.DMA((7,)),
        ],
        compiler_params=pltpu.CompilerParams(collective_id=0, has_side_effects=True),
        name="halo",
    )(q, k, v, g, rel, wq, wk, rev)


def attention_kernel(rb, q_ref, g_ref, kw_ref, vw_ref, pb_ref, rev_ref, len_ref,
                     dq_ref, dk_ref, dv_ref, bp_ref,
                     q2, g2, k2, pk2, pqr2, qrevt, krevt, sc, dp, dsb,
                     dqa, dka, dva, gt, ht):
    c = lax.axis_index("seq") // 2
    keys = kw_ref.shape[0]
    tiles = keys // T
    span = pb_ref.shape[0]
    ri = lax.broadcasted_iota(jnp.int32, (T, T), 0)
    ci = lax.broadcasted_iota(jnp.int32, (T, T), 1)
    flip = (ri + ci == T - 1).astype(f32).astype(bf16)

    ndocs = len_ref.shape[1]
    e = lax.broadcasted_iota(jnp.int32, (ndocs, ndocs), 1)
    d = lax.broadcasted_iota(jnp.int32, (ndocs, ndocs), 0)
    lens = jnp.broadcast_to(len_ref[...], (ndocs, ndocs))
    ends = jnp.sum(jnp.where(e <= d, lens, 0), axis=1, keepdims=True)
    shift = (c - 2) * 2 * T
    pos = lax.broadcasted_iota(jnp.int32, (ndocs, 2 * T), 1) + c * 2 * T
    first = jnp.max(jnp.where(ends <= pos, ends, 0), axis=0, keepdims=True) - shift
    last = jnp.min(jnp.where(ends > pos, ends, 1 << 30), axis=0, keepdims=True) - shift

    zero_band = jnp.zeros((2 * T, T), bf16)
    for h in range(2):
        def masked(x):
            lane = lax.broadcasted_iota(jnp.int32, x.shape, 1)
            keep = (lane < HD) if h == 0 else (lane >= HD)
            return jnp.where(keep, x, jnp.zeros_like(x))
        qh = masked(q_ref[...])
        q2[h] = qh
        g2[h] = masked(g_ref[...])
        pk2[h] = masked(pb_ref[:, :T])
        pqr2[h, : 2 * T] = zero_band
        pqr2[h, 2 * T : 2 * T + span] = masked(pb_ref[:, T:])
        pqr2[h, 2 * T + span :] = zero_band
        for r in range(2):
            qrevt[h, :, r * T : (r + 1) * T] = jnp.transpose(
                dot(flip, qh[r * T : (r + 1) * T])
            ).astype(bf16)
        for j in range(tiles):
            kh = masked(kw_ref[j * T : (j + 1) * T])
            k2[h, j * T : (j + 1) * T] = kh
            krevt[h, :, j * T : (j + 1) * T] = jnp.transpose(dot(flip, kh)).astype(bf16)
    dqa[...] = jnp.zeros_like(dqa)
    dka[...] = jnp.zeros_like(dka)
    dva[...] = jnp.zeros_like(dva)
    gt[...] = jnp.zeros_like(gt)
    ht[...] = jnp.zeros_like(ht)
    wide = 9 * T

    def head(h, carry):
        sc[...] = jnp.zeros_like(sc)
        for r in range(2):
            a = dot(q2[h, r * T : (r + 1) * T], pb_ref[:, :T], 1, 1)
            a = jnp.concatenate([a, jnp.zeros((T, wide - span), f32)], 1)
            a = pltpu.roll(a, 1, 1, stride=1, stride_axis=0)
            for j in range(9):
                sc[(r + j) * T : (r + j + 1) * T, r * T : (r + 1) * T] = jnp.transpose(
                    a[:, j * T : (j + 1) * T]
                )
        top = jnp.full((8, 2 * T), -1e30, f32)
        for j in range(tiles):
            at = slice(j * T, (j + 1) * T)
            band = slice((9 - j) * T, (9 - j) * T + 3 * T)
            b = dot(kw_ref[at], pqr2[h, band], 1, 1)
            b = pltpu.roll(b, 2 * T + 1, 1, stride=1, stride_axis=0)[:, : 2 * T]
            x = SCALE * (dot(kw_ref[at], q2[h], 1, 1) + sc[at] + b)
            at_key = lax.broadcasted_iota(jnp.int32, (T, 2 * T), 0) + j * T
            x = jnp.where((at_key >= first) & (at_key < last), x, -1e30)
            sc[at] = x
            top = jnp.maximum(top, jnp.max(x.reshape(T // 8, 8, 2 * T), axis=0))
        top = jnp.max(top, axis=0, keepdims=True)
        total = jnp.zeros((8, 2 * T), f32)
        along = jnp.zeros((8, 2 * T), f32)
        for j in range(tiles):
            at = slice(j * T, (j + 1) * T)
            x = jnp.exp(sc[at] - top)
            y = dot(vw_ref[at], g2[h], 1, 1)
            sc[at] = x
            dp[at] = y
            total = total + jnp.sum(x.reshape(T // 8, 8, 2 * T), axis=0)
            along = along + jnp.sum((x * y).reshape(T // 8, 8, 2 * T), axis=0)
        inv = 1.0 / jnp.sum(total, axis=0, keepdims=True)
        row_dot = jnp.sum(along, axis=0, keepdims=True) * inv
        for j in range(tiles):
            at = slice(j * T, (j + 1) * T)
            band = slice((9 - j) * T, (9 - j) * T + 3 * T)
            prob = sc[at] * inv
            ds = (prob * (dp[at] - row_dot)).astype(bf16)
            dsb[at] = ds
            dva[at] += dot(prob.astype(bf16), g2[h])
            back = dot(flip, ds)
            skew = jnp.concatenate([back, jnp.zeros((T, T), f32)], 1)
            skew = pltpu.roll(skew, 0, 1, stride=1, stride_axis=0).astype(bf16)
            dka[at] += dot(back.astype(bf16), q2[h]) + dot(skew, pqr2[h, band])
            ht[:, band] += dot(krevt[h, :, at], skew)
        for r in range(2):
            part = slice(r * T, (r + 1) * T)
            reach = slice(r * T, r * T + wide)
            back = dot(flip, dsb[reach, part], 1, 1)
            skew = pltpu.roll(back, span, 1, stride=1, stride_axis=0)[:, :span].astype(bf16)
            dqa[part] += dot(back.astype(bf16), k2[h, reach]) + dot(skew, pk2[h])
            gt[...] += dot(qrevt[h, :, part], skew)
        return carry

    lax.fori_loop(0, 2, head, 0)

    for r in range(2):
        part = slice(r * T, (r + 1) * T)
        dq_ref[part] = dot(flip, (SCALE * dqa[part]).astype(bf16)).astype(bf16)
    for j in range(tiles):
        at = slice(j * T, (j + 1) * T)
        dk_ref[at] = dot(flip, (SCALE * dka[at]).astype(bf16)).astype(bf16)
        dv_ref[at] = dva[at].astype(bf16)
    n = bp_ref.shape[0]
    buckets = n * rb
    number = lax.broadcasted_iota(jnp.int32, (buckets, span), 0)
    onehot = (number == rev_ref[...]).astype(f32).astype(bf16)
    bk = SCALE * dot(onehot, gt[...].astype(bf16), 1, 1)
    bq = SCALE * dot(onehot, ht[:, 2 * T : 2 * T + span].astype(bf16), 1, 1)
    bp_ref[...] = jnp.concatenate(
        [bk.reshape(n, rb, T), bq.reshape(n, rb, T)], 1
    ).astype(bf16)


def attention(q2, g2, kw, vw, pb, rev, lens, nc, buckets):
    keys, span = kw.shape[0], pb.shape[0]
    rb = buckets // nc
    return pl.pallas_call(
        functools.partial(attention_kernel, rb),
        out_shape=(
            jax.ShapeDtypeStruct((2 * T, T), bf16),
            jax.ShapeDtypeStruct((keys, T), bf16),
            jax.ShapeDtypeStruct((keys, T), bf16),
            jax.ShapeDtypeStruct((nc, 2 * rb, T), bf16),
        ),
        in_specs=[VM] * 7,
        out_specs=(VM,) * 4,
        scratch_shapes=[
            pltpu.VMEM((2, 2 * T, T), bf16),
            pltpu.VMEM((2, 2 * T, T), bf16),
            pltpu.VMEM((2, keys, T), bf16),
            pltpu.VMEM((2, span, T), bf16),
            pltpu.VMEM((2, span + 4 * T, T), bf16),
            pltpu.VMEM((2, T, 2 * T), bf16),
            pltpu.VMEM((2, T, keys), bf16),
            pltpu.VMEM((keys, 2 * T), f32),
            pltpu.VMEM((keys, 2 * T), f32),
            pltpu.VMEM((keys, 2 * T), bf16),
            pltpu.VMEM((2 * T, T), f32),
            pltpu.VMEM((keys, T), f32),
            pltpu.VMEM((keys, T), f32),
            pltpu.VMEM((T, span), f32),
            pltpu.VMEM((T, span + 4 * T), f32),
        ],
        name="attention",
    )(q2, g2, kw, vw, pb, rev, lens)


def sums_kernel(nz, ny, nx, bp_ref, dq_ref, dk_ref, dv_ref, rel_ref, wq_ref, wk_ref,
                dqo_ref, dko_ref, dvo_ref, relo_ref, wqo_ref, wko_ref,
                wv, relb, rkv, rq, yrecv, zsend, zrecv, own, ag, xpart, xrecv,
                relz, rely, relp, wtmp, wsend, wrecv, send, recv, local):
    nc = nz * ny
    s = lax.axis_index("seq")
    hx = lax.axis_index("head")
    c, p = s // 2, lax.rem(s, 2)
    o = 1 - p
    z, y = c // ny, lax.rem(c, ny)
    rb2 = bp_ref.shape[1]
    rb = rb2 // 2
    width = rel_ref.shape[1]
    dr2 = width // nc
    dr = dr2 // 2
    m = 2 * hx + p
    hops = [-2, 2, -1, 1]

    def chip(d):
        return lax.rem(c + d + nc, nc)

    def ypeer(k):
        return lax.rem(y + k, ny)

    def zpeer(k):
        return lax.rem(z + k, nz)

    def mpeer(k):
        return lax.rem(m + k, 2 * nx)

    def at(zz, yy):
        return 2 * (zz * ny + yy) + p

    yk = sorted(range(1, ny), key=lambda k: -min(k, ny - k))
    zk = sorted(range(1, nz), key=lambda k: -min(k, nz - k))
    mk = range(1, 2 * nx)
    mate = 2 * c + o

    for k in zk:
        greet(at(zpeer(k), y))
    for k in yk:
        greet(at(z, ypeer(k)))
    for d in hops:
        for pp in range(2):
            greet(2 * chip(d) + pp)
    for k in mk:
        greet(2 * c + lax.rem(mpeer(k), 2), mpeer(k) // 2)
    greet(mate)

    loads = []

    def load(src, dst):
        copy = pltpu.make_async_copy(src, dst, local.at[len(loads)])
        copy.start()
        loads.append(copy)

    load(wk_ref.at[:, lanes(p)], wv.at[0])
    load(wq_ref.at[:, lanes(p)], wv.at[1])
    load(rel_ref.at[:, lanes(c * dr2 // T)], relb)
    load(dk_ref.at[rows(4 * T + p * T)], rkv.at[2, p, 0])
    load(dv_ref.at[rows(4 * T + p * T)], rkv.at[2, p, 1])
    load(dq_ref.at[rows(p * T)], rq.at[p])

    pl.semaphore_wait(
        pltpu.get_barrier_semaphore(), len(zk) + len(yk) + 8 + len(mk) + 1
    )

    sent = []
    slots = [0]

    def push(src, dst, slot, seq, head=None):
        copy = remote(src, dst, send.at[len(sent)], recv.at[slot], seq, head)
        copy.start()
        sent.append(copy)

    def take(count):
        base = slots[0]
        slots[0] += count
        return base

    def arrive(dst, slot):
        remote(dst, dst, send.at[0], recv.at[slot], s).wait_recv()

    ys = take(ny)
    for k in yk:
        push(bp_ref.at[pl.ds(nz * ypeer(k), nz)], yrecv.at[k - 1], ys + k - 1, at(z, ypeer(k)))

    rs = take(20)
    qs = take(1)
    for d in hops:
        for pp in range(2):
            row = pl.ds(2 * T * (d + 2) + T * pp, T)
            slot = rs + ((d + 2) * 2 + p) * 2
            push(dk_ref.at[row], rkv.at[d + 2, p, 0], slot, 2 * chip(d) + pp)
            push(dv_ref.at[row], rkv.at[d + 2, p, 1], slot + 1, 2 * chip(d) + pp)
    slot = rs + (2 * 2 + p) * 2
    push(dk_ref.at[rows(4 * T + T * o)], rkv.at[2, p, 0], slot, mate)
    push(dv_ref.at[rows(4 * T + T * o)], rkv.at[2, p, 1], slot + 1, mate)
    push(dq_ref.at[rows(T * o)], rq.at[p], qs, mate)

    part = bp_ref[pl.ds(nz * y, nz)].astype(f32)
    for k in yk:
        arrive(yrecv.at[k - 1], ys + k - 1)
    for k in yk:
        part = part + yrecv[k - 1].astype(f32)
    zsend[...] = part.astype(bf16)

    zs = take(nz)
    for k in zk:
        push(zsend.at[zpeer(k)], zrecv.at[k - 1], zs + k - 1, at(zpeer(k), y))
    for copy in loads:
        copy.wait()
    part = zsend[z].astype(f32)
    for k in reversed(zk):
        arrive(zrecv.at[k - 1], zs + k - 1)
        part = part + zrecv[k - 1].astype(f32)
    low = part.astype(bf16)
    own[...] = low
    ag[nz * y + z] = low

    gs = take(nz)
    for k in zk:
        push(own, ag.at[nz * y + z], gs + k - 1, at(zpeer(k), y))

    both = part.astype(bf16).astype(f32)
    rel_part = dot(both[:rb].astype(bf16), wv[0], 1, 1) + dot(both[rb:].astype(bf16), wv[1], 1, 1)
    for i in range(2 * nx):
        xpart[i] = rel_part[:, i * T : (i + 1) * T]
    xs = take(2 * nx)
    for k in mk:
        push(xpart.at[mpeer(k)], xrecv.at[k - 1], xs + k - 1,
             2 * c + lax.rem(mpeer(k), 2), mpeer(k) // 2)
    total = xpart[m]
    for k in mk:
        arrive(xrecv.at[k - 1], xs + k - 1)
        total = total + xrecv[k - 1]
    relz[z] = total
    ls = take(nz)
    for k in zk:
        push(xsum_src(relz, z), relz.at[z], ls + k - 1, at(zpeer(k), y))

    for k in reversed(zk):
        arrive(ag.at[nz * y + zpeer(nz - k)], gs + k - 1)
    hs = take(ny)
    mine = pl.ds(nz * y, nz)
    for k in yk:
        push(ag.at[mine], ag.at[mine], hs + k - 1, at(z, ypeer(k)))
    for k in reversed(zk):
        arrive(relz.at[zpeer(nz - k)], ls + k - 1)
    rely[y] = relz[...].reshape(nz * rb, T).astype(bf16)
    ms = take(ny)
    es = take(ny)
    for k in yk:
        push(rely.at[y], rely.at[y], ms + k - 1, at(z, ypeer(k)))
    push(rely.at[y], relp.at[y], es, mate)

    for d in (-2, -1, 0, 1, 2):
        for pp in range(2):
            if d != 0:
                arrive(rkv.at[d + 2, pp, 0], rs + ((d + 2) * 2 + pp) * 2)
                arrive(rkv.at[d + 2, pp, 1], rs + ((d + 2) * 2 + pp) * 2 + 1)
    arrive(rkv.at[2, o, 0], rs + (2 * 2 + o) * 2)
    arrive(rkv.at[2, o, 1], rs + (2 * 2 + o) * 2 + 1)
    arrive(rq.at[o], qs)
    for pp in range(2):
        col = slice(pp * T, (pp + 1) * T)
        dqo_ref[:, col] = rq[pp]
        for i, out in ((0, dko_ref), (1, dvo_ref)):
            x = rkv[0, pp, i].astype(f32)
            for d in range(1, 5):
                x = x + rkv[d, pp, i].astype(f32)
            out[:, col] = x.astype(bf16)

    for k in reversed(yk):
        arrive(ag.at[pl.ds(nz * ypeer(ny - k), nz)], hs + k - 1)
    every = ag[...].astype(f32)
    for i in range(2):
        grad = every[:, i * rb : (i + 1) * rb].reshape(nc * rb, T).astype(bf16)
        wtmp[i] = dot(relb[...], grad, 0, 0)
    first = lax.rem(c * dr2, T)
    theirs = pl.ds(pl.multiple_of(first + dr * o, dr), dr)
    ours = pl.ds(pl.multiple_of(first + dr * p, dr), dr)
    wsend[...] = wtmp[:, theirs]
    ws = take(1)
    push(wsend, wrecv, ws, mate)
    wko_ref[:, lanes(p)] = wtmp[0, ours]
    wqo_ref[:, lanes(p)] = wtmp[1, ours]

    for k in reversed(yk):
        arrive(rely.at[ypeer(ny - k)], ms + k - 1)
        push(rely.at[ypeer(ny - k)], relp.at[ypeer(ny - k)], es + k, mate)
    relo_ref[:, lanes(p)] = rely[...].reshape(nc * rb, T).astype(f32)
    arrive(wrecv, ws)
    wko_ref[:, lanes(o)] = wrecv[0]
    wqo_ref[:, lanes(o)] = wrecv[1]
    arrive(relp.at[y], es)
    for k in reversed(yk):
        arrive(relp.at[ypeer(ny - k)], es + k)
    relo_ref[:, lanes(o)] = relp[...].reshape(nc * rb, T).astype(f32)
    for copy in sent:
        copy.wait_send()


def xsum_src(ref, z):
    return ref.at[z]


def sums(bp, dq, dk, dv, rel, wq, wk, nz, ny, nx):
    nc = nz * ny
    buckets, width = rel.shape
    rb = buckets // nc
    dr = width // nc // 2
    return pl.pallas_call(
        functools.partial(sums_kernel, nz, ny, nx),
        out_shape=(
            jax.ShapeDtypeStruct((T, 2 * T), bf16),
            jax.ShapeDtypeStruct((T, 2 * T), bf16),
            jax.ShapeDtypeStruct((T, 2 * T), bf16),
            jax.ShapeDtypeStruct((buckets, 2 * T), f32),
            jax.ShapeDtypeStruct((dr, 2 * T), f32),
            jax.ShapeDtypeStruct((dr, 2 * T), f32),
        ),
        in_specs=[VM] + [ANY] * 6,
        out_specs=(VM,) * 6,
        scratch_shapes=[
            pltpu.VMEM((2, width, T), bf16),
            pltpu.VMEM((buckets, T), bf16),
            pltpu.VMEM((5, 2, 2, T, T), bf16),
            pltpu.VMEM((2, T, T), bf16),
            pltpu.VMEM((ny, nz, 2 * rb, T), bf16),
            pltpu.VMEM((nz, 2 * rb, T), bf16),
            pltpu.VMEM((nz, 2 * rb, T), bf16),
            pltpu.VMEM((2 * rb, T), bf16),
            pltpu.VMEM((nc, 2 * rb, T), bf16),
            pltpu.VMEM((2 * nx, rb, T), f32),
            pltpu.VMEM((2 * nx, rb, T), f32),
            pltpu.VMEM((nz, rb, T), f32),
            pltpu.VMEM((ny, nz * rb, T), bf16),
            pltpu.VMEM((ny, nz * rb, T), bf16),
            pltpu.VMEM((2, T, T), f32),
            pltpu.VMEM((2, dr, T), f32),
            pltpu.VMEM((2, dr, T), f32),
            pltpu.SemaphoreType.DMA((128,)),
            pltpu.SemaphoreType.DMA((128,)),
            pltpu.SemaphoreType.DMA((6,)),
        ],
        compiler_params=pltpu.CompilerParams(collective_id=1, has_side_effects=True),
        name="sums",
    )(bp, dq, dk, dv, rel, wq, wk)


def body(ny, queries, keys, values, out_grad, rel_emb, w_query, w_key, doc_lengths, bucket_table):
    nc = lax.axis_size("seq") // 2
    nx = lax.axis_size("head")
    rev = jnp.flip(bucket_table).reshape(1, -1)
    lens = doc_lengths.reshape(1, -1)
    q2, g2, kw, vw, pb = halo(queries, keys, values, out_grad, rel_emb, w_query, w_key, rev, nc)
    dq, dk, dv, bp = attention(q2, g2, kw, vw, pb, rev, lens, nc, rel_emb.shape[0])
    query_grad, key_grad, value_grad, rel_grad, wq_grad, wk_grad = sums(
        bp, dq, dk, dv, rel_emb, w_query, w_key, nc // ny, ny, nx
    )
    return (query_grad, key_grad, value_grad, rel_grad, wq_grad, wk_grad)


def solution(mesh, ny=NY):
    shard = P("seq", "head")
    return jax.shard_map(
        functools.partial(body, ny),
        mesh=mesh,
        in_specs=(shard,) * 4 + (P(), P(None, "head"), P(None, "head"), P(), P()),
        out_specs=(shard, shard, shard, P(None, "head"), shard, shard),
        check_vma=False,
    )
```

```python
import functools
import math

import jax
import jax.numpy as jnp
from jax import lax
from jax.experimental import pallas as pl
from jax.experimental.pallas import tpu as pltpu
from jax.sharding import PartitionSpec as P

HD = 64
T = 128
NY = 4
HALO = 2
TILES = 2 * (2 * HALO + 1)
WIDE = 9 * T
f32 = jnp.float32
bf16 = jnp.bfloat16
SCALE = 1.0 / math.sqrt(3.0 * HD)
ANY = pl.BlockSpec(memory_space=pl.ANY)
VM = pl.BlockSpec(memory_space=pltpu.VMEM)


def dot(a, b, ca=1, cb=0):
    return lax.dot_general(a, b, (((ca,), (cb,)), ((), ())), preferred_element_type=f32)


def remote(src, dst, send, recv, seq, head=None):
    where = {"seq": seq} if head is None else {"seq": seq, "head": head}
    return pltpu.make_async_remote_copy(
        src_ref=src, dst_ref=dst, send_sem=send, recv_sem=recv,
        device_id=where, device_id_type=pl.DeviceIdType.MESH,
    )


def greet(seq, head=None):
    where = {"seq": seq} if head is None else {"seq": seq, "head": head}
    pl.semaphore_signal(
        pltpu.get_barrier_semaphore(), inc=1, device_id=where,
        device_id_type=pl.DeviceIdType.MESH,
    )


def lanes(p):
    return pl.ds(pl.multiple_of(p * T, T), T)


def rows(start):
    return pl.ds(pl.multiple_of(start, T), T)


def tile(j):
    return slice(j * T, (j + 1) * T)


def skewed(x, first):
    return pltpu.roll(x, first, 1, stride=1, stride_axis=0)


def head_only(x, h):
    lane = lax.broadcasted_iota(jnp.int32, x.shape, 1)
    return jnp.where((lane < HD) if h == 0 else (lane >= HD), x, jnp.zeros_like(x))


def indicator(match):
    return match.astype(f32).astype(bf16)


def whole_kernel(
    nz, ny, nx,
    q_ref, k_ref, v_ref, g_ref, rel_ref, wq_ref, wk_ref, tab_ref, len_ref,
    dqo, dko, dvo, relo, relq, wko, wqo,
    rel_v, wv, qw, gw, kw, vw, pb, oht, q2, g2, k2, pqr, qrt, krt,
    sc, dp, prb, dsb, dsr, skb, dsa, ska, dkb, dvb, dqb, gt, ht,
    bp, rkv, rq, yrecv, zsend, zrecv, own, ag, xpart, xrecv, relz,
    wtmp, wsend, wrecv, send, recv, local,
):
    nc = nz * ny
    s = lax.axis_index("seq")
    hx = lax.axis_index("head")
    c, p = s // 2, lax.rem(s, 2)
    o = 1 - p
    mate = 2 * c + o
    z, y = c // ny, lax.rem(c, ny)
    m = 2 * hx + p
    buckets, width = rel_ref.shape
    span = tab_ref.shape[1]
    rb = buckets // nc
    dr2 = width // nc
    dr = dr2 // 2
    hops = [-1, 1, -2, 2]

    def chip(d):
        return lax.rem(c + d + nc, nc)

    def ypeer(k):
        return lax.rem(y + k, ny)

    def zpeer(k):
        return lax.rem(z + k, nz)

    def mpeer(k):
        return lax.rem(m + k, 2 * nx)

    def at(zz, yy):
        return 2 * (zz * ny + yy) + p

    yk = sorted(range(1, ny), key=lambda k: -min(k, ny - k))
    zk = sorted(range(1, nz), key=lambda k: -min(k, nz - k))
    mk = range(1, 2 * nx)

    for k in zk:
        greet(at(zpeer(k), y))
    for k in yk:
        greet(at(z, ypeer(k)))
    for d in hops:
        for pp in range(2):
            greet(2 * chip(d) + pp)
    for k in mk:
        greet(2 * c + lax.rem(mpeer(k), 2), mpeer(k) // 2)
    greet(mate)

    loads = []

    def load(src, dst):
        copy = pltpu.make_async_copy(src, dst, local.at[len(loads)])
        copy.start()
        loads.append(copy)

    load(rel_ref, rel_v)
    load(wk_ref.at[:, lanes(p)], wv.at[0])
    load(wq_ref.at[:, lanes(p)], wv.at[1])
    load(k_ref.at[:, lanes(p)], kw.at[rows(2 * HALO * T + T * p)])
    load(v_ref.at[:, lanes(p)], vw.at[rows(2 * HALO * T + T * p)])
    load(q_ref.at[:, lanes(p)], qw.at[rows(T * p)])
    load(g_ref.at[:, lanes(p)], gw.at[rows(T * p)])

    ri = lax.broadcasted_iota(jnp.int32, (T, T), 0)
    ci = lax.broadcasted_iota(jnp.int32, (T, T), 1)
    flip = indicator(ri + ci == T - 1)
    table = jnp.broadcast_to(tab_ref[...], (8, span))
    high = table // 256
    low = (table - 256 * high).astype(f32).astype(bf16)
    high = high.astype(f32).astype(bf16)
    blocks = span // T
    rev = jnp.concatenate(
        [
            256.0 * dot(high[:, tile(blocks - 1 - b)], flip) + dot(low[:, tile(blocks - 1 - b)], flip)
            for b in range(blocks)
        ],
        1,
    )[:1]
    number = lax.broadcasted_iota(jnp.int32, (T, span), 0).astype(f32)
    for b in range(buckets // T):
        oht[tile(b)] = indicator(number + float(b * T) == rev)
    column = jnp.transpose(jnp.broadcast_to(rev, (T, span)))
    lane = lax.broadcasted_iota(jnp.int32, column.shape, 1).astype(f32)
    onehot = jnp.concatenate(
        [indicator(column == lane + float(T * b)) for b in range(buckets // T)], 1
    )

    ndocs = len_ref.shape[1]
    de = lax.broadcasted_iota(jnp.int32, (ndocs, ndocs), 1)
    dd = lax.broadcasted_iota(jnp.int32, (ndocs, ndocs), 0)
    lens = jnp.broadcast_to(len_ref[...], (ndocs, ndocs))
    ends = jnp.sum(jnp.where(de <= dd, lens, 0), axis=1, keepdims=True)
    shift = (c - HALO) * 2 * T
    pos = lax.broadcasted_iota(jnp.int32, (ndocs, 2 * T), 1) + c * 2 * T
    first = jnp.max(jnp.where(ends <= pos, ends, 0), axis=0, keepdims=True) - shift
    last = jnp.min(jnp.where(ends > pos, ends, 1 << 30), axis=0, keepdims=True) - shift

    for copy in loads[:3]:
        copy.wait()
    pos_key = dot(rel_v[...], wv[0]).astype(bf16)
    pos_query = dot(rel_v[...], wv[1]).astype(bf16)
    pb[...] = dot(onehot, jnp.concatenate([pos_key, pos_query], 1)).astype(bf16)
    for h in range(2):
        pqr[h, : 2 * T] = jnp.zeros((2 * T, T), bf16)
        pqr[h, 2 * T : 2 * T + span] = head_only(pb[:, T:], h)
        pqr[h, 2 * T + span :] = jnp.zeros((2 * T, T), bf16)
    ht[...] = jnp.zeros_like(ht)

    pl.semaphore_wait(
        pltpu.get_barrier_semaphore(), len(zk) + len(yk) + 8 + len(mk) + 1
    )

    sent = []
    slots = [0]

    def push(src, dst, slot, seq, head=None):
        copy = remote(src, dst, send.at[len(sent)], recv.at[slot], seq, head)
        copy.start()
        sent.append(copy)

    def take(count):
        base = slots[0]
        slots[0] += count
        return base

    def arrive(dst, slot):
        remote(dst, dst, send.at[0], recv.at[slot], s).wait_recv()

    near = take(4)
    hs = take(20)
    row = rows(T * p)
    push(q_ref.at[:, lanes(o)], qw.at[row], near, mate)
    push(g_ref.at[:, lanes(o)], gw.at[row], near + 1, mate)
    row = rows(2 * HALO * T + T * p)
    push(k_ref.at[:, lanes(o)], kw.at[row], near + 2, mate)
    push(v_ref.at[:, lanes(o)], vw.at[row], near + 3, mate)
    for d in hops:
        for pp in range(2):
            row = rows(2 * T * (HALO - d) + T * p)
            base = hs + ((d + HALO) * 2 + p) * 2
            push(k_ref.at[:, pl.ds(pp * T, T)], kw.at[row], base, 2 * chip(d) + pp)
            push(v_ref.at[:, pl.ds(pp * T, T)], vw.at[row], base + 1, 2 * chip(d) + pp)
    for copy in loads[3:]:
        copy.wait()
    arrive(qw.at[rows(T * o)], near)
    arrive(gw.at[rows(T * o)], near + 1)

    for h in range(2):
        q2[h] = head_only(qw[...], h)
        g2[h] = head_only(gw[...], h)
    for r in range(2):
        qrt[:, tile(r)] = jnp.transpose(dot(flip, qw[tile(r)])).astype(bf16)
    for h in range(2):
        sc[h, WIDE:, :T] = jnp.zeros((T, T), f32)
        sc[h, :T, T:] = jnp.zeros((T, T), f32)
        for r in range(2):
            a = dot(q2[h, tile(r)], pb[:, :T], 1, 1)
            a = skewed(jnp.concatenate([a, jnp.zeros((T, WIDE - span), f32)], 1), 1)
            for j in range(9):
                sc[h, tile(r + j), tile(r)] = jnp.transpose(a[:, tile(j)])

    arrive(kw.at[rows(2 * HALO * T + T * o)], near + 2)
    arrive(vw.at[rows(2 * HALO * T + T * o)], near + 3)

    top = [jnp.full((8, 2 * T), -1e30, f32) for _ in range(2)]

    def band(j):
        return slice((9 - j) * T, (9 - j) * T + 3 * T)

    def fold(x, op):
        return op(x.reshape(T // 8, 8, 2 * T), axis=0)

    def score(j):
        kt = kw[tile(j)]
        krt[:, tile(j)] = jnp.transpose(dot(flip, kt)).astype(bf16)
        key = lax.broadcasted_iota(jnp.int32, (T, 2 * T), 0) + j * T
        keep = (key >= first) & (key < last)
        for h in range(2):
            k2[h, tile(j)] = head_only(kt, h)
            b = skewed(dot(kt, pqr[h, band(j)], 1, 1), 2 * T + 1)[:, : 2 * T]
            x = SCALE * (dot(kt, q2[h], 1, 1) + sc[h, tile(j)] + b)
            x = jnp.where(keep, x, -1e30)
            sc[h, tile(j)] = x
            top[h] = jnp.maximum(top[h], fold(x, jnp.max))
            dp[h, tile(j)] = dot(vw[tile(j)], g2[h], 1, 1)

    score(4)
    score(5)
    for d in (-1, 1, -2, 2):
        for pp in range(2):
            j = 2 * (HALO - (-d)) + pp
            base = hs + ((-d + HALO) * 2 + pp) * 2
            arrive(kw.at[tile(j)], base)
            arrive(vw.at[tile(j)], base + 1)
        score(2 * (HALO + d))
        score(2 * (HALO + d) + 1)

    for h in range(2):
        high_score = jnp.max(top[h], axis=0, keepdims=True)
        total = jnp.zeros((8, 2 * T), f32)
        along = jnp.zeros((8, 2 * T), f32)
        for j in range(TILES):
            x = jnp.exp(sc[h, tile(j)] - high_score)
            sc[h, tile(j)] = x
            total = total + fold(x, jnp.sum)
            along = along + fold(x * dp[h, tile(j)], jnp.sum)
        inv = 1.0 / jnp.sum(total, axis=0, keepdims=True)
        row_dot = jnp.sum(along, axis=0, keepdims=True) * inv
        half = slice(h * HD, (h + 1) * HD)
        for j in range(TILES):
            prob = sc[h, tile(j)] * inv
            ds = (prob * (dp[h, tile(j)] - row_dot)).astype(bf16)
            prb[h, tile(j)] = prob.astype(bf16)
            dsb[h, tile(j)] = ds
            back = dot(flip, ds)
            dsr[h, tile(j)] = back.astype(bf16)
            skew = skewed(jnp.concatenate([back, jnp.zeros((T, T), f32)], 1), 0).astype(bf16)
            skb[h, tile(j)] = skew
            ht[half, band(j)] += dot(krt[half, tile(j)], skew)
        for r in range(2):
            back = dot(flip, dsb[h, r * T : r * T + WIDE, tile(r)], 1, 1)
            dsa[h, tile(r)] = back.astype(bf16)
            skew = skewed(back, span)[:, :span].astype(bf16)
            ska[h, tile(r)] = skew
            part = dot(qrt[half, tile(r)], skew)
            if r == 0:
                gt[half] = part
            else:
                gt[half] += part

    bk = SCALE * dot(oht[...], gt[...].astype(bf16), 1, 1)
    bq = SCALE * dot(oht[...], ht[:, 2 * T : 2 * T + span].astype(bf16), 1, 1)
    bp[...] = jnp.concatenate([bk.reshape(nc, rb, T), bq.reshape(nc, rb, T)], 1).astype(bf16)

    ys = take(ny)
    for k in yk:
        push(bp.at[pl.ds(nz * ypeer(k), nz)], yrecv.at[k - 1], ys + k - 1, at(z, ypeer(k)))

    for j in (0, 1, 8, 9, 2, 3, 6, 7, 4, 5):
        dv = dot(prb[0, tile(j)], g2[0]) + dot(prb[1, tile(j)], g2[1])
        dvb[tile(j)] = dv.astype(bf16)
        dk = dot(dsr[0, tile(j)], q2[0]) + dot(dsr[1, tile(j)], q2[1])
        dk = dk + dot(skb[0, tile(j)], pqr[0, band(j)]) + dot(skb[1, tile(j)], pqr[1, band(j)])
        dkb[tile(j)] = dot(flip, (SCALE * dk).astype(bf16)).astype(bf16)
    for r in range(2):
        reach = slice(r * T, r * T + WIDE)
        dq = dot(dsa[0, tile(r)], k2[0, reach]) + dot(dsa[1, tile(r)], k2[1, reach])
        for h in range(2):
            dq = dq + head_only(dot(ska[h, tile(r)], pb[:, :T]), h)
        dqb[tile(r)] = dot(flip, (SCALE * dq).astype(bf16)).astype(bf16)

    part = bp[pl.ds(nz * y, nz)].astype(f32)
    for k in yk:
        arrive(yrecv.at[k - 1], ys + k - 1)
    for k in yk:
        part = part + yrecv[k - 1].astype(f32)
    zsend[...] = part.astype(bf16)

    zs = take(nz)
    for k in zk:
        push(zsend.at[zpeer(k)], zrecv.at[k - 1], zs + k - 1, at(zpeer(k), y))

    rs = take(20)
    qs = take(1)
    for d in hops:
        for pp in range(2):
            row = tile(2 * (d + HALO) + pp)
            slot = rs + ((d + HALO) * 2 + p) * 2
            push(dkb.at[row], rkv.at[d + HALO, p, 0], slot, 2 * chip(d) + pp)
            push(dvb.at[row], rkv.at[d + HALO, p, 1], slot + 1, 2 * chip(d) + pp)
    row = rows(2 * HALO * T + T * o)
    slot = rs + (HALO * 2 + p) * 2
    push(dkb.at[row], rkv.at[HALO, p, 0], slot, mate)
    push(dvb.at[row], rkv.at[HALO, p, 1], slot + 1, mate)
    push(dqb.at[rows(T * o)], rq, qs, mate)

    part = zsend[z].astype(f32)
    for k in reversed(zk):
        arrive(zrecv.at[k - 1], zs + k - 1)
        part = part + zrecv[k - 1].astype(f32)
    low = part.astype(bf16)
    own[...] = low
    ag[nz * y + z] = low

    gs = take(nz)
    for k in zk:
        push(own, ag.at[nz * y + z], gs + k - 1, at(zpeer(k), y))

    both = low.astype(f32)
    rel_part = dot(both[:rb].astype(bf16), wv[0], 1, 1) + dot(both[rb:].astype(bf16), wv[1], 1, 1)
    for i in range(2 * nx):
        xpart[i] = rel_part[:, tile(i)]
    xs = take(2 * nx)
    for k in mk:
        push(xpart.at[mpeer(k)], xrecv.at[k - 1], xs + k - 1,
             2 * c + lax.rem(mpeer(k), 2), mpeer(k) // 2)
    total = xpart[m]
    for k in mk:
        arrive(xrecv.at[k - 1], xs + k - 1)
        total = total + xrecv[k - 1]
    relz[z] = total
    ls = take(nz)
    for k in zk:
        push(relz.at[z], relz.at[z], ls + k - 1, at(zpeer(k), y))

    for k in reversed(zk):
        arrive(ag.at[nz * y + zpeer(nz - k)], gs + k - 1)
    us = take(ny)
    mine = pl.ds(nz * y, nz)
    for k in yk:
        push(ag.at[mine], ag.at[mine], us + k - 1, at(z, ypeer(k)))

    dqo[:, lanes(p)] = dqb[rows(T * p)]
    arrive(rq, qs)
    dqo[:, lanes(o)] = rq[...]
    row = rows(2 * HALO * T + T * p)
    rkv[HALO, p, 0] = dkb[row]
    rkv[HALO, p, 1] = dvb[row]
    arrive(rkv.at[HALO, o, 0], rs + (HALO * 2 + o) * 2)
    arrive(rkv.at[HALO, o, 1], rs + (HALO * 2 + o) * 2 + 1)
    for d in hops:
        for pp in range(2):
            arrive(rkv.at[d + HALO, pp, 0], rs + ((d + HALO) * 2 + pp) * 2)
            arrive(rkv.at[d + HALO, pp, 1], rs + ((d + HALO) * 2 + pp) * 2 + 1)
    for pp in range(2):
        for i, out in ((0, dko), (1, dvo)):
            x = rkv[0, pp, i].astype(f32)
            for d in range(1, 2 * HALO + 1):
                x = x + rkv[d, pp, i].astype(f32)
            out[:, tile(pp)] = x.astype(bf16)

    for k in reversed(zk):
        arrive(relz.at[zpeer(nz - k)], ls + k - 1)
    relo[y] = relz[...].reshape(nz * rb, T).astype(bf16)
    ms = take(ny)
    es = take(ny)
    for k in yk:
        push(relo.at[y], relo.at[y], ms + k - 1, at(z, ypeer(k)))
    push(relo.at[y], relq.at[y], es, mate)

    for k in reversed(yk):
        arrive(ag.at[pl.ds(nz * ypeer(ny - k), nz)], us + k - 1)
    every = ag[...].astype(f32)
    for i in range(2):
        grad = every[:, i * rb : (i + 1) * rb].reshape(buckets, T).astype(bf16)
        wtmp[i] = dot(rel_v[:, lanes(c * dr2 // T)], grad, 0, 0)
    start = lax.rem(c * dr2, T)
    wsend[...] = wtmp[:, pl.ds(pl.multiple_of(start + dr * o, dr), dr)]
    ws = take(1)
    push(wsend, wrecv, ws, mate)
    ours = pl.ds(pl.multiple_of(start + dr * p, dr), dr)
    wko[:, lanes(p)] = wtmp[0, ours]
    wqo[:, lanes(p)] = wtmp[1, ours]

    for k in reversed(yk):
        arrive(relo.at[ypeer(ny - k)], ms + k - 1)
        push(relo.at[ypeer(ny - k)], relq.at[ypeer(ny - k)], es + k, mate)
    arrive(wrecv, ws)
    wko[:, lanes(o)] = wrecv[0]
    wqo[:, lanes(o)] = wrecv[1]
    arrive(relq.at[y], es)
    for k in reversed(yk):
        arrive(relq.at[ypeer(ny - k)], es + k)
    for copy in sent:
        copy.wait_send()


def copy_kernel(dq, dk, dv, rel, relq, wk, wq, dqo, dko, dvo, relo, wqo, wko):
    p = lax.rem(lax.axis_index("seq"), 2)
    dqo[...] = dq[...]
    dko[...] = dk[...]
    dvo[...] = dv[...]
    relo[:, lanes(p)] = rel[...].reshape(relo.shape[0], T).astype(f32)
    relo[:, lanes(1 - p)] = relq[...].reshape(relo.shape[0], T).astype(f32)
    wqo[...] = wq[...]
    wko[...] = wk[...]


def body(ny, queries, keys, values, out_grad, rel_emb, w_query, w_key, doc_lengths, bucket_table):
    nc = lax.axis_size("seq") // 2
    nx = lax.axis_size("head")
    nz = nc // ny
    buckets, width = rel_emb.shape
    span = bucket_table.shape[0]
    rb = buckets // nc
    dr = width // nc // 2
    keys_in = TILES * T
    shape = jax.ShapeDtypeStruct
    tab = bucket_table.reshape(1, -1)
    lens = doc_lengths.reshape(1, -1)
    results = pl.pallas_call(
        functools.partial(whole_kernel, nz, ny, nx),
        out_shape=(
            shape((T, 2 * T), bf16),
            shape((T, 2 * T), bf16),
            shape((T, 2 * T), bf16),
            shape((ny, nz * rb, T), bf16),
            shape((ny, nz * rb, T), bf16),
            shape((dr, 2 * T), f32),
            shape((dr, 2 * T), f32),
        ),
        in_specs=[ANY] * 7 + [VM] * 2,
        out_specs=(VM,) * 7,
        scratch_shapes=[
            pltpu.VMEM((buckets, width), bf16),
            pltpu.VMEM((2, width, T), bf16),
            pltpu.VMEM((2 * T, T), bf16),
            pltpu.VMEM((2 * T, T), bf16),
            pltpu.VMEM((keys_in, T), bf16),
            pltpu.VMEM((keys_in, T), bf16),
            pltpu.VMEM((span, 2 * T), bf16),
            pltpu.VMEM((buckets, span), bf16),
            pltpu.VMEM((2, 2 * T, T), bf16),
            pltpu.VMEM((2, 2 * T, T), bf16),
            pltpu.VMEM((2, keys_in, T), bf16),
            pltpu.VMEM((2, span + 4 * T, T), bf16),
            pltpu.VMEM((T, 2 * T), bf16),
            pltpu.VMEM((T, keys_in), bf16),
            pltpu.VMEM((2, keys_in, 2 * T), f32),
            pltpu.VMEM((2, keys_in, 2 * T), f32),
            pltpu.VMEM((2, keys_in, 2 * T), bf16),
            pltpu.VMEM((2, keys_in, 2 * T), bf16),
            pltpu.VMEM((2, keys_in, 2 * T), bf16),
            pltpu.VMEM((2, keys_in, 3 * T), bf16),
            pltpu.VMEM((2, 2 * T, WIDE), bf16),
            pltpu.VMEM((2, 2 * T, span), bf16),
            pltpu.VMEM((keys_in, T), bf16),
            pltpu.VMEM((keys_in, T), bf16),
            pltpu.VMEM((2 * T, T), bf16),
            pltpu.VMEM((T, span), f32),
            pltpu.VMEM((T, span + 4 * T), f32),
            pltpu.VMEM((nc, 2 * rb, T), bf16),
            pltpu.VMEM((5, 2, 2, T, T), bf16),
            pltpu.VMEM((T, T), bf16),
            pltpu.VMEM((ny, nz, 2 * rb, T), bf16),
            pltpu.VMEM((nz, 2 * rb, T), bf16),
            pltpu.VMEM((nz, 2 * rb, T), bf16),
            pltpu.VMEM((2 * rb, T), bf16),
            pltpu.VMEM((nc, 2 * rb, T), bf16),
            pltpu.VMEM((2 * nx, rb, T), f32),
            pltpu.VMEM((2 * nx, rb, T), f32),
            pltpu.VMEM((nz, rb, T), f32),
            pltpu.VMEM((2, T, T), f32),
            pltpu.VMEM((2, dr, T), f32),
            pltpu.VMEM((2, dr, T), f32),
            pltpu.SemaphoreType.DMA((144,)),
            pltpu.SemaphoreType.DMA((144,)),
            pltpu.SemaphoreType.DMA((7,)),
        ],
        compiler_params=pltpu.CompilerParams(collective_id=0, has_side_effects=True),
        name="whole",
    )(queries, keys, values, out_grad, rel_emb, w_query, w_key, tab, lens)
    return tuple(
        pl.pallas_call(
            copy_kernel,
            out_shape=(
                shape((T, 2 * T), bf16),
                shape((T, 2 * T), bf16),
                shape((T, 2 * T), bf16),
                shape((buckets, 2 * T), f32),
                shape((dr, 2 * T), f32),
                shape((dr, 2 * T), f32),
            ),
            in_specs=[VM] * 7,
            out_specs=(VM,) * 6,
            name="results",
        )(*results)
    )


def solution(mesh, ny=NY):
    shard = P("seq", "head")
    return jax.shard_map(
        functools.partial(body, ny),
        mesh=mesh,
        in_specs=(shard,) * 4 + (P(), P(None, "head"), P(None, "head"), P(), P()),
        out_specs=(shard, shard, shard, P(None, "head"), shard, shard),
        check_vma=False,
    )
```

```python
import functools
import math

import jax
import jax.numpy as jnp
from jax import lax
from jax.experimental import pallas as pl
from jax.experimental.pallas import tpu as pltpu
from jax.sharding import PartitionSpec as P

HD = 64
T = 128
NY = 4
HALO = 2
TILES = 2 * (2 * HALO + 1)
WIDE = 9 * T
f32 = jnp.float32
bf16 = jnp.bfloat16
SCALE = 1.0 / math.sqrt(3.0 * HD)
ANY = pl.BlockSpec(memory_space=pl.ANY)
VM = pl.BlockSpec(memory_space=pltpu.VMEM)


def dot(a, b, ca=1, cb=0):
    return lax.dot_general(a, b, (((ca,), (cb,)), ((), ())), preferred_element_type=f32)


def remote(src, dst, send, recv, seq, head=None):
    where = {"seq": seq} if head is None else {"seq": seq, "head": head}
    return pltpu.make_async_remote_copy(
        src_ref=src, dst_ref=dst, send_sem=send, recv_sem=recv,
        device_id=where, device_id_type=pl.DeviceIdType.MESH,
    )


def greet(seq, head=None):
    where = {"seq": seq} if head is None else {"seq": seq, "head": head}
    pl.semaphore_signal(
        pltpu.get_barrier_semaphore(), inc=1, device_id=where,
        device_id_type=pl.DeviceIdType.MESH,
    )


def lanes(p):
    return pl.ds(pl.multiple_of(p * T, T), T)


def rows(start):
    return pl.ds(pl.multiple_of(start, T), T)


def tile(j):
    return slice(j * T, (j + 1) * T)


def skewed(x, first):
    return pltpu.roll(x, first, 1, stride=1, stride_axis=0)


def head_only(x, h):
    lane = lax.broadcasted_iota(jnp.int32, x.shape, 1)
    return jnp.where((lane < HD) if h == 0 else (lane >= HD), x, jnp.zeros_like(x))


def indicator(match):
    return match.astype(f32).astype(bf16)


def whole_kernel(
    nz, ny, nx,
    q_ref, k_ref, v_ref, g_ref, rel_ref, wq_ref, wk_ref, tab_ref, len_ref,
    dqo, dko, dvo, relo, relq, wko, wqo,
    rel_v, wv, qw, gw, kw, vw, pb, oht, q2, g2, k2, pqr, qrt, krt,
    sc, dp, dsb, dsr, skb, dsa, ska, dkb, dvb, dqb, gt, ht,
    bp, rkv, rq, yrecv, zsend, zrecv, own, ag, xpart, xrecv, relz,
    wtmp, wsend, wrecv, send, recv, local,
):
    nc = nz * ny
    s = lax.axis_index("seq")
    hx = lax.axis_index("head")
    c, p = s // 2, lax.rem(s, 2)
    o = 1 - p
    mate = 2 * c + o
    z, y = c // ny, lax.rem(c, ny)
    m = 2 * hx + p
    buckets, width = rel_ref.shape
    span = tab_ref.shape[1]
    rb = buckets // nc
    dr2 = width // nc
    dr = dr2 // 2
    hops = [-1, 1, -2, 2]

    def chip(d):
        return lax.rem(c + d + nc, nc)

    def ypeer(k):
        return lax.rem(y + k, ny)

    def zpeer(k):
        return lax.rem(z + k, nz)

    def mpeer(k):
        return lax.rem(m + k, 2 * nx)

    def at(zz, yy):
        return 2 * (zz * ny + yy) + p

    yk = sorted(range(1, ny), key=lambda k: -min(k, ny - k))
    zk = sorted(range(1, nz), key=lambda k: -min(k, nz - k))
    mk = range(1, 2 * nx)

    for k in zk:
        greet(at(zpeer(k), y))
    for k in yk:
        greet(at(z, ypeer(k)))
    for d in hops:
        for pp in range(2):
            greet(2 * chip(d) + pp)
    for k in mk:
        greet(2 * c + lax.rem(mpeer(k), 2), mpeer(k) // 2)
    greet(mate)

    loads = []

    def load(src, dst):
        copy = pltpu.make_async_copy(src, dst, local.at[len(loads)])
        copy.start()
        loads.append(copy)

    load(rel_ref, rel_v)
    load(wk_ref.at[:, lanes(p)], wv.at[0])
    load(wq_ref.at[:, lanes(p)], wv.at[1])
    load(k_ref.at[:, lanes(p)], kw.at[rows(2 * HALO * T + T * p)])
    load(v_ref.at[:, lanes(p)], vw.at[rows(2 * HALO * T + T * p)])
    load(q_ref.at[:, lanes(p)], qw.at[rows(T * p)])
    load(g_ref.at[:, lanes(p)], gw.at[rows(T * p)])

    pl.semaphore_wait(
        pltpu.get_barrier_semaphore(), len(zk) + len(yk) + 8 + len(mk) + 1
    )

    sent = []
    slots = [0]

    def push(src, dst, slot, seq, head=None):
        copy = remote(src, dst, send.at[len(sent)], recv.at[slot], seq, head)
        copy.start()
        sent.append(copy)

    def take(count):
        base = slots[0]
        slots[0] += count
        return base

    def arrive(dst, slot):
        remote(dst, dst, send.at[0], recv.at[slot], s).wait_recv()

    near = take(4)
    hs = take(20)
    row = rows(T * p)
    push(q_ref.at[:, lanes(o)], qw.at[row], near, mate)
    push(g_ref.at[:, lanes(o)], gw.at[row], near + 1, mate)
    row = rows(2 * HALO * T + T * p)
    push(k_ref.at[:, lanes(o)], kw.at[row], near + 2, mate)
    push(v_ref.at[:, lanes(o)], vw.at[row], near + 3, mate)
    for d in hops:
        for pp in range(2):
            row = rows(2 * T * (HALO - d) + T * p)
            base = hs + ((d + HALO) * 2 + p) * 2
            push(k_ref.at[:, pl.ds(pp * T, T)], kw.at[row], base, 2 * chip(d) + pp)
            push(v_ref.at[:, pl.ds(pp * T, T)], vw.at[row], base + 1, 2 * chip(d) + pp)
    ri = lax.broadcasted_iota(jnp.int32, (T, T), 0)
    ci = lax.broadcasted_iota(jnp.int32, (T, T), 1)
    flip = indicator(ri + ci == T - 1)
    table = jnp.broadcast_to(tab_ref[...], (8, span))
    high = table // 256
    low = (table - 256 * high).astype(f32).astype(bf16)
    high = high.astype(f32).astype(bf16)
    blocks = span // T
    rev = jnp.concatenate(
        [
            256.0 * dot(high[:, tile(blocks - 1 - b)], flip) + dot(low[:, tile(blocks - 1 - b)], flip)
            for b in range(blocks)
        ],
        1,
    )[:1]
    number = lax.broadcasted_iota(jnp.int32, (T, span), 0).astype(f32)
    for b in range(buckets // T):
        oht[tile(b)] = indicator(number + float(b * T) == rev)
    column = jnp.transpose(jnp.broadcast_to(rev, (T, span)))
    lane = lax.broadcasted_iota(jnp.int32, column.shape, 1).astype(f32)
    onehot = jnp.concatenate(
        [indicator(column == lane + float(T * b)) for b in range(buckets // T)], 1
    )

    ndocs = len_ref.shape[1]
    de = lax.broadcasted_iota(jnp.int32, (ndocs, ndocs), 1)
    dd = lax.broadcasted_iota(jnp.int32, (ndocs, ndocs), 0)
    lens = jnp.broadcast_to(len_ref[...], (ndocs, ndocs))
    ends = jnp.sum(jnp.where(de <= dd, lens, 0), axis=1, keepdims=True)
    shift = (c - HALO) * 2 * T
    pos = lax.broadcasted_iota(jnp.int32, (ndocs, 2 * T), 1) + c * 2 * T
    first = jnp.max(jnp.where(ends <= pos, ends, 0), axis=0, keepdims=True) - shift
    last = jnp.min(jnp.where(ends > pos, ends, 1 << 30), axis=0, keepdims=True) - shift

    for copy in loads[:3]:
        copy.wait()
    pos_key = dot(rel_v[...], wv[0]).astype(bf16)
    pos_query = dot(rel_v[...], wv[1]).astype(bf16)
    pb[...] = dot(onehot, jnp.concatenate([pos_key, pos_query], 1)).astype(bf16)
    for h in range(2):
        pqr[h, : 2 * T] = jnp.zeros((2 * T, T), bf16)
        pqr[h, 2 * T : 2 * T + span] = head_only(pb[:, T:], h)
        pqr[h, 2 * T + span :] = jnp.zeros((2 * T, T), bf16)
    ht[...] = jnp.zeros_like(ht)

    for copy in loads[3:]:
        copy.wait()
    arrive(qw.at[rows(T * o)], near)
    arrive(gw.at[rows(T * o)], near + 1)

    for h in range(2):
        q2[h] = head_only(qw[...], h)
        g2[h] = head_only(gw[...], h)
    for r in range(2):
        qrt[:, tile(r)] = jnp.transpose(dot(flip, qw[tile(r)])).astype(bf16)
    for h in range(2):
        sc[h, WIDE:, :T] = jnp.zeros((T, T), f32)
        sc[h, :T, T:] = jnp.zeros((T, T), f32)
        for r in range(2):
            a = dot(q2[h, tile(r)], pb[:, :T], 1, 1)
            a = skewed(jnp.concatenate([a, jnp.zeros((T, WIDE - span), f32)], 1), 1)
            for j in range(9):
                sc[h, tile(r + j), tile(r)] = jnp.transpose(a[:, tile(j)])

    arrive(kw.at[rows(2 * HALO * T + T * o)], near + 2)
    arrive(vw.at[rows(2 * HALO * T + T * o)], near + 3)

    top = [jnp.full((8, 2 * T), -1e30, f32) for _ in range(2)]

    def band(j):
        return slice((9 - j) * T, (9 - j) * T + 3 * T)

    def fold(x, op):
        return op(x.reshape(T // 8, 8, 2 * T), axis=0)

    def score(j):
        kt = kw[tile(j)]
        krt[:, tile(j)] = jnp.transpose(dot(flip, kt)).astype(bf16)
        key = lax.broadcasted_iota(jnp.int32, (T, 2 * T), 0) + j * T
        keep = (key >= first) & (key < last)
        for h in range(2):
            k2[h, tile(j)] = head_only(kt, h)
            b = skewed(dot(kt, pqr[h, band(j)], 1, 1), 2 * T + 1)[:, : 2 * T]
            x = SCALE * (dot(kt, q2[h], 1, 1) + sc[h, tile(j)] + b)
            x = jnp.where(keep, x, -1e30)
            sc[h, tile(j)] = x
            top[h] = jnp.maximum(top[h], fold(x, jnp.max))
            dp[h, tile(j)] = dot(vw[tile(j)], g2[h], 1, 1)

    score(4)
    score(5)
    for d in (-1, 1, -2, 2):
        for pp in range(2):
            j = 2 * (HALO - (-d)) + pp
            base = hs + ((-d + HALO) * 2 + pp) * 2
            arrive(kw.at[tile(j)], base)
            arrive(vw.at[tile(j)], base + 1)
        score(2 * (HALO + d))
        score(2 * (HALO + d) + 1)

    inv, row_dot = [], []
    for h in range(2):
        high_score = jnp.max(top[h], axis=0, keepdims=True)
        total = jnp.zeros((8, 2 * T), f32)
        along = jnp.zeros((8, 2 * T), f32)
        for j in range(TILES):
            x = jnp.exp(sc[h, tile(j)] - high_score)
            sc[h, tile(j)] = x
            total = total + fold(x, jnp.sum)
            along = along + fold(x * dp[h, tile(j)], jnp.sum)
        inv.append(1.0 / jnp.sum(total, axis=0, keepdims=True))
        row_dot.append(jnp.sum(along, axis=0, keepdims=True) * inv[h])

    far_first = [j for d in (-2, 2, -1, 1, 0) for j in (2 * (d + HALO), 2 * (d + HALO) + 1)]
    for j in far_first:
        dv = jnp.zeros((T, T), f32)
        for h in range(2):
            prob = (sc[h, tile(j)] * inv[h]).astype(bf16)
            dv = dv + dot(prob, g2[h])
        dvb[tile(j)] = dv.astype(bf16)
    rs = take(20)

    def give_back(grad, i):
        for d in reversed(hops):
            for pp in range(2):
                push(grad.at[tile(2 * (d + HALO) + pp)], rkv.at[d + HALO, p, i],
                     rs + ((d + HALO) * 2 + p) * 2 + i, 2 * chip(d) + pp)
        push(grad.at[rows(2 * HALO * T + T * o)], rkv.at[HALO, p, i],
             rs + (HALO * 2 + p) * 2 + i, mate)

    give_back(dvb, 1)

    for h in range(2):
        half = slice(h * HD, (h + 1) * HD)
        for j in range(TILES):
            prob = sc[h, tile(j)] * inv[h]
            ds = (prob * (dp[h, tile(j)] - row_dot[h])).astype(bf16)
            dsb[h, tile(j)] = ds
            back = dot(flip, ds)
            dsr[h, tile(j)] = back.astype(bf16)
            skew = skewed(jnp.concatenate([back, jnp.zeros((T, T), f32)], 1), 0).astype(bf16)
            skb[h, tile(j)] = skew
            ht[half, band(j)] += dot(krt[half, tile(j)], skew)
        for r in range(2):
            back = dot(flip, dsb[h, r * T : r * T + WIDE, tile(r)], 1, 1)
            dsa[h, tile(r)] = back.astype(bf16)
            skew = skewed(back, span)[:, :span].astype(bf16)
            ska[h, tile(r)] = skew
            part = dot(qrt[half, tile(r)], skew)
            if r == 0:
                gt[half] = part
            else:
                gt[half] += part

    bk = SCALE * dot(oht[...], gt[...].astype(bf16), 1, 1)
    bq = SCALE * dot(oht[...], ht[:, 2 * T : 2 * T + span].astype(bf16), 1, 1)
    bp[...] = jnp.concatenate([bk.reshape(nc, rb, T), bq.reshape(nc, rb, T)], 1).astype(bf16)

    ys = take(ny)
    for k in yk:
        push(bp.at[pl.ds(nz * ypeer(k), nz)], yrecv.at[k - 1], ys + k - 1, at(z, ypeer(k)))

    for j in far_first:
        dk = dot(dsr[0, tile(j)], q2[0]) + dot(dsr[1, tile(j)], q2[1])
        dk = dk + dot(skb[0, tile(j)], pqr[0, band(j)]) + dot(skb[1, tile(j)], pqr[1, band(j)])
        dkb[tile(j)] = dot(flip, (SCALE * dk).astype(bf16)).astype(bf16)
    for r in range(2):
        reach = slice(r * T, r * T + WIDE)
        dq = dot(dsa[0, tile(r)], k2[0, reach]) + dot(dsa[1, tile(r)], k2[1, reach])
        for h in range(2):
            dq = dq + head_only(dot(ska[h, tile(r)], pb[:, :T]), h)
        dqb[tile(r)] = dot(flip, (SCALE * dq).astype(bf16)).astype(bf16)

    part = bp[pl.ds(nz * y, nz)].astype(f32)
    for k in yk:
        arrive(yrecv.at[k - 1], ys + k - 1)
    for k in yk:
        part = part + yrecv[k - 1].astype(f32)
    zsend[...] = part.astype(bf16)

    zs = take(nz)
    for k in zk:
        push(zsend.at[zpeer(k)], zrecv.at[k - 1], zs + k - 1, at(zpeer(k), y))

    qs = take(1)
    push(dqb.at[rows(T * o)], rq, qs, mate)
    give_back(dkb, 0)

    part = zsend[z].astype(f32)
    for k in reversed(zk):
        arrive(zrecv.at[k - 1], zs + k - 1)
        part = part + zrecv[k - 1].astype(f32)
    low = part.astype(bf16)
    own[...] = low
    ag[nz * y + z] = low

    gs = take(nz)
    for k in zk:
        push(own, ag.at[nz * y + z], gs + k - 1, at(zpeer(k), y))

    both = low.astype(f32)
    rel_part = dot(both[:rb].astype(bf16), wv[0], 1, 1) + dot(both[rb:].astype(bf16), wv[1], 1, 1)
    for i in range(2 * nx):
        xpart[i] = rel_part[:, tile(i)]
    xs = take(2 * nx)
    for k in mk:
        push(xpart.at[mpeer(k)], xrecv.at[k - 1], xs + k - 1,
             2 * c + lax.rem(mpeer(k), 2), mpeer(k) // 2)
    total = xpart[m]
    for k in mk:
        arrive(xrecv.at[k - 1], xs + k - 1)
        total = total + xrecv[k - 1]
    relz[z] = total
    ls = take(nz)
    for k in zk:
        push(relz.at[z], relz.at[z], ls + k - 1, at(zpeer(k), y))

    for k in reversed(zk):
        arrive(ag.at[nz * y + zpeer(nz - k)], gs + k - 1)
    us = take(ny)
    mine = pl.ds(nz * y, nz)
    for k in yk:
        push(ag.at[mine], ag.at[mine], us + k - 1, at(z, ypeer(k)))

    for k in reversed(yk):
        arrive(ag.at[pl.ds(nz * ypeer(ny - k), nz)], us + k - 1)
    every = ag[...].astype(f32)
    for i in range(2):
        grad = every[:, i * rb : (i + 1) * rb].reshape(buckets, T).astype(bf16)
        wtmp[i] = dot(rel_v[:, lanes(c * dr2 // T)], grad, 0, 0)
    start = lax.rem(c * dr2, T)
    wsend[...] = wtmp[:, pl.ds(pl.multiple_of(start + dr * o, dr), dr)]
    ws = take(1)
    push(wsend, wrecv, ws, mate)
    ours = pl.ds(pl.multiple_of(start + dr * p, dr), dr)
    wko[:, lanes(p)] = wtmp[0, ours]
    wqo[:, lanes(p)] = wtmp[1, ours]

    for k in reversed(zk):
        arrive(relz.at[zpeer(nz - k)], ls + k - 1)
    relo[y] = relz[...].reshape(nz * rb, T).astype(bf16)
    ms = take(ny)
    es = take(ny)
    for k in yk:
        push(relo.at[y], relo.at[y], ms + k - 1, at(z, ypeer(k)))
    push(relo.at[y], relq.at[y], es, mate)

    dqo[:, lanes(p)] = dqb[rows(T * p)]
    arrive(rq, qs)
    dqo[:, lanes(o)] = rq[...]
    row = rows(2 * HALO * T + T * p)
    rkv[HALO, p, 0] = dkb[row]
    rkv[HALO, p, 1] = dvb[row]
    arrive(rkv.at[HALO, o, 0], rs + (HALO * 2 + o) * 2)
    arrive(rkv.at[HALO, o, 1], rs + (HALO * 2 + o) * 2 + 1)
    for d in hops:
        for pp in range(2):
            arrive(rkv.at[d + HALO, pp, 0], rs + ((d + HALO) * 2 + pp) * 2)
            arrive(rkv.at[d + HALO, pp, 1], rs + ((d + HALO) * 2 + pp) * 2 + 1)
    for pp in range(2):
        for i, out in ((0, dko), (1, dvo)):
            x = rkv[0, pp, i].astype(f32)
            for d in range(1, 2 * HALO + 1):
                x = x + rkv[d, pp, i].astype(f32)
            out[:, tile(pp)] = x.astype(bf16)

    for k in reversed(yk):
        arrive(relo.at[ypeer(ny - k)], ms + k - 1)
        push(relo.at[ypeer(ny - k)], relq.at[ypeer(ny - k)], es + k, mate)
    arrive(wrecv, ws)
    wko[:, lanes(o)] = wrecv[0]
    wqo[:, lanes(o)] = wrecv[1]
    arrive(relq.at[y], es)
    for k in reversed(yk):
        arrive(relq.at[ypeer(ny - k)], es + k)
    for copy in sent:
        copy.wait_send()


def copy_kernel(dq, dk, dv, rel, relq, wk, wq, dqo, dko, dvo, relo, wqo, wko):
    p = lax.rem(lax.axis_index("seq"), 2)
    dqo[...] = dq[...]
    dko[...] = dk[...]
    dvo[...] = dv[...]
    relo[:, lanes(p)] = rel[...].reshape(relo.shape[0], T).astype(f32)
    relo[:, lanes(1 - p)] = relq[...].reshape(relo.shape[0], T).astype(f32)
    wqo[...] = wq[...]
    wko[...] = wk[...]


def body(ny, queries, keys, values, out_grad, rel_emb, w_query, w_key, doc_lengths, bucket_table):
    nc = lax.axis_size("seq") // 2
    nx = lax.axis_size("head")
    nz = nc // ny
    buckets, width = rel_emb.shape
    span = bucket_table.shape[0]
    rb = buckets // nc
    dr = width // nc // 2
    keys_in = TILES * T
    shape = jax.ShapeDtypeStruct
    tab = bucket_table.reshape(1, -1)
    lens = doc_lengths.reshape(1, -1)
    results = pl.pallas_call(
        functools.partial(whole_kernel, nz, ny, nx),
        out_shape=(
            shape((T, 2 * T), bf16),
            shape((T, 2 * T), bf16),
            shape((T, 2 * T), bf16),
            shape((ny, nz * rb, T), bf16),
            shape((ny, nz * rb, T), bf16),
            shape((dr, 2 * T), f32),
            shape((dr, 2 * T), f32),
        ),
        in_specs=[ANY] * 7 + [VM] * 2,
        out_specs=(VM,) * 7,
        scratch_shapes=[
            pltpu.VMEM((buckets, width), bf16),
            pltpu.VMEM((2, width, T), bf16),
            pltpu.VMEM((2 * T, T), bf16),
            pltpu.VMEM((2 * T, T), bf16),
            pltpu.VMEM((keys_in, T), bf16),
            pltpu.VMEM((keys_in, T), bf16),
            pltpu.VMEM((span, 2 * T), bf16),
            pltpu.VMEM((buckets, span), bf16),
            pltpu.VMEM((2, 2 * T, T), bf16),
            pltpu.VMEM((2, 2 * T, T), bf16),
            pltpu.VMEM((2, keys_in, T), bf16),
            pltpu.VMEM((2, span + 4 * T, T), bf16),
            pltpu.VMEM((T, 2 * T), bf16),
            pltpu.VMEM((T, keys_in), bf16),
            pltpu.VMEM((2, keys_in, 2 * T), f32),
            pltpu.VMEM((2, keys_in, 2 * T), f32),
            pltpu.VMEM((2, keys_in, 2 * T), bf16),
            pltpu.VMEM((2, keys_in, 2 * T), bf16),
            pltpu.VMEM((2, keys_in, 3 * T), bf16),
            pltpu.VMEM((2, 2 * T, WIDE), bf16),
            pltpu.VMEM((2, 2 * T, span), bf16),
            pltpu.VMEM((keys_in, T), bf16),
            pltpu.VMEM((keys_in, T), bf16),
            pltpu.VMEM((2 * T, T), bf16),
            pltpu.VMEM((T, span), f32),
            pltpu.VMEM((T, span + 4 * T), f32),
            pltpu.VMEM((nc, 2 * rb, T), bf16),
            pltpu.VMEM((5, 2, 2, T, T), bf16),
            pltpu.VMEM((T, T), bf16),
            pltpu.VMEM((ny, nz, 2 * rb, T), bf16),
            pltpu.VMEM((nz, 2 * rb, T), bf16),
            pltpu.VMEM((nz, 2 * rb, T), bf16),
            pltpu.VMEM((2 * rb, T), bf16),
            pltpu.VMEM((nc, 2 * rb, T), bf16),
            pltpu.VMEM((2 * nx, rb, T), f32),
            pltpu.VMEM((2 * nx, rb, T), f32),
            pltpu.VMEM((nz, rb, T), f32),
            pltpu.VMEM((2, T, T), f32),
            pltpu.VMEM((2, dr, T), f32),
            pltpu.VMEM((2, dr, T), f32),
            pltpu.SemaphoreType.DMA((144,)),
            pltpu.SemaphoreType.DMA((144,)),
            pltpu.SemaphoreType.DMA((7,)),
        ],
        compiler_params=pltpu.CompilerParams(collective_id=0, has_side_effects=True),
        name="whole",
    )(queries, keys, values, out_grad, rel_emb, w_query, w_key, tab, lens)
    return tuple(
        pl.pallas_call(
            copy_kernel,
            out_shape=(
                shape((T, 2 * T), bf16),
                shape((T, 2 * T), bf16),
                shape((T, 2 * T), bf16),
                shape((buckets, 2 * T), f32),
                shape((dr, 2 * T), f32),
                shape((dr, 2 * T), f32),
            ),
            in_specs=[VM] * 7,
            out_specs=(VM,) * 6,
            name="results",
        )(*results)
    )


def solution(mesh, ny=NY):
    shard = P("seq", "head")
    return jax.shard_map(
        functools.partial(body, ny),
        mesh=mesh,
        in_specs=(shard,) * 4 + (P(), P(None, "head"), P(None, "head"), P(), P()),
        out_specs=(shard, shard, shard, P(None, "head"), shard, shard),
        check_vma=False,
    )
```

```python
import functools
import math

import jax
import jax.numpy as jnp
from jax import lax
from jax.experimental import pallas as pl
from jax.experimental.pallas import tpu as pltpu
from jax.sharding import PartitionSpec as P

HD = 64
T = 128
NY = 4
HALO = 2
TILES = 2 * (2 * HALO + 1)
WIDE = 9 * T
f32 = jnp.float32
bf16 = jnp.bfloat16
SCALE = 1.0 / math.sqrt(3.0 * HD)
ANY = pl.BlockSpec(memory_space=pl.ANY)
VM = pl.BlockSpec(memory_space=pltpu.VMEM)


def dot(a, b, ca=1, cb=0):
    return lax.dot_general(a, b, (((ca,), (cb,)), ((), ())), preferred_element_type=f32)


def remote(src, dst, send, recv, seq, head=None):
    where = {"seq": seq} if head is None else {"seq": seq, "head": head}
    return pltpu.make_async_remote_copy(
        src_ref=src, dst_ref=dst, send_sem=send, recv_sem=recv,
        device_id=where, device_id_type=pl.DeviceIdType.MESH,
    )


def greet(seq, head=None):
    where = {"seq": seq} if head is None else {"seq": seq, "head": head}
    pl.semaphore_signal(
        pltpu.get_barrier_semaphore(), inc=1, device_id=where,
        device_id_type=pl.DeviceIdType.MESH,
    )


def lanes(p):
    return pl.ds(pl.multiple_of(p * T, T), T)


def rows(start):
    return pl.ds(pl.multiple_of(start, T), T)


def tile(j):
    return slice(j * T, (j + 1) * T)


def skewed(x, first):
    return pltpu.roll(x, first, 1, stride=1, stride_axis=0)


def head_only(x, h):
    lane = lax.broadcasted_iota(jnp.int32, x.shape, 1)
    return jnp.where((lane < HD) if h == 0 else (lane >= HD), x, jnp.zeros_like(x))


def indicator(match):
    return match.astype(f32).astype(bf16)


def whole_kernel(
    nz, ny, nx,
    q_ref, k_ref, v_ref, g_ref, rel_ref, wq_ref, wk_ref, tab_ref, len_ref,
    dqo, dko, dvo, relo, relq, wko, wqo,
    rel_v, wv, qw, gw, kw, vw, pb, oht, q2, g2, k2, pqr, qrt, krt,
    sc, dp, prb, dsb, dsr, skb, dsa, ska, dkb, dvb, dqb, gt, ht,
    bp, rkv, rq, yrecv, zsend, zrecv, own, ag, xpart, xrecv, relz,
    wtmp, wsend, wrecv, send, recv, local, known,
):
    nc = nz * ny
    s = lax.axis_index("seq")
    hx = lax.axis_index("head")
    c, p = s // 2, lax.rem(s, 2)
    o = 1 - p
    mate = 2 * c + o
    z, y = c // ny, lax.rem(c, ny)
    m = 2 * hx + p
    buckets, width = rel_ref.shape
    span = tab_ref.shape[1]
    rb = buckets // nc
    dr2 = width // nc
    dr = dr2 // 2
    hops = [-1, 1, -2, 2]

    def chip(d):
        return lax.rem(c + d + nc, nc)

    def ypeer(k):
        return lax.rem(y + k, ny)

    def zpeer(k):
        return lax.rem(z + k, nz)

    def mpeer(k):
        return lax.rem(m + k, 2 * nx)

    def at(zz, yy):
        return 2 * (zz * ny + yy) + p

    yk = sorted(range(1, ny), key=lambda k: -min(k, ny - k))
    zk = sorted(range(1, nz), key=lambda k: -min(k, nz - k))
    mk = range(1, 2 * nx)

    for k in (1, nz - 1):
        greet(at(zpeer(k), y))
    for k in yk:
        greet(at(z, ypeer(k)))
    for d in hops:
        for pp in range(2):
            greet(2 * chip(d) + pp)
    for k in mk:
        greet(2 * c + lax.rem(mpeer(k), 2), mpeer(k) // 2)
    greet(mate)

    loads = []

    def load(src, dst):
        copy = pltpu.make_async_copy(src, dst, local.at[len(loads)])
        copy.start()
        loads.append(copy)

    load(rel_ref, rel_v)
    load(wk_ref.at[:, lanes(p)], wv.at[0])
    load(wq_ref.at[:, lanes(p)], wv.at[1])
    load(k_ref.at[:, lanes(p)], kw.at[rows(2 * HALO * T + T * p)])
    load(v_ref.at[:, lanes(p)], vw.at[rows(2 * HALO * T + T * p)])
    load(q_ref.at[:, lanes(p)], qw.at[rows(T * p)])
    load(g_ref.at[:, lanes(p)], gw.at[rows(T * p)])

    pl.semaphore_wait(
        pltpu.get_barrier_semaphore(), 2 + len(yk) + 8 + len(mk) + 1
    )

    sent = []
    slots = [0]

    def push(src, dst, slot, seq, head=None):
        copy = remote(src, dst, send.at[len(sent)], recv.at[slot], seq, head)
        copy.start()
        sent.append(copy)

    def take(count):
        base = slots[0]
        slots[0] += count
        return base

    def arrive(dst, slot):
        remote(dst, dst, send.at[0], recv.at[slot], s).wait_recv()

    step = [1 << i for i in range(nz.bit_length()) if (1 << i) < nz // 2]

    def tell(i):
        if i < len(step):
            for k in (step[i], nz - step[i]):
                pl.semaphore_signal(known.at[i], inc=1, device_id={"seq": at(zpeer(k), y)},
                                    device_id_type=pl.DeviceIdType.MESH)

    def hear(i):
        if i < len(step):
            pl.semaphore_wait(known.at[i], 2)

    near = take(4)
    hs = take(8)
    fs = take(4)
    row = rows(T * p)
    push(q_ref.at[:, lanes(o)], qw.at[row], near, mate)
    push(g_ref.at[:, lanes(o)], gw.at[row], near + 1, mate)
    row = rows(2 * HALO * T + T * p)
    push(k_ref.at[:, lanes(o)], kw.at[row], near + 2, mate)
    push(v_ref.at[:, lanes(o)], vw.at[row], near + 3, mate)
    for i, src, dst in ((0, k_ref, kw), (1, v_ref, vw)):
        for d in (-1, 1):
            for pp in range(2):
                push(src.at[:, pl.ds(pp * T, T)], dst.at[rows(2 * T * (HALO - d) + T * p)],
                     hs + (d + 1) * 2 + p * 2 + i, 2 * chip(d) + pp)
    tell(0)

    def pass_on(i, ref):
        for d in (-1, 1):
            for pp in range(2):
                arrive(ref.at[tile(2 * (HALO + d) + pp)], hs + (1 - d) * 2 + pp * 2 + i)
            near_rows = pl.ds(2 * T * (HALO + d), 2 * T)
            far_rows = pl.ds(2 * T * (HALO + 2 * d), 2 * T)
            push(ref.at[near_rows], ref.at[far_rows], fs + d + 1 + i, 2 * chip(-d) + p)

    def passed(i, ref):
        for d in (-1, 1):
            arrive(ref.at[pl.ds(2 * T * (HALO + 2 * d), 2 * T)], fs + d + 1 + i)

    ri = lax.broadcasted_iota(jnp.int32, (T, T), 0)
    ci = lax.broadcasted_iota(jnp.int32, (T, T), 1)
    flip = indicator(ri + ci == T - 1)
    table = jnp.broadcast_to(tab_ref[...], (8, span))
    high = table // 256
    low = (table - 256 * high).astype(f32).astype(bf16)
    high = high.astype(f32).astype(bf16)
    blocks = span // T
    rev = jnp.concatenate(
        [
            256.0 * dot(high[:, tile(blocks - 1 - b)], flip) + dot(low[:, tile(blocks - 1 - b)], flip)
            for b in range(blocks)
        ],
        1,
    )[:1]
    number = lax.broadcasted_iota(jnp.int32, (T, span), 0).astype(f32)
    for b in range(buckets // T):
        oht[tile(b)] = indicator(number + float(b * T) == rev)
    column = jnp.transpose(jnp.broadcast_to(rev, (T, span)))
    lane = lax.broadcasted_iota(jnp.int32, column.shape, 1).astype(f32)
    onehot = jnp.concatenate(
        [indicator(column == lane + float(T * b)) for b in range(buckets // T)], 1
    )

    ndocs = len_ref.shape[1]
    de = lax.broadcasted_iota(jnp.int32, (ndocs, ndocs), 1)
    dd = lax.broadcasted_iota(jnp.int32, (ndocs, ndocs), 0)
    lens = jnp.broadcast_to(len_ref[...], (ndocs, ndocs))
    ends = jnp.sum(jnp.where(de <= dd, lens, 0), axis=1, keepdims=True)
    shift = (c - HALO) * 2 * T
    pos = lax.broadcasted_iota(jnp.int32, (ndocs, 2 * T), 1) + c * 2 * T
    first = jnp.max(jnp.where(ends <= pos, ends, 0), axis=0, keepdims=True) - shift
    last = jnp.min(jnp.where(ends > pos, ends, 1 << 30), axis=0, keepdims=True) - shift

    for copy in loads[:3]:
        copy.wait()
    pos_key = dot(rel_v[...], wv[0]).astype(bf16)
    pass_on(0, kw)
    pos_query = dot(rel_v[...], wv[1]).astype(bf16)
    pb[...] = dot(onehot, jnp.concatenate([pos_key, pos_query], 1)).astype(bf16)
    for h in range(2):
        pqr[h, : 2 * T] = jnp.zeros((2 * T, T), bf16)
        pqr[h, 2 * T : 2 * T + span] = head_only(pb[:, T:], h)
        pqr[h, 2 * T + span :] = jnp.zeros((2 * T, T), bf16)
    ht[...] = jnp.zeros_like(ht)

    hear(0)
    tell(1)
    for copy in loads[3:]:
        copy.wait()
    pass_on(1, vw)
    arrive(qw.at[rows(T * o)], near)
    arrive(gw.at[rows(T * o)], near + 1)

    for h in range(2):
        q2[h] = head_only(qw[...], h)
        g2[h] = head_only(gw[...], h)
    for r in range(2):
        qrt[:, tile(r)] = jnp.transpose(dot(flip, qw[tile(r)])).astype(bf16)
    for h in range(2):
        sc[h, WIDE:, :T] = jnp.zeros((T, T), f32)
        sc[h, :T, T:] = jnp.zeros((T, T), f32)
        for r in range(2):
            a = dot(q2[h, tile(r)], pb[:, :T], 1, 1)
            a = skewed(jnp.concatenate([a, jnp.zeros((T, WIDE - span), f32)], 1), 1)
            for j in range(9):
                sc[h, tile(r + j), tile(r)] = jnp.transpose(a[:, tile(j)])

    arrive(kw.at[rows(2 * HALO * T + T * o)], near + 2)
    arrive(vw.at[rows(2 * HALO * T + T * o)], near + 3)

    top = [jnp.full((8, 2 * T), -1e30, f32) for _ in range(2)]

    def band(j):
        return slice((9 - j) * T, (9 - j) * T + 3 * T)

    def fold(x, op):
        return op(x.reshape(T // 8, 8, 2 * T), axis=0)

    def score(j):
        kt = kw[tile(j)]
        krt[:, tile(j)] = jnp.transpose(dot(flip, kt)).astype(bf16)
        key = lax.broadcasted_iota(jnp.int32, (T, 2 * T), 0) + j * T
        keep = (key >= first) & (key < last)
        for h in range(2):
            k2[h, tile(j)] = head_only(kt, h)
            b = skewed(dot(kt, pqr[h, band(j)], 1, 1), 2 * T + 1)[:, : 2 * T]
            x = SCALE * (dot(kt, q2[h], 1, 1) + sc[h, tile(j)] + b)
            x = jnp.where(keep, x, -1e30)
            sc[h, tile(j)] = x
            top[h] = jnp.maximum(top[h], fold(x, jnp.max))

    def through_values(j):
        for h in range(2):
            dp[h, tile(j)] = dot(vw[tile(j)], g2[h], 1, 1)

    inner, outer = (4, 5, 2, 3, 6, 7), (0, 1, 8, 9)
    for j in inner:
        score(j)
    hear(1)
    tell(2)
    for j in inner:
        through_values(j)
    passed(0, kw)
    for j in outer:
        score(j)
    passed(1, vw)
    for j in outer:
        through_values(j)

    inv, row_dot = [], []
    for h in range(2):
        high_score = jnp.max(top[h], axis=0, keepdims=True)
        total = jnp.zeros((8, 2 * T), f32)
        along = jnp.zeros((8, 2 * T), f32)
        for j in range(TILES):
            x = jnp.exp(sc[h, tile(j)] - high_score)
            sc[h, tile(j)] = x
            total = total + fold(x, jnp.sum)
            along = along + fold(x * dp[h, tile(j)], jnp.sum)
        inv.append(1.0 / jnp.sum(total, axis=0, keepdims=True))
        row_dot.append(jnp.sum(along, axis=0, keepdims=True) * inv[h])

    for h in range(2):
        half = slice(h * HD, (h + 1) * HD)
        for j in range(TILES):
            prob = sc[h, tile(j)] * inv[h]
            ds = (prob * (dp[h, tile(j)] - row_dot[h])).astype(bf16)
            prb[h, tile(j)] = prob.astype(bf16)
            dsb[h, tile(j)] = ds
            back = dot(flip, ds)
            dsr[h, tile(j)] = back.astype(bf16)
            skew = skewed(jnp.concatenate([back, jnp.zeros((T, T), f32)], 1), 0).astype(bf16)
            skb[h, tile(j)] = skew
            ht[half, band(j)] += dot(krt[half, tile(j)], skew)
        for r in range(2):
            back = dot(flip, dsb[h, r * T : r * T + WIDE, tile(r)], 1, 1)
            dsa[h, tile(r)] = back.astype(bf16)
            skew = skewed(back, span)[:, :span].astype(bf16)
            ska[h, tile(r)] = skew
            part = dot(qrt[half, tile(r)], skew)
            if r == 0:
                gt[half] = part
            else:
                gt[half] += part

    bk = SCALE * dot(oht[...], gt[...].astype(bf16), 1, 1)
    bq = SCALE * dot(oht[...], ht[:, 2 * T : 2 * T + span].astype(bf16), 1, 1)
    bp[...] = jnp.concatenate([bk.reshape(nc, rb, T), bq.reshape(nc, rb, T)], 1).astype(bf16)

    ys = take(ny)
    for k in yk:
        push(bp.at[pl.ds(nz * ypeer(k), nz)], yrecv.at[k - 1], ys + k - 1, at(z, ypeer(k)))

    far_first = [j for d in (-2, 2, -1, 1, 0) for j in (2 * (d + HALO), 2 * (d + HALO) + 1)]
    for j in far_first:
        dv = dot(prb[0, tile(j)], g2[0]) + dot(prb[1, tile(j)], g2[1])
        dvb[tile(j)] = dv.astype(bf16)
        dk = dot(dsr[0, tile(j)], q2[0]) + dot(dsr[1, tile(j)], q2[1])
        dk = dk + dot(skb[0, tile(j)], pqr[0, band(j)]) + dot(skb[1, tile(j)], pqr[1, band(j)])
        dkb[tile(j)] = dot(flip, (SCALE * dk).astype(bf16)).astype(bf16)
    for r in range(2):
        reach = slice(r * T, r * T + WIDE)
        dq = dot(dsa[0, tile(r)], k2[0, reach]) + dot(dsa[1, tile(r)], k2[1, reach])
        for h in range(2):
            dq = dq + head_only(dot(ska[h, tile(r)], pb[:, :T]), h)
        dqb[tile(r)] = dot(flip, (SCALE * dq).astype(bf16)).astype(bf16)

    part = bp[pl.ds(nz * y, nz)].astype(f32)
    for k in yk:
        arrive(yrecv.at[k - 1], ys + k - 1)
    for k in yk:
        part = part + yrecv[k - 1].astype(f32)
    zsend[...] = part.astype(bf16)

    hear(2)
    zs = take(nz)
    for k in zk:
        push(zsend.at[zpeer(k)], zrecv.at[k - 1], zs + k - 1, at(zpeer(k), y))

    rs = take(20)

    def give_back(grad, i):
        for d in reversed(hops):
            for pp in range(2):
                push(grad.at[tile(2 * (d + HALO) + pp)], rkv.at[d + HALO, p, i],
                     rs + ((d + HALO) * 2 + p) * 2 + i, 2 * chip(d) + pp)
        push(grad.at[rows(2 * HALO * T + T * o)], rkv.at[HALO, p, i],
             rs + (HALO * 2 + p) * 2 + i, mate)

    qs = take(1)
    push(dqb.at[rows(T * o)], rq, qs, mate)
    give_back(dkb, 0)
    give_back(dvb, 1)

    part = zsend[z].astype(f32)
    for k in reversed(zk):
        arrive(zrecv.at[k - 1], zs + k - 1)
        part = part + zrecv[k - 1].astype(f32)
    low = part.astype(bf16)
    own[...] = low
    ag[nz * y + z] = low

    gs = take(nz)
    for k in zk:
        push(own, ag.at[nz * y + z], gs + k - 1, at(zpeer(k), y))

    both = low.astype(f32)
    rel_part = dot(both[:rb].astype(bf16), wv[0], 1, 1) + dot(both[rb:].astype(bf16), wv[1], 1, 1)
    for i in range(2 * nx):
        xpart[i] = rel_part[:, tile(i)]
    xs = take(2 * nx)
    for k in mk:
        push(xpart.at[mpeer(k)], xrecv.at[k - 1], xs + k - 1,
             2 * c + lax.rem(mpeer(k), 2), mpeer(k) // 2)
    total = xpart[m]
    for k in mk:
        arrive(xrecv.at[k - 1], xs + k - 1)
        total = total + xrecv[k - 1]
    relz[z] = total
    ls = take(nz)
    for k in zk:
        push(relz.at[z], relz.at[z], ls + k - 1, at(zpeer(k), y))

    for k in reversed(zk):
        arrive(ag.at[nz * y + zpeer(nz - k)], gs + k - 1)
    us = take(ny)
    mine = pl.ds(nz * y, nz)
    for k in yk:
        push(ag.at[mine], ag.at[mine], us + k - 1, at(z, ypeer(k)))

    for k in reversed(yk):
        arrive(ag.at[pl.ds(nz * ypeer(ny - k), nz)], us + k - 1)
    every = ag[...].astype(f32)
    for i in range(2):
        grad = every[:, i * rb : (i + 1) * rb].reshape(buckets, T).astype(bf16)
        wtmp[i] = dot(rel_v[:, lanes(c * dr2 // T)], grad, 0, 0)
    start = lax.rem(c * dr2, T)
    wsend[...] = wtmp[:, pl.ds(pl.multiple_of(start + dr * o, dr), dr)]
    ws = take(1)
    push(wsend, wrecv, ws, mate)
    ours = pl.ds(pl.multiple_of(start + dr * p, dr), dr)
    wko[:, lanes(p)] = wtmp[0, ours]
    wqo[:, lanes(p)] = wtmp[1, ours]

    for k in reversed(zk):
        arrive(relz.at[zpeer(nz - k)], ls + k - 1)
    relo[y] = relz[...].reshape(nz * rb, T).astype(bf16)
    ms = take(ny)
    es = take(ny)
    for k in yk:
        push(relo.at[y], relo.at[y], ms + k - 1, at(z, ypeer(k)))
    push(relo.at[y], relq.at[y], es, mate)

    dqo[:, lanes(p)] = dqb[rows(T * p)]
    arrive(rq, qs)
    dqo[:, lanes(o)] = rq[...]
    row = rows(2 * HALO * T + T * p)
    rkv[HALO, p, 0] = dkb[row]
    rkv[HALO, p, 1] = dvb[row]
    arrive(rkv.at[HALO, o, 0], rs + (HALO * 2 + o) * 2)
    arrive(rkv.at[HALO, o, 1], rs + (HALO * 2 + o) * 2 + 1)
    for d in hops:
        for pp in range(2):
            arrive(rkv.at[d + HALO, pp, 0], rs + ((d + HALO) * 2 + pp) * 2)
            arrive(rkv.at[d + HALO, pp, 1], rs + ((d + HALO) * 2 + pp) * 2 + 1)
    for pp in range(2):
        for i, out in ((0, dko), (1, dvo)):
            x = rkv[0, pp, i].astype(f32)
            for d in range(1, 2 * HALO + 1):
                x = x + rkv[d, pp, i].astype(f32)
            out[:, tile(pp)] = x.astype(bf16)

    for k in reversed(yk):
        arrive(relo.at[ypeer(ny - k)], ms + k - 1)
        push(relo.at[ypeer(ny - k)], relq.at[ypeer(ny - k)], es + k, mate)
    arrive(wrecv, ws)
    wko[:, lanes(o)] = wrecv[0]
    wqo[:, lanes(o)] = wrecv[1]
    arrive(relq.at[y], es)
    for k in reversed(yk):
        arrive(relq.at[ypeer(ny - k)], es + k)
    for copy in sent:
        copy.wait_send()


def copy_kernel(dq, dk, dv, rel, relq, wk, wq, dqo, dko, dvo, relo, wqo, wko):
    p = lax.rem(lax.axis_index("seq"), 2)
    dqo[...] = dq[...]
    dko[...] = dk[...]
    dvo[...] = dv[...]
    relo[:, lanes(p)] = rel[...].reshape(relo.shape[0], T).astype(f32)
    relo[:, lanes(1 - p)] = relq[...].reshape(relo.shape[0], T).astype(f32)
    wqo[...] = wq[...]
    wko[...] = wk[...]


def body(ny, queries, keys, values, out_grad, rel_emb, w_query, w_key, doc_lengths, bucket_table):
    nc = lax.axis_size("seq") // 2
    nx = lax.axis_size("head")
    nz = nc // ny
    buckets, width = rel_emb.shape
    span = bucket_table.shape[0]
    rb = buckets // nc
    dr = width // nc // 2
    keys_in = TILES * T
    shape = jax.ShapeDtypeStruct
    tab = bucket_table.reshape(1, -1)
    lens = doc_lengths.reshape(1, -1)
    results = pl.pallas_call(
        functools.partial(whole_kernel, nz, ny, nx),
        out_shape=(
            shape((T, 2 * T), bf16),
            shape((T, 2 * T), bf16),
            shape((T, 2 * T), bf16),
            shape((ny, nz * rb, T), bf16),
            shape((ny, nz * rb, T), bf16),
            shape((dr, 2 * T), f32),
            shape((dr, 2 * T), f32),
        ),
        in_specs=[ANY] * 7 + [VM] * 2,
        out_specs=(VM,) * 7,
        scratch_shapes=[
            pltpu.VMEM((buckets, width), bf16),
            pltpu.VMEM((2, width, T), bf16),
            pltpu.VMEM((2 * T, T), bf16),
            pltpu.VMEM((2 * T, T), bf16),
            pltpu.VMEM((keys_in, T), bf16),
            pltpu.VMEM((keys_in, T), bf16),
            pltpu.VMEM((span, 2 * T), bf16),
            pltpu.VMEM((buckets, span), bf16),
            pltpu.VMEM((2, 2 * T, T), bf16),
            pltpu.VMEM((2, 2 * T, T), bf16),
            pltpu.VMEM((2, keys_in, T), bf16),
            pltpu.VMEM((2, span + 4 * T, T), bf16),
            pltpu.VMEM((T, 2 * T), bf16),
            pltpu.VMEM((T, keys_in), bf16),
            pltpu.VMEM((2, keys_in, 2 * T), f32),
            pltpu.VMEM((2, keys_in, 2 * T), f32),
            pltpu.VMEM((2, keys_in, 2 * T), bf16),
            pltpu.VMEM((2, keys_in, 2 * T), bf16),
            pltpu.VMEM((2, keys_in, 2 * T), bf16),
            pltpu.VMEM((2, keys_in, 3 * T), bf16),
            pltpu.VMEM((2, 2 * T, WIDE), bf16),
            pltpu.VMEM((2, 2 * T, span), bf16),
            pltpu.VMEM((keys_in, T), bf16),
            pltpu.VMEM((keys_in, T), bf16),
            pltpu.VMEM((2 * T, T), bf16),
            pltpu.VMEM((T, span), f32),
            pltpu.VMEM((T, span + 4 * T), f32),
            pltpu.VMEM((nc, 2 * rb, T), bf16),
            pltpu.VMEM((5, 2, 2, T, T), bf16),
            pltpu.VMEM((T, T), bf16),
            pltpu.VMEM((ny, nz, 2 * rb, T), bf16),
            pltpu.VMEM((nz, 2 * rb, T), bf16),
            pltpu.VMEM((nz, 2 * rb, T), bf16),
            pltpu.VMEM((2 * rb, T), bf16),
            pltpu.VMEM((nc, 2 * rb, T), bf16),
            pltpu.VMEM((2 * nx, rb, T), f32),
            pltpu.VMEM((2 * nx, rb, T), f32),
            pltpu.VMEM((nz, rb, T), f32),
            pltpu.VMEM((2, T, T), f32),
            pltpu.VMEM((2, dr, T), f32),
            pltpu.VMEM((2, dr, T), f32),
            pltpu.SemaphoreType.DMA((144,)),
            pltpu.SemaphoreType.DMA((144,)),
            pltpu.SemaphoreType.DMA((7,)),
            pltpu.SemaphoreType.REGULAR((3,)),
        ],
        compiler_params=pltpu.CompilerParams(collective_id=0, has_side_effects=True),
        name="whole",
    )(queries, keys, values, out_grad, rel_emb, w_query, w_key, tab, lens)
    return tuple(
        pl.pallas_call(
            copy_kernel,
            out_shape=(
                shape((T, 2 * T), bf16),
                shape((T, 2 * T), bf16),
                shape((T, 2 * T), bf16),
                shape((buckets, 2 * T), f32),
                shape((dr, 2 * T), f32),
                shape((dr, 2 * T), f32),
            ),
            in_specs=[VM] * 7,
            out_specs=(VM,) * 6,
            name="results",
        )(*results)
    )


def solution(mesh, ny=NY):
    shard = P("seq", "head")
    return jax.shard_map(
        functools.partial(body, ny),
        mesh=mesh,
        in_specs=(shard,) * 4 + (P(), P(None, "head"), P(None, "head"), P(), P()),
        out_specs=(shard, shard, shard, P(None, "head"), shard, shard),
        check_vma=False,
    )
```

```python
import functools
import math

import jax
import jax.numpy as jnp
from jax import lax
from jax.experimental import pallas as pl
from jax.experimental.pallas import tpu as pltpu
from jax.sharding import PartitionSpec as P

HD = 64
T = 128
NY = 4
HALO = 2
TILES = 2 * (2 * HALO + 1)
WIDE = 9 * T
f32 = jnp.float32
bf16 = jnp.bfloat16
SCALE = 1.0 / math.sqrt(3.0 * HD)
ANY = pl.BlockSpec(memory_space=pl.ANY)
VM = pl.BlockSpec(memory_space=pltpu.VMEM)


def dot(a, b, ca=1, cb=0):
    return lax.dot_general(a, b, (((ca,), (cb,)), ((), ())), preferred_element_type=f32)


def remote(src, dst, send, recv, seq, head=None):
    where = {"seq": seq} if head is None else {"seq": seq, "head": head}
    return pltpu.make_async_remote_copy(
        src_ref=src, dst_ref=dst, send_sem=send, recv_sem=recv,
        device_id=where, device_id_type=pl.DeviceIdType.MESH,
    )


def greet(seq, head=None):
    where = {"seq": seq} if head is None else {"seq": seq, "head": head}
    pl.semaphore_signal(
        pltpu.get_barrier_semaphore(), inc=1, device_id=where,
        device_id_type=pl.DeviceIdType.MESH,
    )


def lanes(p):
    return pl.ds(pl.multiple_of(p * T, T), T)


def rows(start):
    return pl.ds(pl.multiple_of(start, T), T)


def tile(j):
    return slice(j * T, (j + 1) * T)


def skewed(x, first):
    return pltpu.roll(x, first, 1, stride=1, stride_axis=0)


def head_only(x, h):
    lane = lax.broadcasted_iota(jnp.int32, x.shape, 1)
    return jnp.where((lane < HD) if h == 0 else (lane >= HD), x, jnp.zeros_like(x))


def indicator(match):
    return match.astype(f32).astype(bf16)


def whole_kernel(
    nz, ny, nx,
    q_ref, k_ref, v_ref, g_ref, rel_ref, wq_ref, wk_ref, tab_ref, len_ref,
    dqo, dko, dvo, relo, relq, wko, wqo,
    rel_v, wv, qw, gw, kw, vw, pb, oht, q2, g2, k2, pqr, qrt, krt,
    sc, dp, prb, dsb, dsr, skb, dsa, ska, dkb, dvb, dqb, gt, ht,
    bp, rkv, rq, yrecv, zsend, zrecv, own, ag, xpart, xrecv, relz,
    wtmp, wy, wsum, wrecv, send, recv, local, known,
):
    nc = nz * ny
    s = lax.axis_index("seq")
    hx = lax.axis_index("head")
    c, p = s // 2, lax.rem(s, 2)
    o = 1 - p
    mate = 2 * c + o
    z, y = c // ny, lax.rem(c, ny)
    m = 2 * hx + p
    buckets, width = rel_ref.shape
    span = tab_ref.shape[1]
    rb = buckets // nc
    dr2 = width // nc
    dr = dr2 // 2
    hops = [-1, 1, -2, 2]

    def chip(d):
        return lax.rem(c + d + nc, nc)

    def ypeer(k):
        return lax.rem(y + k, ny)

    def zpeer(k):
        return lax.rem(z + k, nz)

    def mpeer(k):
        return lax.rem(m + k, 2 * nx)

    def at(zz, yy):
        return 2 * (zz * ny + yy) + p

    def plane(yy):
        return pl.ds(pl.multiple_of(nz * rb * yy, nz * rb), nz * rb)

    yk = sorted(range(1, ny), key=lambda k: -min(k, ny - k))
    zk = sorted(range(1, nz), key=lambda k: -min(k, nz - k))
    mk = range(1, 2 * nx)

    for k in (1, nz - 1):
        greet(at(zpeer(k), y))
    for k in yk:
        greet(at(z, ypeer(k)))
    for d in (-1, 1):
        for pp in range(2):
            greet(2 * chip(d) + pp)
    for k in mk:
        greet(2 * c + lax.rem(mpeer(k), 2), mpeer(k) // 2)
    greet(mate)

    loads = []

    def load(src, dst):
        copy = pltpu.make_async_copy(src, dst, local.at[len(loads)])
        copy.start()
        loads.append(copy)

    load(rel_ref, rel_v)
    load(wk_ref.at[:, lanes(p)], wv.at[0])
    load(wq_ref.at[:, lanes(p)], wv.at[1])
    load(k_ref.at[:, lanes(p)], kw.at[rows(2 * HALO * T + T * p)])
    load(v_ref.at[:, lanes(p)], vw.at[rows(2 * HALO * T + T * p)])
    load(q_ref.at[:, lanes(p)], qw.at[rows(T * p)])
    load(g_ref.at[:, lanes(p)], gw.at[rows(T * p)])

    pl.semaphore_wait(
        pltpu.get_barrier_semaphore(), 2 + len(yk) + 4 + len(mk) + 1
    )

    sent = []
    slots = [0]

    def push(src, dst, slot, seq, head=None):
        copy = remote(src, dst, send.at[len(sent)], recv.at[slot], seq, head)
        copy.start()
        sent.append(copy)

    def take(count):
        base = slots[0]
        slots[0] += count
        return base

    def arrive(dst, slot):
        remote(dst, dst, send.at[0], recv.at[slot], s).wait_recv()

    step = [1 << i for i in range(nz.bit_length()) if (1 << i) < nz // 2]

    def tell(i):
        if i < len(step):
            for k in (step[i], nz - step[i]):
                pl.semaphore_signal(known.at[i], inc=1, device_id={"seq": at(zpeer(k), y)},
                                    device_id_type=pl.DeviceIdType.MESH)

    def hear(i):
        if i < len(step):
            pl.semaphore_wait(known.at[i], 2)

    near = take(4)
    hs = take(8)
    fs = take(4)
    row = rows(T * p)
    push(q_ref.at[:, lanes(o)], qw.at[row], near, mate)
    push(g_ref.at[:, lanes(o)], gw.at[row], near + 1, mate)
    row = rows(2 * HALO * T + T * p)
    push(k_ref.at[:, lanes(o)], kw.at[row], near + 2, mate)
    push(v_ref.at[:, lanes(o)], vw.at[row], near + 3, mate)
    for i, src, dst in ((0, k_ref, kw), (1, v_ref, vw)):
        for d in (-1, 1):
            for pp in range(2):
                push(src.at[:, pl.ds(pp * T, T)], dst.at[rows(2 * T * (HALO - d) + T * p)],
                     hs + (d + 1) * 2 + p * 2 + i, 2 * chip(d) + pp)
    tell(0)

    def pass_on(i, ref):
        for d in (-1, 1):
            for pp in range(2):
                arrive(ref.at[tile(2 * (HALO + d) + pp)], hs + (1 - d) * 2 + pp * 2 + i)
            near_rows = pl.ds(2 * T * (HALO + d), 2 * T)
            far_rows = pl.ds(2 * T * (HALO + 2 * d), 2 * T)
            push(ref.at[near_rows], ref.at[far_rows], fs + d + 1 + i, 2 * chip(-d) + p)

    def passed(i, ref):
        for d in (-1, 1):
            arrive(ref.at[pl.ds(2 * T * (HALO + 2 * d), 2 * T)], fs + d + 1 + i)

    ri = lax.broadcasted_iota(jnp.int32, (T, T), 0)
    ci = lax.broadcasted_iota(jnp.int32, (T, T), 1)
    flip = indicator(ri + ci == T - 1)
    table = jnp.broadcast_to(tab_ref[...], (8, span))
    high = table // 256
    low = (table - 256 * high).astype(f32).astype(bf16)
    high = high.astype(f32).astype(bf16)
    blocks = span // T
    rev = jnp.concatenate(
        [
            256.0 * dot(high[:, tile(blocks - 1 - b)], flip) + dot(low[:, tile(blocks - 1 - b)], flip)
            for b in range(blocks)
        ],
        1,
    )[:1]
    number = lax.broadcasted_iota(jnp.int32, (T, span), 0).astype(f32)
    for b in range(buckets // T):
        oht[tile(b)] = indicator(number + float(b * T) == rev)
    column = jnp.transpose(jnp.broadcast_to(rev, (T, span)))
    lane = lax.broadcasted_iota(jnp.int32, column.shape, 1).astype(f32)
    onehot = jnp.concatenate(
        [indicator(column == lane + float(T * b)) for b in range(buckets // T)], 1
    )

    ndocs = len_ref.shape[1]
    de = lax.broadcasted_iota(jnp.int32, (ndocs, ndocs), 1)
    dd = lax.broadcasted_iota(jnp.int32, (ndocs, ndocs), 0)
    lens = jnp.broadcast_to(len_ref[...], (ndocs, ndocs))
    ends = jnp.sum(jnp.where(de <= dd, lens, 0), axis=1, keepdims=True)
    shift = (c - HALO) * 2 * T
    pos = lax.broadcasted_iota(jnp.int32, (ndocs, 2 * T), 1) + c * 2 * T
    first = jnp.max(jnp.where(ends <= pos, ends, 0), axis=0, keepdims=True) - shift
    last = jnp.min(jnp.where(ends > pos, ends, 1 << 30), axis=0, keepdims=True) - shift

    for copy in loads[:3]:
        copy.wait()
    pos_key = dot(rel_v[...], wv[0]).astype(bf16)
    pass_on(0, kw)
    pos_query = dot(rel_v[...], wv[1]).astype(bf16)
    pb[...] = dot(onehot, jnp.concatenate([pos_key, pos_query], 1)).astype(bf16)
    for h in range(2):
        pqr[h, : 2 * T] = jnp.zeros((2 * T, T), bf16)
        pqr[h, 2 * T : 2 * T + span] = head_only(pb[:, T:], h)
        pqr[h, 2 * T + span :] = jnp.zeros((2 * T, T), bf16)
    ht[...] = jnp.zeros_like(ht)

    hear(0)
    tell(1)
    for copy in loads[3:]:
        copy.wait()
    pass_on(1, vw)
    arrive(qw.at[rows(T * o)], near)
    arrive(gw.at[rows(T * o)], near + 1)

    for h in range(2):
        q2[h] = head_only(qw[...], h)
        g2[h] = head_only(gw[...], h)
    for r in range(2):
        qrt[:, tile(r)] = jnp.transpose(dot(flip, qw[tile(r)])).astype(bf16)
    for h in range(2):
        sc[h, WIDE:, :T] = jnp.zeros((T, T), f32)
        sc[h, :T, T:] = jnp.zeros((T, T), f32)
        for r in range(2):
            a = dot(q2[h, tile(r)], pb[:, :T], 1, 1)
            a = skewed(jnp.concatenate([a, jnp.zeros((T, WIDE - span), f32)], 1), 1)
            for j in range(9):
                sc[h, tile(r + j), tile(r)] = jnp.transpose(a[:, tile(j)])

    arrive(kw.at[rows(2 * HALO * T + T * o)], near + 2)
    arrive(vw.at[rows(2 * HALO * T + T * o)], near + 3)

    top = [jnp.full((8, 2 * T), -1e30, f32) for _ in range(2)]

    def band(j):
        return slice((9 - j) * T, (9 - j) * T + 3 * T)

    def fold(x, op):
        return op(x.reshape(T // 8, 8, 2 * T), axis=0)

    def score(j):
        kt = kw[tile(j)]
        krt[:, tile(j)] = jnp.transpose(dot(flip, kt)).astype(bf16)
        key = lax.broadcasted_iota(jnp.int32, (T, 2 * T), 0) + j * T
        keep = (key >= first) & (key < last)
        for h in range(2):
            k2[h, tile(j)] = head_only(kt, h)
            b = skewed(dot(kt, pqr[h, band(j)], 1, 1), 2 * T + 1)[:, : 2 * T]
            x = SCALE * (dot(kt, q2[h], 1, 1) + sc[h, tile(j)] + b)
            x = jnp.where(keep, x, -1e30)
            sc[h, tile(j)] = x
            top[h] = jnp.maximum(top[h], fold(x, jnp.max))

    def through_values(j):
        for h in range(2):
            dp[h, tile(j)] = dot(vw[tile(j)], g2[h], 1, 1)

    inner, outer = (4, 5, 2, 3, 6, 7), (0, 1, 8, 9)
    for j in inner:
        score(j)
    hear(1)
    tell(2)
    for j in inner:
        through_values(j)
    passed(0, kw)
    for j in outer:
        score(j)
    passed(1, vw)
    for j in outer:
        through_values(j)

    inv, row_dot = [], []
    for h in range(2):
        high_score = jnp.max(top[h], axis=0, keepdims=True)
        total = jnp.zeros((8, 2 * T), f32)
        along = jnp.zeros((8, 2 * T), f32)
        for j in range(TILES):
            x = jnp.exp(sc[h, tile(j)] - high_score)
            sc[h, tile(j)] = x
            total = total + fold(x, jnp.sum)
            along = along + fold(x * dp[h, tile(j)], jnp.sum)
        inv.append(1.0 / jnp.sum(total, axis=0, keepdims=True))
        row_dot.append(jnp.sum(along, axis=0, keepdims=True) * inv[h])

    for h in range(2):
        half = slice(h * HD, (h + 1) * HD)
        for j in range(TILES):
            prob = sc[h, tile(j)] * inv[h]
            ds = (prob * (dp[h, tile(j)] - row_dot[h])).astype(bf16)
            prb[h, tile(j)] = prob.astype(bf16)
            dsb[h, tile(j)] = ds
            back = dot(flip, ds)
            dsr[h, tile(j)] = back.astype(bf16)
            skew = skewed(jnp.concatenate([back, jnp.zeros((T, T), f32)], 1), 0).astype(bf16)
            skb[h, tile(j)] = skew
            ht[half, band(j)] += dot(krt[half, tile(j)], skew)

    ys = take(2 * ny)

    def scatter(i, offsets):
        bp[i] = (SCALE * dot(oht[...], offsets.astype(bf16), 1, 1)).astype(bf16)
        for k in yk:
            push(bp.at[i, plane(ypeer(k))], yrecv.at[i, k - 1],
                 ys + i * ny + k - 1, at(z, ypeer(k)))

    scatter(1, ht[:, 2 * T : 2 * T + span])
    for h in range(2):
        half = slice(h * HD, (h + 1) * HD)
        for r in range(2):
            back = dot(flip, dsb[h, r * T : r * T + WIDE, tile(r)], 1, 1)
            dsa[h, tile(r)] = back.astype(bf16)
            skew = skewed(back, span)[:, :span].astype(bf16)
            ska[h, tile(r)] = skew
            part = dot(qrt[half, tile(r)], skew)
            if r == 0:
                gt[half] = part
            else:
                gt[half] += part
    scatter(0, gt[...])

    far_first = [j for d in (-2, 2, -1, 1, 0) for j in (2 * (d + HALO), 2 * (d + HALO) + 1)]
    for j in far_first:
        dv = dot(prb[0, tile(j)], g2[0]) + dot(prb[1, tile(j)], g2[1])
        dvb[tile(j)] = dv.astype(bf16)
    for r in range(2):
        reach = slice(r * T, r * T + WIDE)
        dq = dot(dsa[0, tile(r)], k2[0, reach]) + dot(dsa[1, tile(r)], k2[1, reach])
        for h in range(2):
            dq = dq + head_only(dot(ska[h, tile(r)], pb[:, :T]), h)
        dqb[tile(r)] = dot(flip, (SCALE * dq).astype(bf16)).astype(bf16)

    parts = []
    for i in range(2):
        part = bp[i, plane(y)].astype(f32)
        for k in yk:
            arrive(yrecv.at[i, k - 1], ys + i * ny + k - 1)
        for k in yk:
            part = part + yrecv[i, k - 1].astype(f32)
        parts.append(part.reshape(nz, rb, T))
    zsend[...] = jnp.concatenate(parts, 1).astype(bf16)

    hear(2)
    zs = take(nz)
    for k in zk:
        push(zsend.at[zpeer(k)], zrecv.at[k - 1], zs + k - 1, at(zpeer(k), y))

    for j in far_first:
        dk = dot(dsr[0, tile(j)], q2[0]) + dot(dsr[1, tile(j)], q2[1])
        dk = dk + dot(skb[0, tile(j)], pqr[0, band(j)]) + dot(skb[1, tile(j)], pqr[1, band(j)])
        dkb[tile(j)] = dot(flip, (SCALE * dk).astype(bf16)).astype(bf16)
    rs = take(20)

    def give_back(grad, i):
        for d in reversed(hops):
            for pp in range(2):
                push(grad.at[tile(2 * (d + HALO) + pp)], rkv.at[d + HALO, p, i],
                     rs + ((d + HALO) * 2 + p) * 2 + i, 2 * chip(d) + pp)
        push(grad.at[rows(2 * HALO * T + T * o)], rkv.at[HALO, p, i],
             rs + (HALO * 2 + p) * 2 + i, mate)

    qs = take(1)
    push(dqb.at[rows(T * o)], rq, qs, mate)
    give_back(dvb, 1)
    give_back(dkb, 0)

    part = zsend[z].astype(f32)
    for k in reversed(zk):
        arrive(zrecv.at[k - 1], zs + k - 1)
        part = part + zrecv[k - 1].astype(f32)
    low = part.astype(bf16)
    own[...] = low
    ag[z] = low

    both = low.astype(f32)
    rel_part = dot(both[:rb].astype(bf16), wv[0], 1, 1) + dot(both[rb:].astype(bf16), wv[1], 1, 1)
    for i in range(2 * nx):
        xpart[i] = rel_part[:, tile(i)]
    xs = take(2 * nx)
    for k in mk:
        push(xpart.at[mpeer(k)], xrecv.at[k - 1], xs + k - 1,
             2 * c + lax.rem(mpeer(k), 2), mpeer(k) // 2)

    gs = take(nz)
    for k in zk:
        push(own, ag.at[z], gs + k - 1, at(zpeer(k), y))
    total = xpart[m]
    for k in mk:
        arrive(xrecv.at[k - 1], xs + k - 1)
        total = total + xrecv[k - 1]
    relz[z] = total.astype(bf16)
    ls = take(nz)
    for k in zk:
        push(relz.at[z], relz.at[z], ls + k - 1, at(zpeer(k), y))

    for k in reversed(zk):
        arrive(ag.at[zpeer(nz - k)], gs + k - 1)
    every = ag[...].astype(f32)
    for i in range(2):
        grad = every[:, i * rb : (i + 1) * rb].reshape(nz * rb, T).astype(bf16)
        block = rel_v[plane(y), lanes(z * ny * dr2 // T)]
        wtmp[i] = dot(block, grad, 0, 0)
    start = lax.rem(z * ny * dr2, T)

    def of(yy):
        return pl.ds(pl.multiple_of(start + dr2 * yy, dr2), dr2)

    us = take(ny)
    for k in yk:
        push(wtmp.at[:, of(ypeer(k))], wy.at[k - 1], us + k - 1, at(z, ypeer(k)))
    dqo[:, lanes(p)] = dqb[rows(T * p)]
    arrive(rq, qs)
    dqo[:, lanes(o)] = rq[...]
    total = wtmp[:, of(y)]
    for k in yk:
        arrive(wy.at[k - 1], us + k - 1)
        total = total + wy[k - 1]
    wsum[...] = total
    ws = take(1)
    push(wsum.at[:, pl.ds(pl.multiple_of(dr * o, dr), dr)], wrecv, ws, mate)
    ours = pl.ds(pl.multiple_of(dr * p, dr), dr)
    wko[:, lanes(p)] = wsum[0, ours]
    wqo[:, lanes(p)] = wsum[1, ours]

    for k in reversed(zk):
        arrive(relz.at[zpeer(nz - k)], ls + k - 1)
    relo[y] = relz[...].astype(f32).reshape(nz * rb, T).astype(bf16)
    ms = take(ny)
    es = take(ny)
    for k in yk:
        push(relo.at[y], relo.at[y], ms + k - 1, at(z, ypeer(k)))
    push(relo.at[y], relq.at[y], es, mate)

    row = rows(2 * HALO * T + T * p)
    rkv[HALO, p, 0] = dkb[row]
    rkv[HALO, p, 1] = dvb[row]
    arrive(rkv.at[HALO, o, 0], rs + (HALO * 2 + o) * 2)
    arrive(rkv.at[HALO, o, 1], rs + (HALO * 2 + o) * 2 + 1)
    for d in hops:
        for pp in range(2):
            arrive(rkv.at[d + HALO, pp, 0], rs + ((d + HALO) * 2 + pp) * 2)
            arrive(rkv.at[d + HALO, pp, 1], rs + ((d + HALO) * 2 + pp) * 2 + 1)
    for pp in range(2):
        for i, out in ((0, dko), (1, dvo)):
            x = rkv[0, pp, i].astype(f32)
            for d in range(1, 2 * HALO + 1):
                x = x + rkv[d, pp, i].astype(f32)
            out[:, tile(pp)] = x.astype(bf16)

    for k in reversed(yk):
        arrive(relo.at[ypeer(ny - k)], ms + k - 1)
        push(relo.at[ypeer(ny - k)], relq.at[ypeer(ny - k)], es + k, mate)
    arrive(wrecv, ws)
    wko[:, lanes(o)] = wrecv[0]
    wqo[:, lanes(o)] = wrecv[1]
    arrive(relq.at[y], es)
    for k in reversed(yk):
        arrive(relq.at[ypeer(ny - k)], es + k)
    for copy in sent:
        copy.wait_send()


def copy_kernel(dq, dk, dv, rel, relq, wk, wq, dqo, dko, dvo, relo, wqo, wko):
    p = lax.rem(lax.axis_index("seq"), 2)
    dqo[...] = dq[...]
    dko[...] = dk[...]
    dvo[...] = dv[...]
    relo[:, lanes(p)] = rel[...].reshape(relo.shape[0], T).astype(f32)
    relo[:, lanes(1 - p)] = relq[...].reshape(relo.shape[0], T).astype(f32)
    wqo[...] = wq[...]
    wko[...] = wk[...]


def body(ny, queries, keys, values, out_grad, rel_emb, w_query, w_key, doc_lengths, bucket_table):
    nc = lax.axis_size("seq") // 2
    nx = lax.axis_size("head")
    nz = nc // ny
    buckets, width = rel_emb.shape
    span = bucket_table.shape[0]
    rb = buckets // nc
    dr2 = width // nc
    dr = dr2 // 2
    keys_in = TILES * T
    shape = jax.ShapeDtypeStruct
    tab = bucket_table.reshape(1, -1)
    lens = doc_lengths.reshape(1, -1)
    results = pl.pallas_call(
        functools.partial(whole_kernel, nz, ny, nx),
        out_shape=(
            shape((T, 2 * T), bf16),
            shape((T, 2 * T), bf16),
            shape((T, 2 * T), bf16),
            shape((ny, nz * rb, T), bf16),
            shape((ny, nz * rb, T), bf16),
            shape((dr, 2 * T), f32),
            shape((dr, 2 * T), f32),
        ),
        in_specs=[ANY] * 7 + [VM] * 2,
        out_specs=(VM,) * 7,
        scratch_shapes=[
            pltpu.VMEM((buckets, width), bf16),
            pltpu.VMEM((2, width, T), bf16),
            pltpu.VMEM((2 * T, T), bf16),
            pltpu.VMEM((2 * T, T), bf16),
            pltpu.VMEM((keys_in, T), bf16),
            pltpu.VMEM((keys_in, T), bf16),
            pltpu.VMEM((span, 2 * T), bf16),
            pltpu.VMEM((buckets, span), bf16),
            pltpu.VMEM((2, 2 * T, T), bf16),
            pltpu.VMEM((2, 2 * T, T), bf16),
            pltpu.VMEM((2, keys_in, T), bf16),
            pltpu.VMEM((2, span + 4 * T, T), bf16),
            pltpu.VMEM((T, 2 * T), bf16),
            pltpu.VMEM((T, keys_in), bf16),
            pltpu.VMEM((2, keys_in, 2 * T), f32),
            pltpu.VMEM((2, keys_in, 2 * T), f32),
            pltpu.VMEM((2, keys_in, 2 * T), bf16),
            pltpu.VMEM((2, keys_in, 2 * T), bf16),
            pltpu.VMEM((2, keys_in, 2 * T), bf16),
            pltpu.VMEM((2, keys_in, 3 * T), bf16),
            pltpu.VMEM((2, 2 * T, WIDE), bf16),
            pltpu.VMEM((2, 2 * T, span), bf16),
            pltpu.VMEM((keys_in, T), bf16),
            pltpu.VMEM((keys_in, T), bf16),
            pltpu.VMEM((2 * T, T), bf16),
            pltpu.VMEM((T, span), f32),
            pltpu.VMEM((T, span + 4 * T), f32),
            pltpu.VMEM((2, buckets, T), bf16),
            pltpu.VMEM((5, 2, 2, T, T), bf16),
            pltpu.VMEM((T, T), bf16),
            pltpu.VMEM((2, ny, nz * rb, T), bf16),
            pltpu.VMEM((nz, 2 * rb, T), bf16),
            pltpu.VMEM((nz, 2 * rb, T), bf16),
            pltpu.VMEM((2 * rb, T), bf16),
            pltpu.VMEM((nz, 2 * rb, T), bf16),
            pltpu.VMEM((2 * nx, rb, T), f32),
            pltpu.VMEM((2 * nx, rb, T), f32),
            pltpu.VMEM((nz, rb, T), bf16),
            pltpu.VMEM((2, T, T), f32),
            pltpu.VMEM((ny, 2, dr2, T), f32),
            pltpu.VMEM((2, dr2, T), f32),
            pltpu.VMEM((2, dr, T), f32),
            pltpu.SemaphoreType.DMA((144,)),
            pltpu.SemaphoreType.DMA((144,)),
            pltpu.SemaphoreType.DMA((7,)),
            pltpu.SemaphoreType.REGULAR((3,)),
        ],
        compiler_params=pltpu.CompilerParams(collective_id=0, has_side_effects=True),
        name="whole",
    )(queries, keys, values, out_grad, rel_emb, w_query, w_key, tab, lens)
    return tuple(
        pl.pallas_call(
            copy_kernel,
            out_shape=(
                shape((T, 2 * T), bf16),
                shape((T, 2 * T), bf16),
                shape((T, 2 * T), bf16),
                shape((buckets, 2 * T), f32),
                shape((dr, 2 * T), f32),
                shape((dr, 2 * T), f32),
            ),
            in_specs=[VM] * 7,
            out_specs=(VM,) * 6,
            name="results",
        )(*results)
    )


def solution(mesh, ny=NY):
    shard = P("seq", "head")
    return jax.shard_map(
        functools.partial(body, ny),
        mesh=mesh,
        in_specs=(shard,) * 4 + (P(), P(None, "head"), P(None, "head"), P(), P()),
        out_specs=(shard, shard, shard, P(None, "head"), shard, shard),
        check_vma=False,
    )
```

```python
import functools
import math

import jax
import jax.numpy as jnp
from jax import lax
from jax.experimental import pallas as pl
from jax.experimental.pallas import tpu as pltpu
from jax.sharding import PartitionSpec as P

HD = 64
T = 128
NY = 4
HALO = 2
TILES = 2 * (2 * HALO + 1)
WIDE = 9 * T
f32 = jnp.float32
bf16 = jnp.bfloat16
SCALE = 1.0 / math.sqrt(3.0 * HD)
ANY = pl.BlockSpec(memory_space=pl.ANY)
VM = pl.BlockSpec(memory_space=pltpu.VMEM)


def dot(a, b, ca=1, cb=0):
    return lax.dot_general(a, b, (((ca,), (cb,)), ((), ())), preferred_element_type=f32)


def remote(src, dst, send, recv, seq, head=None):
    where = {"seq": seq} if head is None else {"seq": seq, "head": head}
    return pltpu.make_async_remote_copy(
        src_ref=src, dst_ref=dst, send_sem=send, recv_sem=recv,
        device_id=where, device_id_type=pl.DeviceIdType.MESH,
    )


def greet(seq, head=None):
    where = {"seq": seq} if head is None else {"seq": seq, "head": head}
    pl.semaphore_signal(
        pltpu.get_barrier_semaphore(), inc=1, device_id=where,
        device_id_type=pl.DeviceIdType.MESH,
    )


def lanes(p):
    return pl.ds(pl.multiple_of(p * T, T), T)


def rows(start):
    return pl.ds(pl.multiple_of(start, T), T)


def tile(j):
    return slice(j * T, (j + 1) * T)


def skewed(x, first):
    return pltpu.roll(x, first, 1, stride=1, stride_axis=0)


def by_distance(nz):
    return sorted(range(nz), key=lambda k: min(k, nz - k))


def head_only(x, h):
    lane = lax.broadcasted_iota(jnp.int32, x.shape, 1)
    return jnp.where((lane < HD) if h == 0 else (lane >= HD), x, jnp.zeros_like(x))


def indicator(match):
    return match.astype(f32).astype(bf16)


def whole_kernel(
    nz, ny, nx,
    q_ref, k_ref, v_ref, g_ref, rel_ref, wq_ref, wk_ref, tab_ref, len_ref,
    dqo, dko, dvo, relo, relq, wko, wqo,
    rel_v, wv, qw, gw, kw, vw, pb, oht, q2, g2, k2, pqr, qrt, krt,
    sc, dp, prb, dsb, dsr, skb, dsa, ska, dkb, dvb, dqb, gt, ht,
    bp, rkv, rq, yrecv, zsend, zrecv, own, ag, xpart, xrecv,
    wtmp, wy, wsum, wrecv, send, recv, local, known,
):
    nc = nz * ny
    s = lax.axis_index("seq")
    hx = lax.axis_index("head")
    c, p = s // 2, lax.rem(s, 2)
    o = 1 - p
    mate = 2 * c + o
    z, y = c // ny, lax.rem(c, ny)
    m = 2 * hx + p
    buckets, width = rel_ref.shape
    span = tab_ref.shape[1]
    rb = buckets // nc
    dr2 = width // nc
    dr = dr2 // 2
    hops = [-1, 1, -2, 2]

    def chip(d):
        return lax.rem(c + d + nc, nc)

    def ypeer(k):
        return lax.rem(y + k, ny)

    def zpeer(k):
        return lax.rem(z + k, nz)

    def mpeer(k):
        return lax.rem(m + k, 2 * nx)

    def at(zz, yy):
        return 2 * (zz * ny + yy) + p

    def plane(yy):
        return pl.ds(pl.multiple_of(nz * rb * yy, nz * rb), nz * rb)

    yk = sorted(range(1, ny), key=lambda k: -min(k, ny - k))
    zk = sorted(range(1, nz), key=lambda k: -min(k, nz - k))
    mk = range(1, 2 * nx)
    order = by_distance(nz)

    for k in (1, nz - 1):
        greet(at(zpeer(k), y))
    for k in yk:
        greet(at(z, ypeer(k)))
    for d in (-1, 1):
        for pp in range(2):
            greet(2 * chip(d) + pp)
    for k in mk:
        greet(2 * c + lax.rem(mpeer(k), 2), mpeer(k) // 2)
    greet(mate)

    loads = []

    def load(src, dst):
        copy = pltpu.make_async_copy(src, dst, local.at[len(loads)])
        copy.start()
        loads.append(copy)

    load(rel_ref, rel_v)
    load(wk_ref.at[:, lanes(p)], wv.at[0])
    load(wq_ref.at[:, lanes(p)], wv.at[1])
    load(k_ref.at[:, lanes(p)], kw.at[rows(2 * HALO * T + T * p)])
    load(v_ref.at[:, lanes(p)], vw.at[rows(2 * HALO * T + T * p)])
    load(q_ref.at[:, lanes(p)], qw.at[rows(T * p)])
    load(g_ref.at[:, lanes(p)], gw.at[rows(T * p)])

    pl.semaphore_wait(
        pltpu.get_barrier_semaphore(), 2 + len(yk) + 4 + len(mk) + 1
    )

    sent = []
    slots = [0]

    def push(src, dst, slot, seq, head=None):
        copy = remote(src, dst, send.at[len(sent)], recv.at[slot], seq, head)
        copy.start()
        sent.append(copy)

    def take(count):
        base = slots[0]
        slots[0] += count
        return base

    def arrive(dst, slot):
        remote(dst, dst, send.at[0], recv.at[slot], s).wait_recv()

    step = [1 << i for i in range(nz.bit_length()) if (1 << i) < nz // 2]

    def tell(i):
        if i < len(step):
            for k in (step[i], nz - step[i]):
                pl.semaphore_signal(known.at[i], inc=1, device_id={"seq": at(zpeer(k), y)},
                                    device_id_type=pl.DeviceIdType.MESH)

    def hear(i):
        if i < len(step):
            pl.semaphore_wait(known.at[i], 2)

    near = take(4)
    hs = take(8)
    fs = take(4)
    row = rows(T * p)
    push(q_ref.at[:, lanes(o)], qw.at[row], near, mate)
    push(g_ref.at[:, lanes(o)], gw.at[row], near + 1, mate)
    row = rows(2 * HALO * T + T * p)
    push(k_ref.at[:, lanes(o)], kw.at[row], near + 2, mate)
    push(v_ref.at[:, lanes(o)], vw.at[row], near + 3, mate)
    for i, src, dst in ((0, k_ref, kw), (1, v_ref, vw)):
        for d in (-1, 1):
            for pp in range(2):
                push(src.at[:, pl.ds(pp * T, T)], dst.at[rows(2 * T * (HALO - d) + T * p)],
                     hs + (d + 1) * 2 + p * 2 + i, 2 * chip(d) + pp)
    tell(0)

    def pass_on(i, ref):
        for d in (-1, 1):
            for pp in range(2):
                arrive(ref.at[tile(2 * (HALO + d) + pp)], hs + (1 - d) * 2 + pp * 2 + i)
            near_rows = pl.ds(2 * T * (HALO + d), 2 * T)
            far_rows = pl.ds(2 * T * (HALO + 2 * d), 2 * T)
            push(ref.at[near_rows], ref.at[far_rows], fs + d + 1 + i, 2 * chip(-d) + p)

    def passed(i, ref):
        for d in (-1, 1):
            arrive(ref.at[pl.ds(2 * T * (HALO + 2 * d), 2 * T)], fs + d + 1 + i)

    ri = lax.broadcasted_iota(jnp.int32, (T, T), 0)
    ci = lax.broadcasted_iota(jnp.int32, (T, T), 1)
    flip = indicator(ri + ci == T - 1)
    table = jnp.broadcast_to(tab_ref[...], (8, span))
    high = table // 256
    low = (table - 256 * high).astype(f32).astype(bf16)
    high = high.astype(f32).astype(bf16)
    blocks = span // T
    rev = jnp.concatenate(
        [
            256.0 * dot(high[:, tile(blocks - 1 - b)], flip) + dot(low[:, tile(blocks - 1 - b)], flip)
            for b in range(blocks)
        ],
        1,
    )[:1]
    number = lax.broadcasted_iota(jnp.int32, (T, span), 0).astype(f32)
    for b in range(buckets // T):
        oht[tile(b)] = indicator(number + float(b * T) == rev)
    column = jnp.transpose(jnp.broadcast_to(rev, (T, span)))
    lane = lax.broadcasted_iota(jnp.int32, column.shape, 1).astype(f32)
    onehot = jnp.concatenate(
        [indicator(column == lane + float(T * b)) for b in range(buckets // T)], 1
    )

    ndocs = len_ref.shape[1]
    de = lax.broadcasted_iota(jnp.int32, (ndocs, ndocs), 1)
    dd = lax.broadcasted_iota(jnp.int32, (ndocs, ndocs), 0)
    lens = jnp.broadcast_to(len_ref[...], (ndocs, ndocs))
    ends = jnp.sum(jnp.where(de <= dd, lens, 0), axis=1, keepdims=True)
    shift = (c - HALO) * 2 * T
    pos = lax.broadcasted_iota(jnp.int32, (ndocs, 2 * T), 1) + c * 2 * T
    first = jnp.max(jnp.where(ends <= pos, ends, 0), axis=0, keepdims=True) - shift
    last = jnp.min(jnp.where(ends > pos, ends, 1 << 30), axis=0, keepdims=True) - shift

    for copy in loads[:3]:
        copy.wait()
    pos_key = dot(rel_v[...], wv[0]).astype(bf16)
    pass_on(0, kw)
    pos_query = dot(rel_v[...], wv[1]).astype(bf16)
    pb[...] = dot(onehot, jnp.concatenate([pos_key, pos_query], 1)).astype(bf16)
    for h in range(2):
        pqr[h, : 2 * T] = jnp.zeros((2 * T, T), bf16)
        pqr[h, 2 * T : 2 * T + span] = head_only(pb[:, T:], h)
        pqr[h, 2 * T + span :] = jnp.zeros((2 * T, T), bf16)
    ht[...] = jnp.zeros_like(ht)

    hear(0)
    tell(1)
    for copy in loads[3:]:
        copy.wait()
    pass_on(1, vw)
    arrive(qw.at[rows(T * o)], near)
    arrive(gw.at[rows(T * o)], near + 1)

    for h in range(2):
        q2[h] = head_only(qw[...], h)
        g2[h] = head_only(gw[...], h)
    for r in range(2):
        qrt[:, tile(r)] = jnp.transpose(dot(flip, qw[tile(r)])).astype(bf16)
    for h in range(2):
        sc[h, WIDE:, :T] = jnp.zeros((T, T), f32)
        sc[h, :T, T:] = jnp.zeros((T, T), f32)
        for r in range(2):
            a = dot(q2[h, tile(r)], pb[:, :T], 1, 1)
            a = skewed(jnp.concatenate([a, jnp.zeros((T, WIDE - span), f32)], 1), 1)
            for j in range(9):
                sc[h, tile(r + j), tile(r)] = jnp.transpose(a[:, tile(j)])

    arrive(kw.at[rows(2 * HALO * T + T * o)], near + 2)
    arrive(vw.at[rows(2 * HALO * T + T * o)], near + 3)

    top = [jnp.full((8, 2 * T), -1e30, f32) for _ in range(2)]

    def band(j):
        return slice((9 - j) * T, (9 - j) * T + 3 * T)

    def fold(x, op):
        return op(x.reshape(T // 8, 8, 2 * T), axis=0)

    def score(j):
        kt = kw[tile(j)]
        krt[:, tile(j)] = jnp.transpose(dot(flip, kt)).astype(bf16)
        key = lax.broadcasted_iota(jnp.int32, (T, 2 * T), 0) + j * T
        keep = (key >= first) & (key < last)
        for h in range(2):
            k2[h, tile(j)] = head_only(kt, h)
            b = skewed(dot(kt, pqr[h, band(j)], 1, 1), 2 * T + 1)[:, : 2 * T]
            x = SCALE * (dot(kt, q2[h], 1, 1) + sc[h, tile(j)] + b)
            x = jnp.where(keep, x, -1e30)
            sc[h, tile(j)] = x
            top[h] = jnp.maximum(top[h], fold(x, jnp.max))

    def through_values(j):
        for h in range(2):
            dp[h, tile(j)] = dot(vw[tile(j)], g2[h], 1, 1)

    inner, outer = (4, 5, 2, 3, 6, 7), (0, 1, 8, 9)
    for j in inner:
        score(j)
    hear(1)
    tell(2)
    for j in inner:
        through_values(j)
    passed(0, kw)
    for j in outer:
        score(j)
    passed(1, vw)
    for j in outer:
        through_values(j)

    inv, row_dot = [], []
    for h in range(2):
        high_score = jnp.max(top[h], axis=0, keepdims=True)
        total = jnp.zeros((8, 2 * T), f32)
        along = jnp.zeros((8, 2 * T), f32)
        for j in range(TILES):
            x = jnp.exp(sc[h, tile(j)] - high_score)
            sc[h, tile(j)] = x
            total = total + fold(x, jnp.sum)
            along = along + fold(x * dp[h, tile(j)], jnp.sum)
        inv.append(1.0 / jnp.sum(total, axis=0, keepdims=True))
        row_dot.append(jnp.sum(along, axis=0, keepdims=True) * inv[h])

    for h in range(2):
        half = slice(h * HD, (h + 1) * HD)
        for j in range(TILES):
            prob = sc[h, tile(j)] * inv[h]
            ds = (prob * (dp[h, tile(j)] - row_dot[h])).astype(bf16)
            prb[h, tile(j)] = prob.astype(bf16)
            dsb[h, tile(j)] = ds
            back = dot(flip, ds)
            dsr[h, tile(j)] = back.astype(bf16)
            skew = skewed(jnp.concatenate([back, jnp.zeros((T, T), f32)], 1), 0).astype(bf16)
            skb[h, tile(j)] = skew
            ht[half, band(j)] += dot(krt[half, tile(j)], skew)

    ys = take(2 * ny)

    def scatter(i, offsets):
        bp[i] = (SCALE * dot(oht[...], offsets.astype(bf16), 1, 1)).astype(bf16)
        for k in yk:
            push(bp.at[i, plane(ypeer(k))], yrecv.at[i, k - 1],
                 ys + i * ny + k - 1, at(z, ypeer(k)))

    scatter(1, ht[:, 2 * T : 2 * T + span])
    for h in range(2):
        half = slice(h * HD, (h + 1) * HD)
        for r in range(2):
            back = dot(flip, dsb[h, r * T : r * T + WIDE, tile(r)], 1, 1)
            dsa[h, tile(r)] = back.astype(bf16)
            skew = skewed(back, span)[:, :span].astype(bf16)
            ska[h, tile(r)] = skew
            part = dot(qrt[half, tile(r)], skew)
            if r == 0:
                gt[half] = part
            else:
                gt[half] += part
    scatter(0, gt[...])

    far_first = [j for d in (-2, 2, -1, 1, 0) for j in (2 * (d + HALO), 2 * (d + HALO) + 1)]
    for j in far_first:
        dv = dot(prb[0, tile(j)], g2[0]) + dot(prb[1, tile(j)], g2[1])
        dvb[tile(j)] = dv.astype(bf16)
    for r in range(2):
        reach = slice(r * T, r * T + WIDE)
        dq = dot(dsa[0, tile(r)], k2[0, reach]) + dot(dsa[1, tile(r)], k2[1, reach])
        for h in range(2):
            dq = dq + head_only(dot(ska[h, tile(r)], pb[:, :T]), h)
        dqb[tile(r)] = dot(flip, (SCALE * dq).astype(bf16)).astype(bf16)

    parts = []
    for i in range(2):
        part = bp[i, plane(y)].astype(f32)
        for k in yk:
            arrive(yrecv.at[i, k - 1], ys + i * ny + k - 1)
        for k in yk:
            part = part + yrecv[i, k - 1].astype(f32)
        parts.append(part.reshape(nz, rb, T))
    zsend[...] = jnp.concatenate(parts, 1).astype(bf16)

    hear(2)
    zs = take(nz)
    for k in zk:
        push(zsend.at[zpeer(k)], zrecv.at[k - 1], zs + k - 1, at(zpeer(k), y))

    rs = take(20)

    def give_back(grad, i):
        for d in reversed(hops):
            for pp in range(2):
                push(grad.at[tile(2 * (d + HALO) + pp)], rkv.at[d + HALO, p, i],
                     rs + ((d + HALO) * 2 + p) * 2 + i, 2 * chip(d) + pp)
        push(grad.at[rows(2 * HALO * T + T * o)], rkv.at[HALO, p, i],
             rs + (HALO * 2 + p) * 2 + i, mate)

    qs = take(1)
    push(dqb.at[rows(T * o)], rq, qs, mate)
    give_back(dvb, 1)
    for j in far_first:
        dk = dot(dsr[0, tile(j)], q2[0]) + dot(dsr[1, tile(j)], q2[1])
        dk = dk + dot(skb[0, tile(j)], pqr[0, band(j)]) + dot(skb[1, tile(j)], pqr[1, band(j)])
        dkb[tile(j)] = dot(flip, (SCALE * dk).astype(bf16)).astype(bf16)
    give_back(dkb, 0)

    part = zsend[z].astype(f32)
    for k in reversed(zk):
        arrive(zrecv.at[k - 1], zs + k - 1)
        part = part + zrecv[k - 1].astype(f32)
    low = part.astype(bf16)
    own[...] = low
    ag[z] = low

    both = low.astype(f32)
    rel_part = dot(both[:rb].astype(bf16), wv[0], 1, 1) + dot(both[rb:].astype(bf16), wv[1], 1, 1)
    for i in range(2 * nx):
        xpart[i] = rel_part[:, tile(i)]
    xs = take(2 * nx)
    for k in mk:
        push(xpart.at[mpeer(k)], xrecv.at[k - 1], xs + k - 1,
             2 * c + lax.rem(mpeer(k), 2), mpeer(k) // 2)

    gs = take(nz)
    for k in zk:
        push(own, ag.at[z], gs + k - 1, at(zpeer(k), y))
    total = xpart[m]
    for k in mk:
        arrive(xrecv.at[k - 1], xs + k - 1)
        total = total + xrecv[k - 1]
    relo[y, 0] = total.astype(bf16)
    ls = take(nz)
    for k in zk:
        push(relo.at[y, 0], relo.at[y, order.index(k)], ls + k - 1, at(zpeer(k), y))

    for k in reversed(zk):
        arrive(ag.at[zpeer(nz - k)], gs + k - 1)
    every = ag[...].astype(f32)
    for i in range(2):
        grad = every[:, i * rb : (i + 1) * rb].reshape(nz * rb, T).astype(bf16)
        block = rel_v[plane(y), lanes(z * ny * dr2 // T)]
        wtmp[i] = dot(block, grad, 0, 0)
    start = lax.rem(z * ny * dr2, T)

    def of(yy):
        return pl.ds(pl.multiple_of(start + dr2 * yy, dr2), dr2)

    us = take(ny)
    for k in yk:
        push(wtmp.at[:, of(ypeer(k))], wy.at[k - 1], us + k - 1, at(z, ypeer(k)))

    ms = take(2 * ny)
    es = take(2 * ny)

    def piece(part):
        return pl.ds(part * (nz // 2), nz // 2)

    def spread(part):
        for i in range(part * (nz // 2), (part + 1) * (nz // 2)):
            if i:
                arrive(relo.at[y, i], ls + order[i] - 1)
        for k in yk:
            push(relo.at[y, piece(part)], relo.at[y, piece(part)],
                 ms + part * ny + k - 1, at(z, ypeer(k)))
        push(relo.at[y, piece(part)], relq.at[y, piece(part)], es + part * ny, mate)

    spread(0)
    dqo[:, lanes(p)] = dqb[rows(T * p)]
    arrive(rq, qs)
    dqo[:, lanes(o)] = rq[...]
    total = wtmp[:, of(y)]
    for k in yk:
        arrive(wy.at[k - 1], us + k - 1)
        total = total + wy[k - 1]
    wsum[...] = total
    ws = take(1)
    push(wsum.at[:, pl.ds(pl.multiple_of(dr * o, dr), dr)], wrecv, ws, mate)
    ours = pl.ds(pl.multiple_of(dr * p, dr), dr)
    wko[:, lanes(p)] = wsum[0, ours]
    wqo[:, lanes(p)] = wsum[1, ours]

    spread(1)

    for part in range(2):
        for k in reversed(yk):
            yy = ypeer(ny - k)
            arrive(relo.at[yy, piece(part)], ms + part * ny + k - 1)
            push(relo.at[yy, piece(part)], relq.at[yy, piece(part)], es + part * ny + k, mate)

    row = rows(2 * HALO * T + T * p)
    rkv[HALO, p, 0] = dkb[row]
    rkv[HALO, p, 1] = dvb[row]
    arrive(rkv.at[HALO, o, 0], rs + (HALO * 2 + o) * 2)
    arrive(rkv.at[HALO, o, 1], rs + (HALO * 2 + o) * 2 + 1)
    for d in hops:
        for pp in range(2):
            arrive(rkv.at[d + HALO, pp, 0], rs + ((d + HALO) * 2 + pp) * 2)
            arrive(rkv.at[d + HALO, pp, 1], rs + ((d + HALO) * 2 + pp) * 2 + 1)
    for pp in range(2):
        for i, out in ((0, dko), (1, dvo)):
            x = rkv[0, pp, i].astype(f32)
            for d in range(1, 2 * HALO + 1):
                x = x + rkv[d, pp, i].astype(f32)
            out[:, tile(pp)] = x.astype(bf16)

    arrive(wrecv, ws)
    wko[:, lanes(o)] = wrecv[0]
    wqo[:, lanes(o)] = wrecv[1]
    for part in range(2):
        arrive(relq.at[y, piece(part)], es + part * ny)
        for k in reversed(yk):
            arrive(relq.at[ypeer(ny - k), piece(part)], es + part * ny + k)
    for copy in sent:
        copy.wait_send()


def copy_kernel(ny, dq, dk, dv, rel, relq, wk, wq, dqo, dko, dvo, relo, wqo, wko):
    nz, rb = rel.shape[1:3]
    seq = lax.axis_index("seq")
    p, z = lax.rem(seq, 2), seq // (2 * ny)
    dqo[...] = dq[...]
    dko[...] = dk[...]
    dvo[...] = dv[...]
    for i, k in enumerate(by_distance(nz)):
        zz = lax.rem(z - k + nz, nz)
        for yy in range(ny):
            row = pl.ds(pl.multiple_of((yy * nz + zz) * rb, rb), rb)
            relo[row, lanes(p)] = rel[yy, i].astype(f32)
            relo[row, lanes(1 - p)] = relq[yy, i].astype(f32)
    wqo[...] = wq[...]
    wko[...] = wk[...]


def body(ny, queries, keys, values, out_grad, rel_emb, w_query, w_key, doc_lengths, bucket_table):
    nc = lax.axis_size("seq") // 2
    nx = lax.axis_size("head")
    nz = nc // ny
    buckets, width = rel_emb.shape
    span = bucket_table.shape[0]
    rb = buckets // nc
    dr2 = width // nc
    dr = dr2 // 2
    keys_in = TILES * T
    shape = jax.ShapeDtypeStruct
    tab = bucket_table.reshape(1, -1)
    lens = doc_lengths.reshape(1, -1)
    results = pl.pallas_call(
        functools.partial(whole_kernel, nz, ny, nx),
        out_shape=(
            shape((T, 2 * T), bf16),
            shape((T, 2 * T), bf16),
            shape((T, 2 * T), bf16),
            shape((ny, nz, rb, T), bf16),
            shape((ny, nz, rb, T), bf16),
            shape((dr, 2 * T), f32),
            shape((dr, 2 * T), f32),
        ),
        in_specs=[ANY] * 7 + [VM] * 2,
        out_specs=(VM,) * 7,
        scratch_shapes=[
            pltpu.VMEM((buckets, width), bf16),
            pltpu.VMEM((2, width, T), bf16),
            pltpu.VMEM((2 * T, T), bf16),
            pltpu.VMEM((2 * T, T), bf16),
            pltpu.VMEM((keys_in, T), bf16),
            pltpu.VMEM((keys_in, T), bf16),
            pltpu.VMEM((span, 2 * T), bf16),
            pltpu.VMEM((buckets, span), bf16),
            pltpu.VMEM((2, 2 * T, T), bf16),
            pltpu.VMEM((2, 2 * T, T), bf16),
            pltpu.VMEM((2, keys_in, T), bf16),
            pltpu.VMEM((2, span + 4 * T, T), bf16),
            pltpu.VMEM((T, 2 * T), bf16),
            pltpu.VMEM((T, keys_in), bf16),
            pltpu.VMEM((2, keys_in, 2 * T), f32),
            pltpu.VMEM((2, keys_in, 2 * T), f32),
            pltpu.VMEM((2, keys_in, 2 * T), bf16),
            pltpu.VMEM((2, keys_in, 2 * T), bf16),
            pltpu.VMEM((2, keys_in, 2 * T), bf16),
            pltpu.VMEM((2, keys_in, 3 * T), bf16),
            pltpu.VMEM((2, 2 * T, WIDE), bf16),
            pltpu.VMEM((2, 2 * T, span), bf16),
            pltpu.VMEM((keys_in, T), bf16),
            pltpu.VMEM((keys_in, T), bf16),
            pltpu.VMEM((2 * T, T), bf16),
            pltpu.VMEM((T, span), f32),
            pltpu.VMEM((T, span + 4 * T), f32),
            pltpu.VMEM((2, buckets, T), bf16),
            pltpu.VMEM((5, 2, 2, T, T), bf16),
            pltpu.VMEM((T, T), bf16),
            pltpu.VMEM((2, ny, nz * rb, T), bf16),
            pltpu.VMEM((nz, 2 * rb, T), bf16),
            pltpu.VMEM((nz, 2 * rb, T), bf16),
            pltpu.VMEM((2 * rb, T), bf16),
            pltpu.VMEM((nz, 2 * rb, T), bf16),
            pltpu.VMEM((2 * nx, rb, T), f32),
            pltpu.VMEM((2 * nx, rb, T), f32),
            pltpu.VMEM((2, T, T), f32),
            pltpu.VMEM((ny, 2, dr2, T), f32),
            pltpu.VMEM((2, dr2, T), f32),
            pltpu.VMEM((2, dr, T), f32),
            pltpu.SemaphoreType.DMA((144,)),
            pltpu.SemaphoreType.DMA((144,)),
            pltpu.SemaphoreType.DMA((7,)),
            pltpu.SemaphoreType.REGULAR((3,)),
        ],
        compiler_params=pltpu.CompilerParams(collective_id=0, has_side_effects=True),
        name="whole",
    )(queries, keys, values, out_grad, rel_emb, w_query, w_key, tab, lens)
    return tuple(
        pl.pallas_call(
            functools.partial(copy_kernel, ny),
            out_shape=(
                shape((T, 2 * T), bf16),
                shape((T, 2 * T), bf16),
                shape((T, 2 * T), bf16),
                shape((buckets, 2 * T), f32),
                shape((dr, 2 * T), f32),
                shape((dr, 2 * T), f32),
            ),
            in_specs=[VM] * 7,
            out_specs=(VM,) * 6,
            name="results",
        )(*results)
    )


def solution(mesh, ny=NY):
    shard = P("seq", "head")
    return jax.shard_map(
        functools.partial(body, ny),
        mesh=mesh,
        in_specs=(shard,) * 4 + (P(), P(None, "head"), P(None, "head"), P(), P()),
        out_specs=(shard, shard, shard, P(None, "head"), shard, shard),
        check_vma=False,
    )
```

```python
import functools
import math

import jax
import jax.numpy as jnp
from jax import lax
from jax.experimental import pallas as pl
from jax.experimental.pallas import tpu as pltpu
from jax.sharding import PartitionSpec as P

HD = 64
T = 128
NY = 4
HALO = 2
TILES = 2 * (2 * HALO + 1)
WIDE = 9 * T
f32 = jnp.float32
bf16 = jnp.bfloat16
SCALE = 1.0 / math.sqrt(3.0 * HD)
ANY = pl.BlockSpec(memory_space=pl.ANY)
VM = pl.BlockSpec(memory_space=pltpu.VMEM)


def dot(a, b, ca=1, cb=0):
    return lax.dot_general(a, b, (((ca,), (cb,)), ((), ())), preferred_element_type=f32)


def remote(src, dst, send, recv, seq, head=None):
    where = {"seq": seq} if head is None else {"seq": seq, "head": head}
    return pltpu.make_async_remote_copy(
        src_ref=src, dst_ref=dst, send_sem=send, recv_sem=recv,
        device_id=where, device_id_type=pl.DeviceIdType.MESH,
    )


def greet(seq, head=None):
    where = {"seq": seq} if head is None else {"seq": seq, "head": head}
    pl.semaphore_signal(
        pltpu.get_barrier_semaphore(), inc=1, device_id=where,
        device_id_type=pl.DeviceIdType.MESH,
    )


def lanes(p):
    return pl.ds(pl.multiple_of(p * T, T), T)


def rows(start):
    return pl.ds(pl.multiple_of(start, T), T)


def tile(j):
    return slice(j * T, (j + 1) * T)


def skewed(x, first):
    return pltpu.roll(x, first, 1, stride=1, stride_axis=0)


def by_distance(nz):
    return sorted(range(nz), key=lambda k: min(k, nz - k))


def head_only(x, h):
    lane = lax.broadcasted_iota(jnp.int32, x.shape, 1)
    return jnp.where((lane < HD) if h == 0 else (lane >= HD), x, jnp.zeros_like(x))


def indicator(match):
    return match.astype(f32).astype(bf16)


def whole_kernel(
    nz, ny, nx,
    q_ref, k_ref, v_ref, g_ref, rel_ref, wq_ref, wk_ref, tab_ref, len_ref,
    dqo, dko, dvo, relo, relq, wko, wqo,
    rel_v, wv, qw, gw, kw, vw, pb, oht, q2, g2, k2, pqr, qrt, krt,
    sc, dp, prb, dsb, dsr, skb, dsa, ska, dkb, dvb, dqb, gt, ht,
    bp, rkv, rq, yrecv, zsend, zrecv, own, ag, xpart, xrecv,
    wtmp, wy, wsum, wrecv, send, recv, local, known,
):
    nc = nz * ny
    s = lax.axis_index("seq")
    hx = lax.axis_index("head")
    c, p = s // 2, lax.rem(s, 2)
    o = 1 - p
    mate = 2 * c + o
    z, y = c // ny, lax.rem(c, ny)
    m = 2 * hx + p
    buckets, width = rel_ref.shape
    span = tab_ref.shape[1]
    rb = buckets // nc
    dr2 = width // nc
    dr = dr2 // 2
    hops = [-1, 1, -2, 2]

    def chip(d):
        return lax.rem(c + d + nc, nc)

    def ypeer(k):
        return lax.rem(y + k, ny)

    def zpeer(k):
        return lax.rem(z + k, nz)

    def mpeer(k):
        return lax.rem(m + k, 2 * nx)

    def at(zz, yy):
        return 2 * (zz * ny + yy) + p

    def plane(yy):
        return pl.ds(pl.multiple_of(nz * rb * yy, nz * rb), nz * rb)

    yk = sorted(range(1, ny), key=lambda k: -min(k, ny - k))
    zk = sorted(range(1, nz), key=lambda k: -min(k, nz - k))
    mk = range(1, 2 * nx)
    order = by_distance(nz)

    for d in (-1, 1):
        for pp in range(2):
            greet(2 * chip(d) + pp)
    for k in (1, nz - 1):
        greet(at(zpeer(k), y))
    for k in yk:
        greet(at(z, ypeer(k)))
    for k in mk:
        greet(2 * c + lax.rem(mpeer(k), 2), mpeer(k) // 2)
    greet(mate)

    loads = []

    def load(src, dst):
        copy = pltpu.make_async_copy(src, dst, local.at[len(loads)])
        copy.start()
        loads.append(copy)

    load(rel_ref, rel_v)
    load(wk_ref.at[:, lanes(p)], wv.at[0])
    load(wq_ref.at[:, lanes(p)], wv.at[1])
    load(k_ref.at[:, lanes(p)], kw.at[rows(2 * HALO * T + T * p)])
    load(v_ref.at[:, lanes(p)], vw.at[rows(2 * HALO * T + T * p)])
    load(q_ref.at[:, lanes(p)], qw.at[rows(T * p)])
    load(g_ref.at[:, lanes(p)], gw.at[rows(T * p)])

    pl.semaphore_wait(
        pltpu.get_barrier_semaphore(), 2 + len(yk) + 4 + len(mk) + 1
    )

    sent = []
    slots = [0]

    def push(src, dst, slot, seq, head=None):
        copy = remote(src, dst, send.at[len(sent)], recv.at[slot], seq, head)
        copy.start()
        sent.append(copy)

    def take(count):
        base = slots[0]
        slots[0] += count
        return base

    def arrive(dst, slot):
        remote(dst, dst, send.at[0], recv.at[slot], s).wait_recv()

    step = [1 << i for i in range(nz.bit_length()) if (1 << i) < nz // 2]

    def tell(i):
        if i < len(step):
            for k in (step[i], nz - step[i]):
                pl.semaphore_signal(known.at[i], inc=1, device_id={"seq": at(zpeer(k), y)},
                                    device_id_type=pl.DeviceIdType.MESH)

    def hear(i):
        if i < len(step):
            pl.semaphore_wait(known.at[i], 2)

    near = take(4)
    hs = take(8)
    fs = take(4)
    row = rows(T * p)
    push(q_ref.at[:, lanes(o)], qw.at[row], near, mate)
    push(g_ref.at[:, lanes(o)], gw.at[row], near + 1, mate)
    row = rows(2 * HALO * T + T * p)
    push(k_ref.at[:, lanes(o)], kw.at[row], near + 2, mate)
    push(v_ref.at[:, lanes(o)], vw.at[row], near + 3, mate)
    for i, src, dst in ((0, k_ref, kw), (1, v_ref, vw)):
        for d in (-1, 1):
            for pp in range(2):
                push(src.at[:, pl.ds(pp * T, T)], dst.at[rows(2 * T * (HALO - d) + T * p)],
                     hs + (d + 1) * 2 + p * 2 + i, 2 * chip(d) + pp)
    tell(0)

    def pass_on(i, ref):
        for d in (-1, 1):
            for pp in range(2):
                arrive(ref.at[tile(2 * (HALO + d) + pp)], hs + (1 - d) * 2 + pp * 2 + i)
            near_rows = pl.ds(2 * T * (HALO + d), 2 * T)
            far_rows = pl.ds(2 * T * (HALO + 2 * d), 2 * T)
            push(ref.at[near_rows], ref.at[far_rows], fs + d + 1 + i, 2 * chip(-d) + p)

    def passed(i, ref):
        for d in (-1, 1):
            arrive(ref.at[pl.ds(2 * T * (HALO + 2 * d), 2 * T)], fs + d + 1 + i)

    ri = lax.broadcasted_iota(jnp.int32, (T, T), 0)
    ci = lax.broadcasted_iota(jnp.int32, (T, T), 1)
    flip = indicator(ri + ci == T - 1)
    table = jnp.broadcast_to(tab_ref[...], (8, span))
    high = table // 256
    low = (table - 256 * high).astype(f32).astype(bf16)
    high = high.astype(f32).astype(bf16)
    blocks = span // T
    rev = jnp.concatenate(
        [
            256.0 * dot(high[:, tile(blocks - 1 - b)], flip) + dot(low[:, tile(blocks - 1 - b)], flip)
            for b in range(blocks)
        ],
        1,
    )[:1]
    number = lax.broadcasted_iota(jnp.int32, (T, span), 0).astype(f32)
    for b in range(buckets // T):
        oht[tile(b)] = indicator(number + float(b * T) == rev)
    column = jnp.transpose(jnp.broadcast_to(rev, (T, span)))
    lane = lax.broadcasted_iota(jnp.int32, column.shape, 1).astype(f32)
    onehot = jnp.concatenate(
        [indicator(column == lane + float(T * b)) for b in range(buckets // T)], 1
    )

    ndocs = len_ref.shape[1]
    de = lax.broadcasted_iota(jnp.int32, (ndocs, ndocs), 1)
    dd = lax.broadcasted_iota(jnp.int32, (ndocs, ndocs), 0)
    lens = jnp.broadcast_to(len_ref[...], (ndocs, ndocs))
    ends = jnp.sum(jnp.where(de <= dd, lens, 0), axis=1, keepdims=True)
    shift = (c - HALO) * 2 * T
    pos = lax.broadcasted_iota(jnp.int32, (ndocs, 2 * T), 1) + c * 2 * T
    first = jnp.max(jnp.where(ends <= pos, ends, 0), axis=0, keepdims=True) - shift
    last = jnp.min(jnp.where(ends > pos, ends, 1 << 30), axis=0, keepdims=True) - shift

    for copy in loads[:3]:
        copy.wait()
    pos_key = dot(rel_v[...], wv[0]).astype(bf16)
    pass_on(0, kw)
    pos_query = dot(rel_v[...], wv[1]).astype(bf16)
    pb[...] = dot(onehot, jnp.concatenate([pos_key, pos_query], 1)).astype(bf16)
    for h in range(2):
        pqr[h, : 2 * T] = jnp.zeros((2 * T, T), bf16)
        pqr[h, 2 * T : 2 * T + span] = head_only(pb[:, T:], h)
        pqr[h, 2 * T + span :] = jnp.zeros((2 * T, T), bf16)
    ht[...] = jnp.zeros_like(ht)

    hear(0)
    tell(1)
    for copy in loads[3:]:
        copy.wait()
    pass_on(1, vw)
    arrive(qw.at[rows(T * o)], near)
    arrive(gw.at[rows(T * o)], near + 1)

    for h in range(2):
        q2[h] = head_only(qw[...], h)
        g2[h] = head_only(gw[...], h)
    for r in range(2):
        qrt[:, tile(r)] = jnp.transpose(dot(flip, qw[tile(r)])).astype(bf16)
    for h in range(2):
        sc[h, WIDE:, :T] = jnp.zeros((T, T), f32)
        sc[h, :T, T:] = jnp.zeros((T, T), f32)
        for r in range(2):
            a = dot(q2[h, tile(r)], pb[:, :T], 1, 1)
            a = skewed(jnp.concatenate([a, jnp.zeros((T, WIDE - span), f32)], 1), 1)
            for j in range(9):
                sc[h, tile(r + j), tile(r)] = jnp.transpose(a[:, tile(j)])

    arrive(kw.at[rows(2 * HALO * T + T * o)], near + 2)
    arrive(vw.at[rows(2 * HALO * T + T * o)], near + 3)

    top = [jnp.full((8, 2 * T), -1e30, f32) for _ in range(2)]

    def band(j):
        return slice((9 - j) * T, (9 - j) * T + 3 * T)

    def fold(x, op):
        return op(x.reshape(T // 8, 8, 2 * T), axis=0)

    def score(j):
        kt = kw[tile(j)]
        krt[:, tile(j)] = jnp.transpose(dot(flip, kt)).astype(bf16)
        key = lax.broadcasted_iota(jnp.int32, (T, 2 * T), 0) + j * T
        keep = (key >= first) & (key < last)
        for h in range(2):
            k2[h, tile(j)] = head_only(kt, h)
            b = skewed(dot(kt, pqr[h, band(j)], 1, 1), 2 * T + 1)[:, : 2 * T]
            x = SCALE * (dot(kt, q2[h], 1, 1) + sc[h, tile(j)] + b)
            x = jnp.where(keep, x, -1e30)
            sc[h, tile(j)] = x
            top[h] = jnp.maximum(top[h], fold(x, jnp.max))

    def through_values(j):
        for h in range(2):
            dp[h, tile(j)] = dot(vw[tile(j)], g2[h], 1, 1)

    inner, outer = (4, 5, 2, 3, 6, 7), (0, 1, 8, 9)
    for j in inner:
        score(j)
    hear(1)
    tell(2)
    for j in inner:
        through_values(j)
    passed(0, kw)
    for j in outer:
        score(j)

    totals, alongs = [], []
    for h in range(2):
        high_score = jnp.max(top[h], axis=0, keepdims=True)
        total = jnp.zeros((8, 2 * T), f32)
        along = jnp.zeros((8, 2 * T), f32)
        for j in inner + outer:
            x = jnp.exp(sc[h, tile(j)] - high_score)
            sc[h, tile(j)] = x
            total = total + fold(x, jnp.sum)
            if j in inner:
                along = along + fold(x * dp[h, tile(j)], jnp.sum)
        totals.append(total)
        alongs.append(along)
    passed(1, vw)
    inv, row_dot = [], []
    for h in range(2):
        along = alongs[h]
        for j in outer:
            x = dot(vw[tile(j)], g2[h], 1, 1)
            dp[h, tile(j)] = x
            along = along + fold(sc[h, tile(j)] * x, jnp.sum)
        inv.append(1.0 / jnp.sum(totals[h], axis=0, keepdims=True))
        row_dot.append(jnp.sum(along, axis=0, keepdims=True) * inv[h])

    for h in range(2):
        half = slice(h * HD, (h + 1) * HD)
        for j in range(TILES):
            prob = sc[h, tile(j)] * inv[h]
            ds = (prob * (dp[h, tile(j)] - row_dot[h])).astype(bf16)
            prb[h, tile(j)] = prob.astype(bf16)
            dsb[h, tile(j)] = ds
            back = dot(flip, ds)
            dsr[h, tile(j)] = back.astype(bf16)
            skew = skewed(jnp.concatenate([back, jnp.zeros((T, T), f32)], 1), 0).astype(bf16)
            skb[h, tile(j)] = skew
            ht[half, band(j)] += dot(krt[half, tile(j)], skew)

    ys = take(2 * ny)

    def scatter(i, offsets):
        bp[i] = (SCALE * dot(oht[...], offsets.astype(bf16), 1, 1)).astype(bf16)
        for k in yk:
            push(bp.at[i, plane(ypeer(k))], yrecv.at[i, k - 1],
                 ys + i * ny + k - 1, at(z, ypeer(k)))

    scatter(1, ht[:, 2 * T : 2 * T + span])
    for h in range(2):
        half = slice(h * HD, (h + 1) * HD)
        for r in range(2):
            back = dot(flip, dsb[h, r * T : r * T + WIDE, tile(r)], 1, 1)
            dsa[h, tile(r)] = back.astype(bf16)
            skew = skewed(back, span)[:, :span].astype(bf16)
            ska[h, tile(r)] = skew
            part = dot(qrt[half, tile(r)], skew)
            if r == 0:
                gt[half] = part
            else:
                gt[half] += part
    scatter(0, gt[...])

    far_first = [j for d in (-2, 2, -1, 1, 0) for j in (2 * (d + HALO), 2 * (d + HALO) + 1)]
    for j in far_first:
        dv = dot(prb[0, tile(j)], g2[0]) + dot(prb[1, tile(j)], g2[1])
        dvb[tile(j)] = dv.astype(bf16)
    for r in range(2):
        reach = slice(r * T, r * T + WIDE)
        dq = dot(dsa[0, tile(r)], k2[0, reach]) + dot(dsa[1, tile(r)], k2[1, reach])
        for h in range(2):
            dq = dq + head_only(dot(ska[h, tile(r)], pb[:, :T]), h)
        dqb[tile(r)] = dot(flip, (SCALE * dq).astype(bf16)).astype(bf16)

    parts = []
    for i in range(2):
        part = bp[i, plane(y)].astype(f32)
        for k in yk:
            arrive(yrecv.at[i, k - 1], ys + i * ny + k - 1)
        for k in yk:
            part = part + yrecv[i, k - 1].astype(f32)
        parts.append(part.reshape(nz, rb, T))
    zsend[...] = jnp.concatenate(parts, 1).astype(bf16)

    hear(2)
    zs = take(nz)
    for k in zk:
        push(zsend.at[zpeer(k)], zrecv.at[k - 1], zs + k - 1, at(zpeer(k), y))

    rs = take(20)

    def give_back(grad, i):
        for d in reversed(hops):
            for pp in range(2):
                push(grad.at[tile(2 * (d + HALO) + pp)], rkv.at[d + HALO, p, i],
                     rs + ((d + HALO) * 2 + p) * 2 + i, 2 * chip(d) + pp)
        push(grad.at[rows(2 * HALO * T + T * o)], rkv.at[HALO, p, i],
             rs + (HALO * 2 + p) * 2 + i, mate)

    qs = take(1)
    push(dqb.at[rows(T * o)], rq, qs, mate)
    give_back(dvb, 1)
    for j in far_first:
        dk = dot(dsr[0, tile(j)], q2[0]) + dot(dsr[1, tile(j)], q2[1])
        dk = dk + dot(skb[0, tile(j)], pqr[0, band(j)]) + dot(skb[1, tile(j)], pqr[1, band(j)])
        dkb[tile(j)] = dot(flip, (SCALE * dk).astype(bf16)).astype(bf16)
    give_back(dkb, 0)

    part = zsend[z].astype(f32)
    for k in reversed(zk):
        arrive(zrecv.at[k - 1], zs + k - 1)
        part = part + zrecv[k - 1].astype(f32)
    low = part.astype(bf16)
    own[...] = low
    ag[z] = low

    both = low.astype(f32)
    rel_part = dot(both[:rb].astype(bf16), wv[0], 1, 1) + dot(both[rb:].astype(bf16), wv[1], 1, 1)
    for i in range(2 * nx):
        xpart[i] = rel_part[:, tile(i)]
    xs = take(2 * nx)
    for k in mk:
        push(xpart.at[mpeer(k)], xrecv.at[k - 1], xs + k - 1,
             2 * c + lax.rem(mpeer(k), 2), mpeer(k) // 2)

    gs = take(nz)
    for k in zk:
        push(own, ag.at[z], gs + k - 1, at(zpeer(k), y))
    total = xpart[m]
    for k in mk:
        arrive(xrecv.at[k - 1], xs + k - 1)
        total = total + xrecv[k - 1]
    relo[y, 0] = total.astype(bf16)
    ls = take(nz)
    for k in zk:
        push(relo.at[y, 0], relo.at[y, order.index(k)], ls + k - 1, at(zpeer(k), y))

    for k in reversed(zk):
        arrive(ag.at[zpeer(nz - k)], gs + k - 1)
    every = ag[...].astype(f32)
    for i in range(2):
        grad = every[:, i * rb : (i + 1) * rb].reshape(nz * rb, T).astype(bf16)
        block = rel_v[plane(y), lanes(z * ny * dr2 // T)]
        wtmp[i] = dot(block, grad, 0, 0)
    start = lax.rem(z * ny * dr2, T)

    def of(yy):
        return pl.ds(pl.multiple_of(start + dr2 * yy, dr2), dr2)

    us = take(ny)
    for k in yk:
        push(wtmp.at[:, of(ypeer(k))], wy.at[k - 1], us + k - 1, at(z, ypeer(k)))

    ms = take(2 * ny)
    es = take(2 * ny)

    def piece(part):
        return pl.ds(part * (nz // 2), nz // 2)

    def spread(part):
        for i in range(part * (nz // 2), (part + 1) * (nz // 2)):
            if i:
                arrive(relo.at[y, i], ls + order[i] - 1)
        for k in yk:
            push(relo.at[y, piece(part)], relo.at[y, piece(part)],
                 ms + part * ny + k - 1, at(z, ypeer(k)))
        push(relo.at[y, piece(part)], relq.at[y, piece(part)], es + part * ny, mate)

    spread(0)
    dqo[:, lanes(p)] = dqb[rows(T * p)]
    arrive(rq, qs)
    dqo[:, lanes(o)] = rq[...]
    total = wtmp[:, of(y)]
    for k in yk:
        arrive(wy.at[k - 1], us + k - 1)
        total = total + wy[k - 1]
    wsum[...] = total
    ws = take(1)
    push(wsum.at[:, pl.ds(pl.multiple_of(dr * o, dr), dr)], wrecv, ws, mate)
    ours = pl.ds(pl.multiple_of(dr * p, dr), dr)
    wko[:, lanes(p)] = wsum[0, ours]
    wqo[:, lanes(p)] = wsum[1, ours]

    spread(1)

    row = rows(2 * HALO * T + T * p)
    rkv[HALO, p, 0] = dkb[row]
    rkv[HALO, p, 1] = dvb[row]
    arrive(rkv.at[HALO, o, 0], rs + (HALO * 2 + o) * 2)
    arrive(rkv.at[HALO, o, 1], rs + (HALO * 2 + o) * 2 + 1)
    for d in hops:
        for pp in range(2):
            arrive(rkv.at[d + HALO, pp, 0], rs + ((d + HALO) * 2 + pp) * 2)
            arrive(rkv.at[d + HALO, pp, 1], rs + ((d + HALO) * 2 + pp) * 2 + 1)
    for pp in range(2):
        for i, out in ((0, dko), (1, dvo)):
            x = rkv[0, pp, i].astype(f32)
            for d in range(1, 2 * HALO + 1):
                x = x + rkv[d, pp, i].astype(f32)
            out[:, tile(pp)] = x.astype(bf16)

    older = len(sent) - ny
    for copy in sent[:older]:
        copy.wait_send()

    for part in range(2):
        for k in reversed(yk):
            yy = ypeer(ny - k)
            arrive(relo.at[yy, piece(part)], ms + part * ny + k - 1)
            push(relo.at[yy, piece(part)], relq.at[yy, piece(part)], es + part * ny + k, mate)

    arrive(wrecv, ws)
    wko[:, lanes(o)] = wrecv[0]
    wqo[:, lanes(o)] = wrecv[1]
    for part in range(2):
        arrive(relq.at[y, piece(part)], es + part * ny)
        for k in reversed(yk):
            arrive(relq.at[ypeer(ny - k), piece(part)], es + part * ny + k)
    for copy in sent[older:]:
        copy.wait_send()


def copy_kernel(ny, dq, dk, dv, rel, relq, wk, wq, dqo, dko, dvo, relo, wqo, wko):
    nz, rb = rel.shape[1:3]
    seq = lax.axis_index("seq")
    p, z = lax.rem(seq, 2), seq // (2 * ny)
    dqo[...] = dq[...]
    dko[...] = dk[...]
    dvo[...] = dv[...]
    for i, k in enumerate(by_distance(nz)):
        zz = lax.rem(z - k + nz, nz)
        for yy in range(ny):
            row = pl.ds(pl.multiple_of((yy * nz + zz) * rb, rb), rb)
            relo[row, lanes(p)] = rel[yy, i].astype(f32)
            relo[row, lanes(1 - p)] = relq[yy, i].astype(f32)
    wqo[...] = wq[...]
    wko[...] = wk[...]


def body(ny, queries, keys, values, out_grad, rel_emb, w_query, w_key, doc_lengths, bucket_table):
    nc = lax.axis_size("seq") // 2
    nx = lax.axis_size("head")
    nz = nc // ny
    buckets, width = rel_emb.shape
    span = bucket_table.shape[0]
    rb = buckets // nc
    dr2 = width // nc
    dr = dr2 // 2
    keys_in = TILES * T
    shape = jax.ShapeDtypeStruct
    tab = bucket_table.reshape(1, -1)
    lens = doc_lengths.reshape(1, -1)
    results = pl.pallas_call(
        functools.partial(whole_kernel, nz, ny, nx),
        out_shape=(
            shape((T, 2 * T), bf16),
            shape((T, 2 * T), bf16),
            shape((T, 2 * T), bf16),
            shape((ny, nz, rb, T), bf16),
            shape((ny, nz, rb, T), bf16),
            shape((dr, 2 * T), f32),
            shape((dr, 2 * T), f32),
        ),
        in_specs=[ANY] * 7 + [VM] * 2,
        out_specs=(VM,) * 7,
        scratch_shapes=[
            pltpu.VMEM((buckets, width), bf16),
            pltpu.VMEM((2, width, T), bf16),
            pltpu.VMEM((2 * T, T), bf16),
            pltpu.VMEM((2 * T, T), bf16),
            pltpu.VMEM((keys_in, T), bf16),
            pltpu.VMEM((keys_in, T), bf16),
            pltpu.VMEM((span, 2 * T), bf16),
            pltpu.VMEM((buckets, span), bf16),
            pltpu.VMEM((2, 2 * T, T), bf16),
            pltpu.VMEM((2, 2 * T, T), bf16),
            pltpu.VMEM((2, keys_in, T), bf16),
            pltpu.VMEM((2, span + 4 * T, T), bf16),
            pltpu.VMEM((T, 2 * T), bf16),
            pltpu.VMEM((T, keys_in), bf16),
            pltpu.VMEM((2, keys_in, 2 * T), f32),
            pltpu.VMEM((2, keys_in, 2 * T), f32),
            pltpu.VMEM((2, keys_in, 2 * T), bf16),
            pltpu.VMEM((2, keys_in, 2 * T), bf16),
            pltpu.VMEM((2, keys_in, 2 * T), bf16),
            pltpu.VMEM((2, keys_in, 3 * T), bf16),
            pltpu.VMEM((2, 2 * T, WIDE), bf16),
            pltpu.VMEM((2, 2 * T, span), bf16),
            pltpu.VMEM((keys_in, T), bf16),
            pltpu.VMEM((keys_in, T), bf16),
            pltpu.VMEM((2 * T, T), bf16),
            pltpu.VMEM((T, span), f32),
            pltpu.VMEM((T, span + 4 * T), f32),
            pltpu.VMEM((2, buckets, T), bf16),
            pltpu.VMEM((5, 2, 2, T, T), bf16),
            pltpu.VMEM((T, T), bf16),
            pltpu.VMEM((2, ny, nz * rb, T), bf16),
            pltpu.VMEM((nz, 2 * rb, T), bf16),
            pltpu.VMEM((nz, 2 * rb, T), bf16),
            pltpu.VMEM((2 * rb, T), bf16),
            pltpu.VMEM((nz, 2 * rb, T), bf16),
            pltpu.VMEM((2 * nx, rb, T), f32),
            pltpu.VMEM((2 * nx, rb, T), f32),
            pltpu.VMEM((2, T, T), f32),
            pltpu.VMEM((ny, 2, dr2, T), f32),
            pltpu.VMEM((2, dr2, T), f32),
            pltpu.VMEM((2, dr, T), f32),
            pltpu.SemaphoreType.DMA((144,)),
            pltpu.SemaphoreType.DMA((144,)),
            pltpu.SemaphoreType.DMA((7,)),
            pltpu.SemaphoreType.REGULAR((3,)),
        ],
        compiler_params=pltpu.CompilerParams(collective_id=0, has_side_effects=True),
        name="whole",
    )(queries, keys, values, out_grad, rel_emb, w_query, w_key, tab, lens)
    return tuple(
        pl.pallas_call(
            functools.partial(copy_kernel, ny),
            out_shape=(
                shape((T, 2 * T), bf16),
                shape((T, 2 * T), bf16),
                shape((T, 2 * T), bf16),
                shape((buckets, 2 * T), f32),
                shape((dr, 2 * T), f32),
                shape((dr, 2 * T), f32),
            ),
            in_specs=[VM] * 7,
            out_specs=(VM,) * 6,
            name="results",
        )(*results)
    )


def solution(mesh, ny=NY):
    shard = P("seq", "head")
    return jax.shard_map(
        functools.partial(body, ny),
        mesh=mesh,
        in_specs=(shard,) * 4 + (P(), P(None, "head"), P(None, "head"), P(), P()),
        out_specs=(shard, shard, shard, P(None, "head"), shard, shard),
        check_vma=False,
    )
```

```python
import functools
import math

import jax
import jax.numpy as jnp
from jax import lax
from jax.experimental import pallas as pl
from jax.experimental.pallas import tpu as pltpu
from jax.sharding import PartitionSpec as P

HD = 64
T = 128
NY = 4
HALO = 2
TILES = 2 * (2 * HALO + 1)
WIDE = 9 * T
f32 = jnp.float32
bf16 = jnp.bfloat16
SCALE = 1.0 / math.sqrt(3.0 * HD)
ANY = pl.BlockSpec(memory_space=pl.ANY)
VM = pl.BlockSpec(memory_space=pltpu.VMEM)


def dot(a, b, ca=1, cb=0):
    return lax.dot_general(a, b, (((ca,), (cb,)), ((), ())), preferred_element_type=f32)


def remote(src, dst, send, recv, seq, head=None):
    where = {"seq": seq} if head is None else {"seq": seq, "head": head}
    return pltpu.make_async_remote_copy(
        src_ref=src, dst_ref=dst, send_sem=send, recv_sem=recv,
        device_id=where, device_id_type=pl.DeviceIdType.MESH,
    )


def greet(seq, head=None):
    where = {"seq": seq} if head is None else {"seq": seq, "head": head}
    pl.semaphore_signal(
        pltpu.get_barrier_semaphore(), inc=1, device_id=where,
        device_id_type=pl.DeviceIdType.MESH,
    )


def lanes(p):
    return pl.ds(pl.multiple_of(p * T, T), T)


def rows(start):
    return pl.ds(pl.multiple_of(start, T), T)


def tile(j):
    return slice(j * T, (j + 1) * T)


def skewed(x, first):
    return pltpu.roll(x, first, 1, stride=1, stride_axis=0)


def by_distance(nz):
    return sorted(range(nz), key=lambda k: min(k, nz - k))


def head_only(x, h):
    lane = lax.broadcasted_iota(jnp.int32, x.shape, 1)
    return jnp.where((lane < HD) if h == 0 else (lane >= HD), x, jnp.zeros_like(x))


def indicator(match):
    return match.astype(f32).astype(bf16)


def whole_kernel(
    nz, ny, nx,
    q_ref, k_ref, v_ref, g_ref, rel_ref, wq_ref, wk_ref, tab_ref, len_ref,
    dqo, dko, dvo, relo, relq, wko, wqo,
    rel_v, wv, qw, gw, kw, vw, pb, oht, q2, g2, k2, pqr, qrt, krt,
    sc, dp, prb, dsb, dsr, skb, dsa, ska, dkb, dvb, dqb, gt, ht,
    bp, rkv, rq, yrecv, zsend, zrecv, own, ag, xpart, xrecv,
    wtmp, wy, wsum, wrecv, send, recv, local, known,
):
    nc = nz * ny
    s = lax.axis_index("seq")
    hx = lax.axis_index("head")
    c, p = s // 2, lax.rem(s, 2)
    o = 1 - p
    mate = 2 * c + o
    z, y = c // ny, lax.rem(c, ny)
    m = 2 * hx + p
    buckets, width = rel_ref.shape
    span = tab_ref.shape[1]
    rb = buckets // nc
    dr2 = width // nc
    dr = dr2 // 2
    hops = [-1, 1, -2, 2]

    def chip(d):
        return lax.rem(c + d + nc, nc)

    def ypeer(k):
        return lax.rem(y + k, ny)

    def zpeer(k):
        return lax.rem(z + k, nz)

    def mpeer(k):
        return lax.rem(m + k, 2 * nx)

    def at(zz, yy):
        return 2 * (zz * ny + yy) + p

    def plane(yy):
        return pl.ds(pl.multiple_of(nz * rb * yy, nz * rb), nz * rb)

    yk = sorted(range(1, ny), key=lambda k: -min(k, ny - k))
    zk = sorted(range(1, nz), key=lambda k: -min(k, nz - k))
    mk = range(1, 2 * nx)
    order = by_distance(nz)

    for d in (-1, 1):
        for pp in range(2):
            greet(2 * chip(d) + pp)
    for k in (1, nz - 1):
        greet(at(zpeer(k), y))
    for k in yk:
        greet(at(z, ypeer(k)))
    for k in mk:
        greet(2 * c + lax.rem(mpeer(k), 2), mpeer(k) // 2)
    greet(mate)

    loads = []

    def load(src, dst):
        copy = pltpu.make_async_copy(src, dst, local.at[len(loads)])
        copy.start()
        loads.append(copy)

    load(rel_ref, rel_v)
    load(wk_ref.at[:, lanes(p)], wv.at[0])
    load(wq_ref.at[:, lanes(p)], wv.at[1])
    load(k_ref.at[:, lanes(p)], kw.at[rows(2 * HALO * T + T * p)])
    load(v_ref.at[:, lanes(p)], vw.at[rows(2 * HALO * T + T * p)])
    load(q_ref.at[:, lanes(p)], qw.at[rows(T * p)])
    load(g_ref.at[:, lanes(p)], gw.at[rows(T * p)])

    pl.semaphore_wait(
        pltpu.get_barrier_semaphore(), 2 + len(yk) + 4 + len(mk) + 1
    )

    sent = []
    slots = [0]

    def push(src, dst, slot, seq, head=None):
        copy = remote(src, dst, send.at[len(sent)], recv.at[slot], seq, head)
        copy.start()
        sent.append(copy)

    def take(count):
        base = slots[0]
        slots[0] += count
        return base

    def arrive(dst, slot):
        remote(dst, dst, send.at[0], recv.at[slot], s).wait_recv()

    step = [1 << i for i in range(nz.bit_length()) if (1 << i) < nz // 2]

    def tell(i):
        if i < len(step):
            for k in (step[i], nz - step[i]):
                pl.semaphore_signal(known.at[i], inc=1, device_id={"seq": at(zpeer(k), y)},
                                    device_id_type=pl.DeviceIdType.MESH)

    def hear(i):
        if i < len(step):
            pl.semaphore_wait(known.at[i], 2)

    near = take(4)
    hs = take(8)
    fs = take(4)
    row = rows(T * p)
    push(q_ref.at[:, lanes(o)], qw.at[row], near, mate)
    push(g_ref.at[:, lanes(o)], gw.at[row], near + 1, mate)
    row = rows(2 * HALO * T + T * p)
    push(k_ref.at[:, lanes(o)], kw.at[row], near + 2, mate)
    push(v_ref.at[:, lanes(o)], vw.at[row], near + 3, mate)
    for i, src, dst in ((0, k_ref, kw), (1, v_ref, vw)):
        for d in (-1, 1):
            for pp in range(2):
                push(src.at[:, pl.ds(pp * T, T)], dst.at[rows(2 * T * (HALO - d) + T * p)],
                     hs + (d + 1) * 2 + p * 2 + i, 2 * chip(d) + pp)
    tell(0)

    def pass_on(i, ref):
        for d in (-1, 1):
            for pp in range(2):
                arrive(ref.at[tile(2 * (HALO + d) + pp)], hs + (1 - d) * 2 + pp * 2 + i)
            near_rows = pl.ds(2 * T * (HALO + d), 2 * T)
            far_rows = pl.ds(2 * T * (HALO + 2 * d), 2 * T)
            push(ref.at[near_rows], ref.at[far_rows], fs + d + 1 + i, 2 * chip(-d) + p)

    def passed(i, ref):
        for d in (-1, 1):
            arrive(ref.at[pl.ds(2 * T * (HALO + 2 * d), 2 * T)], fs + d + 1 + i)

    ri = lax.broadcasted_iota(jnp.int32, (T, T), 0)
    ci = lax.broadcasted_iota(jnp.int32, (T, T), 1)
    flip = indicator(ri + ci == T - 1)
    table = jnp.broadcast_to(tab_ref[...], (8, span))
    high = table // 256
    low = (table - 256 * high).astype(f32).astype(bf16)
    high = high.astype(f32).astype(bf16)
    blocks = span // T
    rev = jnp.concatenate(
        [
            256.0 * dot(high[:, tile(blocks - 1 - b)], flip) + dot(low[:, tile(blocks - 1 - b)], flip)
            for b in range(blocks)
        ],
        1,
    )[:1]
    number = lax.broadcasted_iota(jnp.int32, (T, span), 0).astype(f32)
    for b in range(buckets // T):
        oht[tile(b)] = indicator(number + float(b * T) == rev)
    column = jnp.transpose(jnp.broadcast_to(rev, (T, span)))
    lane = lax.broadcasted_iota(jnp.int32, column.shape, 1).astype(f32)
    onehot = jnp.concatenate(
        [indicator(column == lane + float(T * b)) for b in range(buckets // T)], 1
    )

    ndocs = len_ref.shape[1]
    de = lax.broadcasted_iota(jnp.int32, (ndocs, ndocs), 1)
    dd = lax.broadcasted_iota(jnp.int32, (ndocs, ndocs), 0)
    lens = jnp.broadcast_to(len_ref[...], (ndocs, ndocs))
    ends = jnp.sum(jnp.where(de <= dd, lens, 0), axis=1, keepdims=True)
    shift = (c - HALO) * 2 * T
    pos = lax.broadcasted_iota(jnp.int32, (ndocs, 2 * T), 1) + c * 2 * T
    first = jnp.max(jnp.where(ends <= pos, ends, 0), axis=0, keepdims=True) - shift
    last = jnp.min(jnp.where(ends > pos, ends, 1 << 30), axis=0, keepdims=True) - shift

    for copy in loads[:3]:
        copy.wait()
    pos_key = dot(rel_v[...], wv[0]).astype(bf16)
    pos_query = dot(rel_v[...], wv[1]).astype(bf16)
    pb[...] = dot(onehot, jnp.concatenate([pos_key, pos_query], 1)).astype(bf16)
    for h in range(2):
        pqr[h, : 2 * T] = jnp.zeros((2 * T, T), bf16)
        pqr[h, 2 * T : 2 * T + span] = head_only(pb[:, T:], h)
        pqr[h, 2 * T + span :] = jnp.zeros((2 * T, T), bf16)
    ht[...] = jnp.zeros_like(ht)
    pass_on(0, kw)

    hear(0)
    tell(1)
    for copy in loads[3:]:
        copy.wait()
    arrive(qw.at[rows(T * o)], near)
    arrive(gw.at[rows(T * o)], near + 1)

    for h in range(2):
        q2[h] = head_only(qw[...], h)
        g2[h] = head_only(gw[...], h)
    for r in range(2):
        qrt[:, tile(r)] = jnp.transpose(dot(flip, qw[tile(r)])).astype(bf16)
    for h in range(2):
        sc[h, WIDE:, :T] = jnp.zeros((T, T), f32)
        sc[h, :T, T:] = jnp.zeros((T, T), f32)
        for r in range(2):
            a = dot(q2[h, tile(r)], pb[:, :T], 1, 1)
            a = skewed(jnp.concatenate([a, jnp.zeros((T, WIDE - span), f32)], 1), 1)
            for j in range(9):
                sc[h, tile(r + j), tile(r)] = jnp.transpose(a[:, tile(j)])

    pass_on(1, vw)
    arrive(kw.at[rows(2 * HALO * T + T * o)], near + 2)
    arrive(vw.at[rows(2 * HALO * T + T * o)], near + 3)

    top = [jnp.full((8, 2 * T), -1e30, f32) for _ in range(2)]

    def band(j):
        return slice((9 - j) * T, (9 - j) * T + 3 * T)

    def fold(x, op):
        return op(x.reshape(T // 8, 8, 2 * T), axis=0)

    def score(j):
        kt = kw[tile(j)]
        krt[:, tile(j)] = jnp.transpose(dot(flip, kt)).astype(bf16)
        key = lax.broadcasted_iota(jnp.int32, (T, 2 * T), 0) + j * T
        keep = (key >= first) & (key < last)
        for h in range(2):
            k2[h, tile(j)] = head_only(kt, h)
            b = skewed(dot(kt, pqr[h, band(j)], 1, 1), 2 * T + 1)[:, : 2 * T]
            x = SCALE * (dot(kt, q2[h], 1, 1) + sc[h, tile(j)] + b)
            x = jnp.where(keep, x, -1e30)
            sc[h, tile(j)] = x
            top[h] = jnp.maximum(top[h], fold(x, jnp.max))

    def through_values(j):
        for h in range(2):
            dp[h, tile(j)] = dot(vw[tile(j)], g2[h], 1, 1)

    inner, outer = (4, 5, 2, 3, 6, 7), (0, 1, 8, 9)
    for j in inner:
        score(j)
    hear(1)
    tell(2)
    for j in inner:
        through_values(j)
    passed(0, kw)
    for j in outer:
        score(j)

    totals, alongs = [], []
    for h in range(2):
        high_score = jnp.max(top[h], axis=0, keepdims=True)
        total = jnp.zeros((8, 2 * T), f32)
        along = jnp.zeros((8, 2 * T), f32)
        for j in inner + outer:
            x = jnp.exp(sc[h, tile(j)] - high_score)
            sc[h, tile(j)] = x
            total = total + fold(x, jnp.sum)
            if j in inner:
                along = along + fold(x * dp[h, tile(j)], jnp.sum)
        totals.append(total)
        alongs.append(along)
    passed(1, vw)
    inv, row_dot = [], []
    for h in range(2):
        along = alongs[h]
        for j in outer:
            x = dot(vw[tile(j)], g2[h], 1, 1)
            dp[h, tile(j)] = x
            along = along + fold(sc[h, tile(j)] * x, jnp.sum)
        inv.append(1.0 / jnp.sum(totals[h], axis=0, keepdims=True))
        row_dot.append(jnp.sum(along, axis=0, keepdims=True) * inv[h])

    for h in range(2):
        half = slice(h * HD, (h + 1) * HD)
        for j in range(TILES):
            prob = sc[h, tile(j)] * inv[h]
            ds = (prob * (dp[h, tile(j)] - row_dot[h])).astype(bf16)
            prb[h, tile(j)] = prob.astype(bf16)
            dsb[h, tile(j)] = ds
            back = dot(flip, ds)
            dsr[h, tile(j)] = back.astype(bf16)
            skew = skewed(jnp.concatenate([back, jnp.zeros((T, T), f32)], 1), 0).astype(bf16)
            skb[h, tile(j)] = skew
            ht[half, band(j)] += dot(krt[half, tile(j)], skew)

    ys = take(2 * ny)

    def scatter(i, offsets):
        bp[i] = (SCALE * dot(oht[...], offsets.astype(bf16), 1, 1)).astype(bf16)
        for k in yk:
            push(bp.at[i, plane(ypeer(k))], yrecv.at[i, k - 1],
                 ys + i * ny + k - 1, at(z, ypeer(k)))

    scatter(1, ht[:, 2 * T : 2 * T + span])
    for h in range(2):
        half = slice(h * HD, (h + 1) * HD)
        for r in range(2):
            back = dot(flip, dsb[h, r * T : r * T + WIDE, tile(r)], 1, 1)
            dsa[h, tile(r)] = back.astype(bf16)
            skew = skewed(back, span)[:, :span].astype(bf16)
            ska[h, tile(r)] = skew
            part = dot(qrt[half, tile(r)], skew)
            if r == 0:
                gt[half] = part
            else:
                gt[half] += part
    scatter(0, gt[...])

    far_first = [j for d in (-2, 2, -1, 1, 0) for j in (2 * (d + HALO), 2 * (d + HALO) + 1)]
    for j in far_first:
        dv = dot(prb[0, tile(j)], g2[0]) + dot(prb[1, tile(j)], g2[1])
        dvb[tile(j)] = dv.astype(bf16)
    for r in range(2):
        reach = slice(r * T, r * T + WIDE)
        dq = dot(dsa[0, tile(r)], k2[0, reach]) + dot(dsa[1, tile(r)], k2[1, reach])
        for h in range(2):
            dq = dq + head_only(dot(ska[h, tile(r)], pb[:, :T]), h)
        dqb[tile(r)] = dot(flip, (SCALE * dq).astype(bf16)).astype(bf16)

    parts = []
    for i in range(2):
        part = bp[i, plane(y)].astype(f32)
        for k in yk:
            arrive(yrecv.at[i, k - 1], ys + i * ny + k - 1)
        for k in yk:
            part = part + yrecv[i, k - 1].astype(f32)
        parts.append(part.reshape(nz, rb, T))
    zsend[...] = jnp.concatenate(parts, 1).astype(bf16)

    hear(2)
    zs = take(nz)
    for k in zk:
        push(zsend.at[zpeer(k)], zrecv.at[k - 1], zs + k - 1, at(zpeer(k), y))

    rs = take(20)

    def give_back(grad, i):
        for d in reversed(hops):
            for pp in range(2):
                push(grad.at[tile(2 * (d + HALO) + pp)], rkv.at[d + HALO, p, i],
                     rs + ((d + HALO) * 2 + p) * 2 + i, 2 * chip(d) + pp)
        push(grad.at[rows(2 * HALO * T + T * o)], rkv.at[HALO, p, i],
             rs + (HALO * 2 + p) * 2 + i, mate)

    qs = take(1)
    push(dqb.at[rows(T * o)], rq, qs, mate)
    give_back(dvb, 1)
    for j in far_first:
        dk = dot(dsr[0, tile(j)], q2[0]) + dot(dsr[1, tile(j)], q2[1])
        dk = dk + dot(skb[0, tile(j)], pqr[0, band(j)]) + dot(skb[1, tile(j)], pqr[1, band(j)])
        dkb[tile(j)] = dot(flip, (SCALE * dk).astype(bf16)).astype(bf16)
    give_back(dkb, 0)

    part = zsend[z].astype(f32)
    for k in reversed(zk):
        arrive(zrecv.at[k - 1], zs + k - 1)
        part = part + zrecv[k - 1].astype(f32)
    low = part.astype(bf16)
    own[...] = low
    ag[z] = low

    both = low.astype(f32)
    rel_part = dot(both[:rb].astype(bf16), wv[0], 1, 1) + dot(both[rb:].astype(bf16), wv[1], 1, 1)
    for i in range(2 * nx):
        xpart[i] = rel_part[:, tile(i)]
    xs = take(2 * nx)
    for k in mk:
        push(xpart.at[mpeer(k)], xrecv.at[k - 1], xs + k - 1,
             2 * c + lax.rem(mpeer(k), 2), mpeer(k) // 2)

    gs = take(nz)
    for k in zk:
        push(own, ag.at[z], gs + k - 1, at(zpeer(k), y))
    total = xpart[m]
    for k in mk:
        arrive(xrecv.at[k - 1], xs + k - 1)
        total = total + xrecv[k - 1]
    relo[y, 0] = total.astype(bf16)
    ls = take(nz)
    for k in zk:
        push(relo.at[y, 0], relo.at[y, order.index(k)], ls + k - 1, at(zpeer(k), y))

    for k in reversed(zk):
        arrive(ag.at[zpeer(nz - k)], gs + k - 1)
    every = ag[...].astype(f32)
    for i in range(2):
        grad = every[:, i * rb : (i + 1) * rb].reshape(nz * rb, T).astype(bf16)
        block = rel_v[plane(y), lanes(z * ny * dr2 // T)]
        wtmp[i] = dot(block, grad, 0, 0)
    start = lax.rem(z * ny * dr2, T)

    def of(yy):
        return pl.ds(pl.multiple_of(start + dr2 * yy, dr2), dr2)

    us = take(ny)
    for k in yk:
        push(wtmp.at[:, of(ypeer(k))], wy.at[k - 1], us + k - 1, at(z, ypeer(k)))

    ms = take(2 * ny)
    es = take(2 * ny)

    def piece(part):
        return pl.ds(part * (nz // 2), nz // 2)

    def spread(part):
        for i in range(part * (nz // 2), (part + 1) * (nz // 2)):
            if i:
                arrive(relo.at[y, i], ls + order[i] - 1)
        for k in yk:
            push(relo.at[y, piece(part)], relo.at[y, piece(part)],
                 ms + part * ny + k - 1, at(z, ypeer(k)))
        push(relo.at[y, piece(part)], relq.at[y, piece(part)], es + part * ny, mate)

    spread(0)
    dqo[:, lanes(p)] = dqb[rows(T * p)]
    arrive(rq, qs)
    dqo[:, lanes(o)] = rq[...]
    total = wtmp[:, of(y)]
    for k in yk:
        arrive(wy.at[k - 1], us + k - 1)
        total = total + wy[k - 1]
    wsum[...] = total
    ws = take(1)
    push(wsum.at[:, pl.ds(pl.multiple_of(dr * o, dr), dr)], wrecv, ws, mate)
    ours = pl.ds(pl.multiple_of(dr * p, dr), dr)
    wko[:, lanes(p)] = wsum[0, ours]
    wqo[:, lanes(p)] = wsum[1, ours]

    spread(1)

    row = rows(2 * HALO * T + T * p)
    rkv[HALO, p, 0] = dkb[row]
    rkv[HALO, p, 1] = dvb[row]
    arrive(rkv.at[HALO, o, 0], rs + (HALO * 2 + o) * 2)
    arrive(rkv.at[HALO, o, 1], rs + (HALO * 2 + o) * 2 + 1)
    for d in hops:
        for pp in range(2):
            arrive(rkv.at[d + HALO, pp, 0], rs + ((d + HALO) * 2 + pp) * 2)
            arrive(rkv.at[d + HALO, pp, 1], rs + ((d + HALO) * 2 + pp) * 2 + 1)
    for pp in range(2):
        for i, out in ((0, dko), (1, dvo)):
            x = rkv[0, pp, i].astype(f32)
            for d in range(1, 2 * HALO + 1):
                x = x + rkv[d, pp, i].astype(f32)
            out[:, tile(pp)] = x.astype(bf16)

    older = len(sent) - ny
    for copy in sent[:older]:
        copy.wait_send()

    for part in range(2):
        for k in reversed(yk):
            yy = ypeer(ny - k)
            arrive(relo.at[yy, piece(part)], ms + part * ny + k - 1)
            push(relo.at[yy, piece(part)], relq.at[yy, piece(part)], es + part * ny + k, mate)

    arrive(wrecv, ws)
    wko[:, lanes(o)] = wrecv[0]
    wqo[:, lanes(o)] = wrecv[1]
    for part in range(2):
        arrive(relq.at[y, piece(part)], es + part * ny)
        for k in reversed(yk):
            arrive(relq.at[ypeer(ny - k), piece(part)], es + part * ny + k)
    for copy in sent[older:]:
        copy.wait_send()


def copy_kernel(ny, dq, dk, dv, rel, relq, wk, wq, dqo, dko, dvo, relo, wqo, wko):
    nz, rb = rel.shape[1:3]
    seq = lax.axis_index("seq")
    p, z = lax.rem(seq, 2), seq // (2 * ny)
    dqo[...] = dq[...]
    dko[...] = dk[...]
    dvo[...] = dv[...]
    for i, k in enumerate(by_distance(nz)):
        zz = lax.rem(z - k + nz, nz)
        for yy in range(ny):
            row = pl.ds(pl.multiple_of((yy * nz + zz) * rb, rb), rb)
            relo[row, lanes(p)] = rel[yy, i].astype(f32)
            relo[row, lanes(1 - p)] = relq[yy, i].astype(f32)
    wqo[...] = wq[...]
    wko[...] = wk[...]


def body(ny, queries, keys, values, out_grad, rel_emb, w_query, w_key, doc_lengths, bucket_table):
    nc = lax.axis_size("seq") // 2
    nx = lax.axis_size("head")
    nz = nc // ny
    buckets, width = rel_emb.shape
    span = bucket_table.shape[0]
    rb = buckets // nc
    dr2 = width // nc
    dr = dr2 // 2
    keys_in = TILES * T
    shape = jax.ShapeDtypeStruct
    tab = bucket_table.reshape(1, -1)
    lens = doc_lengths.reshape(1, -1)
    results = pl.pallas_call(
        functools.partial(whole_kernel, nz, ny, nx),
        out_shape=(
            shape((T, 2 * T), bf16),
            shape((T, 2 * T), bf16),
            shape((T, 2 * T), bf16),
            shape((ny, nz, rb, T), bf16),
            shape((ny, nz, rb, T), bf16),
            shape((dr, 2 * T), f32),
            shape((dr, 2 * T), f32),
        ),
        in_specs=[ANY] * 7 + [VM] * 2,
        out_specs=(VM,) * 7,
        scratch_shapes=[
            pltpu.VMEM((buckets, width), bf16),
            pltpu.VMEM((2, width, T), bf16),
            pltpu.VMEM((2 * T, T), bf16),
            pltpu.VMEM((2 * T, T), bf16),
            pltpu.VMEM((keys_in, T), bf16),
            pltpu.VMEM((keys_in, T), bf16),
            pltpu.VMEM((span, 2 * T), bf16),
            pltpu.VMEM((buckets, span), bf16),
            pltpu.VMEM((2, 2 * T, T), bf16),
            pltpu.VMEM((2, 2 * T, T), bf16),
            pltpu.VMEM((2, keys_in, T), bf16),
            pltpu.VMEM((2, span + 4 * T, T), bf16),
            pltpu.VMEM((T, 2 * T), bf16),
            pltpu.VMEM((T, keys_in), bf16),
            pltpu.VMEM((2, keys_in, 2 * T), f32),
            pltpu.VMEM((2, keys_in, 2 * T), f32),
            pltpu.VMEM((2, keys_in, 2 * T), bf16),
            pltpu.VMEM((2, keys_in, 2 * T), bf16),
            pltpu.VMEM((2, keys_in, 2 * T), bf16),
            pltpu.VMEM((2, keys_in, 3 * T), bf16),
            pltpu.VMEM((2, 2 * T, WIDE), bf16),
            pltpu.VMEM((2, 2 * T, span), bf16),
            pltpu.VMEM((keys_in, T), bf16),
            pltpu.VMEM((keys_in, T), bf16),
            pltpu.VMEM((2 * T, T), bf16),
            pltpu.VMEM((T, span), f32),
            pltpu.VMEM((T, span + 4 * T), f32),
            pltpu.VMEM((2, buckets, T), bf16),
            pltpu.VMEM((5, 2, 2, T, T), bf16),
            pltpu.VMEM((T, T), bf16),
            pltpu.VMEM((2, ny, nz * rb, T), bf16),
            pltpu.VMEM((nz, 2 * rb, T), bf16),
            pltpu.VMEM((nz, 2 * rb, T), bf16),
            pltpu.VMEM((2 * rb, T), bf16),
            pltpu.VMEM((nz, 2 * rb, T), bf16),
            pltpu.VMEM((2 * nx, rb, T), f32),
            pltpu.VMEM((2 * nx, rb, T), f32),
            pltpu.VMEM((2, T, T), f32),
            pltpu.VMEM((ny, 2, dr2, T), f32),
            pltpu.VMEM((2, dr2, T), f32),
            pltpu.VMEM((2, dr, T), f32),
            pltpu.SemaphoreType.DMA((144,)),
            pltpu.SemaphoreType.DMA((144,)),
            pltpu.SemaphoreType.DMA((7,)),
            pltpu.SemaphoreType.REGULAR((3,)),
        ],
        compiler_params=pltpu.CompilerParams(collective_id=0, has_side_effects=True),
        name="whole",
    )(queries, keys, values, out_grad, rel_emb, w_query, w_key, tab, lens)
    return tuple(
        pl.pallas_call(
            functools.partial(copy_kernel, ny),
            out_shape=(
                shape((T, 2 * T), bf16),
                shape((T, 2 * T), bf16),
                shape((T, 2 * T), bf16),
                shape((buckets, 2 * T), f32),
                shape((dr, 2 * T), f32),
                shape((dr, 2 * T), f32),
            ),
            in_specs=[VM] * 7,
            out_specs=(VM,) * 6,
            name="results",
        )(*results)
    )


def solution(mesh, ny=NY):
    shard = P("seq", "head")
    return jax.shard_map(
        functools.partial(body, ny),
        mesh=mesh,
        in_specs=(shard,) * 4 + (P(), P(None, "head"), P(None, "head"), P(), P()),
        out_specs=(shard, shard, shard, P(None, "head"), shard, shard),
        check_vma=False,
    )
```
